256 devices in a mesh: gx: 4 (over x), gy: 8 (over z), gz: 8 (over y, core).
Axes of the slice: x: 4, y: 4, z: 8, core: 2. Of those that a mesh axis runs over, the one named last changes fastest.
Arguments:
- patch_fields: bfloat16 [8192, 4, 32768], P(('gx', 'gy', 'gz')), may hold values from -54 to 54
- slot_snapshot: int32 [8192], P(('gx', 'gy', 'gz')), may hold values from -1 to 15, as said below
- slot_brick: int32 [8192], P(('gx', 'gy', 'gz')), may hold values from -1 to 255, as said below
- prior_basis: float32 [64, 32], replicated, may hold values from -0.75 to 0.75
Outputs:
- gram_matrix: float32 [64, 64], replicated
- mode_fields: bfloat16 [64, 128, 4096], P('gx', 'gy', 'gz')
- diffused: bfloat16 [64, 128, 4096], P('gx', 'gy', 'gz')
- reduced: float32 [32, 32], replicated
The draws below stay inside these ranges and needn't reach their ends.
Inputs may be any that keep to these rules, and one draw needn't show every extreme that they name: `slot_snapshot`: -1 marks an empty slot; on every device the live slots come first, and some device has all 32 slots live. `slot_brick`: a brick is named by its device index in the order gx, gy, gz with gz fastest; -1 exactly where slot_snapshot is -1; every pair of a snapshot and a brick is held by exactly one slot; a patch's owner has the same gz index as its brick; no device holds more than 1 patches of one brick, a bound reached in every gz plane.
All inputs are finite; a program needn't handle non-finite values.
Results may differ from the reference program's by a relative error of at most 0.0076.
Values may be sent and summed in bfloat16 or wider, within the bound.
A program may use at most 128 MiB of HBM per device.

```python
import jax
import jax.numpy as jnp
from jax import lax

SNAPS = 16
FIELDS = 4
PATCH = 32
MODES = 32
EDGE = 16
CELLS = 4096
FINE = 32768
COLS = 64
SLOTS = 32
NX = 64
NY = 128
NZ = 128
NCELLS = 1048576
N_GX = 4
N_GY = 8
N_GZ = 8


def slot_tables(key):
    plane_size = N_GX * N_GY
    pair_depth = 2 * SNAPS // plane_size
    slot_count = 2 * SNAPS
    base_key = jax.random.fold_in(key, 7101)

    def one_plane(gz_layer):
        plane_key = jax.random.fold_in(base_key, gz_layer)
        owner_role = jax.random.permutation(jax.random.fold_in(plane_key, 1), plane_size)
        dest_label = jax.random.permutation(jax.random.fold_in(plane_key, 2), plane_size)
        is_heavy = owner_role < plane_size // 4
        is_medium = (owner_role >= plane_size // 4) & (owner_role < plane_size // 2)
        is_light = owner_role >= plane_size // 2
        role_sum = owner_role[:, None] + dest_label[None, :]
        linked = is_heavy[:, None] | is_medium[:, None] & (role_sum % 2 == 0) | is_light[:, None] & (role_sum % 4 == 0)
        entries = jnp.broadcast_to(linked[:, None, :], (plane_size, pair_depth, plane_size))
        linked_flat = entries.reshape(plane_size * pair_depth, plane_size).astype(jnp.int32)
        dest_rank = jnp.cumsum(linked_flat, axis=0) - 1
        snap_orders = jax.vmap(lambda sub_key: jax.random.permutation(sub_key, SNAPS))(jax.random.split(jax.random.fold_in(plane_key, 3), plane_size))
        snap_table = jnp.take_along_axis(snap_orders.T, jnp.clip(dest_rank, 0, SNAPS - 1), axis=0)
        snap_table = snap_table.reshape(plane_size, pair_depth, plane_size).transpose(0, 2, 1).reshape(plane_size, slot_count)
        is_live = entries.transpose(0, 2, 1).reshape(plane_size, slot_count)
        dest_index = jnp.broadcast_to(jnp.arange(plane_size, dtype=jnp.int32)[None, :, None], (plane_size, plane_size, pair_depth)).reshape(plane_size, slot_count)
        brick_index = dest_index * N_GZ + gz_layer
        shuffled = jax.vmap(lambda sub_key: jax.random.permutation(sub_key, slot_count))(jax.random.split(jax.random.fold_in(plane_key, 4), plane_size))
        scores = jnp.where(is_live, shuffled, shuffled + slot_count)
        ranking = jnp.argsort(scores, axis=1)
        live_sorted = jnp.take_along_axis(is_live, ranking, axis=1)
        snap_sorted = jnp.take_along_axis(snap_table, ranking, axis=1)
        brick_sorted = jnp.take_along_axis(brick_index, ranking, axis=1)
        return (jnp.where(live_sorted, snap_sorted, -1), jnp.where(live_sorted, brick_sorted, -1))
    snap_all, brick_all = jax.vmap(one_plane)(jnp.arange(N_GZ, dtype=jnp.int32))
    snap_all = snap_all.transpose(1, 0, 2).reshape(-1).astype(jnp.int32)
    brick_all = brick_all.transpose(1, 0, 2).reshape(-1).astype(jnp.int32)
    return (snap_all, brick_all)


def draw_slot_snapshot(key, part):
    return slot_tables(key)[0]


def draw_slot_brick(key, part):
    return slot_tables(key)[1]


def shared_waves(key, snap_all, brick_all):
    wave_count = 8
    wave_key = jax.random.fold_in(key, 7404)
    lengths = jax.random.uniform(jax.random.fold_in(wave_key, 1), (wave_count, 3), minval=24.0, maxval=96.0)
    signs = (2 * jax.random.randint(jax.random.fold_in(wave_key, 2), (wave_count, 3), 0, 2) - 1).astype(jnp.float32)
    wavenumber = 2.0 * jnp.pi * signs / lengths
    phases = jax.random.uniform(jax.random.fold_in(wave_key, 3), (wave_count,), minval=0.0, maxval=2.0 * jnp.pi)
    weights = jax.random.normal(jax.random.fold_in(wave_key, 4), (SNAPS, FIELDS, wave_count))
    slot_weights = weights[jnp.clip(snap_all, 0, SNAPS - 1)]
    brick = jnp.clip(brick_all, 0, N_GX * N_GY * N_GZ - 1)
    brick_x = brick // (N_GY * N_GZ)
    brick_y = brick // N_GZ % N_GY
    brick_z = brick % N_GZ
    fine_cell = jnp.arange(PATCH * PATCH * PATCH, dtype=jnp.int32)
    fine_x = fine_cell // (PATCH * PATCH)
    fine_y = fine_cell // PATCH % PATCH
    fine_z = fine_cell % PATCH
    place_x = (brick_x[:, None] * PATCH + fine_x[None, :]).astype(jnp.float32)
    place_y = (brick_y[:, None] * PATCH + fine_y[None, :]).astype(jnp.float32)
    place_z = (brick_z[:, None] * PATCH + fine_z[None, :]).astype(jnp.float32)
    summed = jnp.zeros((snap_all.shape[0], FIELDS, PATCH * PATCH * PATCH), jnp.float32)
    for wave in range(wave_count):
        angle = wavenumber[wave, 0] * place_x + wavenumber[wave, 1] * place_y + wavenumber[wave, 2] * place_z + phases[wave]
        summed = summed + slot_weights[:, :, wave][:, :, None] * jnp.cos(angle)[:, None, :]
    return summed * (0.6 / wave_count ** 0.5)


def draw_patch_fields(key, part):
    snap_all, brick_all = slot_tables(key)
    is_live = snap_all >= 0
    log_scales = jax.random.uniform(jax.random.fold_in(key, 7202), (SNAPS, FIELDS), minval=jnp.log(0.3), maxval=jnp.log(3.0))
    column_scale = jnp.exp(log_scales)[jnp.clip(snap_all, 0, SNAPS - 1)]
    column_scale = jnp.where(is_live[:, None], column_scale, 1.0)
    slab_index = jnp.where(is_live, brick_all // (N_GY * N_GZ), 0).astype(jnp.float32)
    rise = 1.0 + 2.0 * slab_index / max(N_GX - 1, 1)
    amplitude = column_scale * rise[:, None]
    shape = (N_GX * N_GY * N_GZ * 2 * SNAPS, FIELDS, PATCH * PATCH * PATCH)
    noise = jnp.clip(jax.random.normal(jax.random.fold_in(key, 7303), shape), -6.0, 6.0)
    total = (noise + shared_waves(key, snap_all, brick_all)) * amplitude[:, :, None]
    return jnp.clip(total, -54.0, 54.0).astype(jnp.bfloat16)


def gaussian(stream_key, dims, width, most, kind=jnp.bfloat16):
    array = width * jax.random.normal(stream_key, dims, jnp.float32)
    return jnp.clip(array, min=-most, max=most).astype(kind)


def setup_inputs(seed: int = 0) -> dict:
    seeds = jax.random.split(jax.random.key(seed), 5)
    patch_fields = draw_patch_fields(jax.random.fold_in(seeds[4], 71), 0)
    slot_snapshot = draw_slot_snapshot(jax.random.fold_in(seeds[4], 71), 0)
    slot_brick = draw_slot_brick(jax.random.fold_in(seeds[4], 71), 0)
    prior_basis = gaussian(seeds[3], (COLS, MODES), COLS ** -0.5, 0.75, jnp.float32)
    return {"patch_fields": patch_fields, "slot_snapshot": slot_snapshot, "slot_brick": slot_brick, "prior_basis": prior_basis}


def average_cells(fine_data):
    row_count = fine_data.shape[0]
    blocks = fine_data.reshape(row_count, FIELDS, EDGE, 2, EDGE, 2, EDGE, 2)
    means = jnp.mean(blocks, axis=(3, 5, 7), dtype=jnp.float32)
    return means.reshape(row_count, FIELDS, CELLS).astype(jnp.bfloat16)

def reference(patch_fields, slot_snapshot, slot_brick, prior_basis):
    bricks = N_GX * N_GY * N_GZ
    per_device = patch_fields.reshape(bricks, SLOTS, FIELDS, FINE)
    coarse = lax.map(average_cells, per_device).reshape(bricks * SLOTS, FIELDS, CELLS)
    target = jnp.where(slot_snapshot >= 0, slot_brick * SNAPS + slot_snapshot, bricks * SNAPS).astype(jnp.int32)
    placed = jnp.zeros((bricks * SNAPS, FIELDS, CELLS), coarse.dtype).at[target].set(coarse, mode='drop')
    grid_data = placed.reshape(N_GX, N_GY, N_GZ, SNAPS, FIELDS, EDGE, EDGE, EDGE)
    grid_data = grid_data.transpose(0, 5, 1, 6, 2, 7, 3, 4).reshape(NCELLS, COLS)
    data_wide = grid_data.astype(jnp.float32)
    gram_matrix = jnp.dot(data_wide.T, data_wide, precision=lax.Precision.HIGHEST) / NCELLS
    lower_factor = jnp.linalg.cholesky(gram_matrix)
    coeffs = lax.linalg.triangular_solve(lower_factor, prior_basis, left_side=True, lower=True, transpose_a=True)
    mode_basis = jnp.dot(data_wide, coeffs, precision=lax.Precision.HIGHEST)
    mode_grid = mode_basis.reshape(NX, NY, NZ, MODES)
    padded = jnp.pad(mode_grid, ((1, 1), (1, 1), (1, 1), (0, 0)))
    beside = padded[2:, 1:-1, 1:-1] + padded[:-2, 1:-1, 1:-1]
    beside = beside + padded[1:-1, 2:, 1:-1] + padded[1:-1, :-2, 1:-1]
    beside = beside + padded[1:-1, 1:-1, 2:] + padded[1:-1, 1:-1, :-2]
    mode_image = (beside - 6.0 * mode_grid).reshape(NCELLS, MODES)
    reduced = jnp.dot(mode_basis.T, mode_image, precision=lax.Precision.HIGHEST) / NCELLS
    mode_fields = mode_basis.reshape(NX, NY, NZ * MODES).astype(jnp.bfloat16)
    diffused = mode_image.reshape(NX, NY, NZ * MODES).astype(jnp.bfloat16)
    return (gram_matrix, mode_fields, diffused, reduced)
```

```python
import jax
import jax.numpy as jnp
from jax import lax
from jax.sharding import Mesh
from jax.sharding import PartitionSpec as P
from jax.experimental import pallas as pl
from jax.experimental.pallas import tpu as pltpu

SNAPS = 16
FIELDS = 4
PATCH = 32
MODES = 32
EDGE = 16
CELLS = 4096
COLS = 64
GZ = ("gz_0", "gz_1")
GX_GY_GZ = ("gx", "gy", "gz_0", "gz_1")


HIGHEST = lax.Precision.HIGHEST


def extended(value, sides, width):
    edges = {}
    for axis, dim in sides:
        devices, length = (lax.axis_size(axis), value.shape[dim])
        up = [(i, (i + 1) % devices) for i in range(devices - 1)]
        last = lax.slice_in_dim(value, length - width, length, axis=dim)
        first = lax.slice_in_dim(value, 0, width, axis=dim)
        edges[dim] = (
            lax.ppermute(last, axis, up),
            lax.ppermute(first, axis, [(b, a) for a, b in up]),
        )
    done = []
    for _, dim in sides:
        low, high = edges[dim]
        around = [(width, width) if d in done else (0, 0) for d in range(value.ndim)]
        value = jnp.concatenate([jnp.pad(low, around), value, jnp.pad(high, around)], axis=dim)
        done.append(dim)
    return value


def extended_2(value, sides, width):
    for axis, dim in sides:
        devices, length = (lax.axis_size(axis), value.shape[dim])
        up = [(i, (i + 1) % devices) for i in range(devices - 1)]
        down = [(j, i) for i, j in up]
        last = lax.slice_in_dim(value, length - width, length, axis=dim)
        first = lax.slice_in_dim(value, 0, width, axis=dim)
        before = lax.ppermute(last, axis, up)
        after = lax.ppermute(first, axis, down)
        value = jnp.concatenate([before, value, after], axis=dim)
    return value


def over_axes(value, axes):
    for axis in axes:
        value = lax.psum(value, axis)
    return value


def pairing_matrix():
    fine = jnp.arange(2 * PATCH * PATCH, dtype=jnp.int32)
    fine_y = fine % (PATCH * PATCH) // PATCH
    fine_z = fine % PATCH
    coarse = jnp.arange(EDGE * EDGE, dtype=jnp.int32)
    hit = ((fine_y // 2 * EDGE + fine_z // 2)[:, None] == coarse[None, :])
    return jnp.where(hit, 0.125, 0.0).astype(jnp.bfloat16)


PAIRS_PER_STEP = 4


def average_kernel(fine_ref, pairing_ref, out_ref):
    rows = fine_ref.shape[0]
    span = 2 * PATCH * PATCH
    stacked = jnp.concatenate(
        [fine_ref[:, i * span : (i + 1) * span] for i in range(PAIRS_PER_STEP)], axis=0
    )
    means = jnp.dot(stacked, pairing_ref[...], preferred_element_type=jnp.float32)
    width = EDGE * EDGE
    for i in range(PAIRS_PER_STEP):
        out_ref[:, i * width : (i + 1) * width] = means[i * rows : (i + 1) * rows].astype(out_ref.dtype)


def average_cells(fine_data):
    row_count = fine_data.shape[0]
    rows = row_count * FIELDS
    flat = fine_data.reshape(rows, PATCH * PATCH * PATCH)
    span = 2 * PATCH * PATCH * PAIRS_PER_STEP
    width = EDGE * EDGE * PAIRS_PER_STEP
    steps = EDGE // PAIRS_PER_STEP
    means = pl.pallas_call(
        average_kernel,
        grid=(steps,),
        in_specs=[
            pl.BlockSpec((rows, span), lambda g: (0, g)),
            pl.BlockSpec((2 * PATCH * PATCH, EDGE * EDGE), lambda g: (0, 0)),
        ],
        out_specs=pl.BlockSpec((rows, width), lambda g: (0, g)),
        out_shape=jax.ShapeDtypeStruct((rows, CELLS), jnp.bfloat16),
    )(flat, pairing_matrix())
    return means.reshape(row_count, FIELDS, CELLS)


def seven_point(center, around_xy, around_z, stride):
    total = around_xy[2:, 1:-1] + around_xy[:-2, 1:-1] + around_xy[1:-1, 2:] + around_xy[1:-1, :-2]
    total = total + around_z[:, :, 2 * stride :] + around_z[:, :, : -2 * stride]
    return total - 6.0 * center


def factor_basis(gram_matrix, prior_basis):
    lower_factor = jnp.linalg.cholesky(gram_matrix)
    return lax.linalg.triangular_solve(
        lower_factor, prior_basis, left_side=True, lower=True, transpose_a=True
    )


def shards(patch_fields, slot_snapshot, slot_brick, prior_basis):
    size_x = lax.axis_size("gx")
    size_y = lax.axis_size("gy")
    size_z = lax.axis_size(GZ)
    plane_size = size_x * size_y
    slot_count = slot_snapshot.shape[0]
    pair_depth = slot_count // plane_size
    total_cells = CELLS * plane_size * size_z
    is_live = slot_snapshot >= 0
    slot_ids = jnp.arange(slot_count, dtype=jnp.int32)
    target_peer = jnp.where(is_live, slot_brick // size_z, plane_size)
    earlier = (target_peer[:, None] == target_peer[None, :]) & (
        slot_ids[None, :] < slot_ids[:, None]
    )
    pair_rank = jnp.sum(earlier.astype(jnp.int32), axis=1)
    position = jnp.where(is_live, target_peer * pair_depth + pair_rank, slot_count)
    slot_hits = position[:, None] == slot_ids[None, :]
    filled = jnp.any(slot_hits, axis=0)
    source = jnp.sum(jnp.where(slot_hits, slot_ids[:, None], 0), axis=0)
    sent_snapshot = jnp.where(filled, jnp.take(slot_snapshot, source), -1)
    payload = jnp.take(average_cells(patch_fields), source, axis=0)
    received, received_snapshot = (
        lax.all_to_all(payload, ("gx", "gy"), split_axis=0, concat_axis=0, tiled=True),
        lax.all_to_all(sent_snapshot, ("gx", "gy"), split_axis=0, concat_axis=0, tiled=True),
    )
    snapshots = jnp.arange(SNAPS, dtype=jnp.int32)
    chosen = jnp.sum(
        jnp.where(received_snapshot[None, :] == snapshots[:, None], slot_ids[None, :], 0), axis=1
    )
    arrived = jnp.take(received, chosen, axis=0)
    columns = arrived.reshape(COLS, CELLS)
    partial_gram = jnp.dot(columns, columns.T, preferred_element_type=jnp.float32)
    data_wide = columns.astype(jnp.float32).T
    data_block = columns.T.reshape(EDGE, EDGE, EDGE * COLS)
    data_xy = extended(data_block, (("gx", 0), ("gy", 1)), 1).astype(jnp.float32)
    data_z = extended_2(data_block, ((GZ, 2),), COLS).astype(jnp.float32)
    data_image = seven_point(data_block.astype(jnp.float32), data_xy, data_z, COLS).reshape(
        CELLS, COLS
    )
    partial_cross = jnp.dot(data_wide.T, data_image, precision=HIGHEST)
    gram_total = lax.psum(partial_gram, GX_GY_GZ)
    cross_total = lax.psum(partial_cross, GX_GY_GZ)
    gram_matrix = gram_total / total_cells
    coeffs = factor_basis(gram_matrix, prior_basis)
    mode_basis = jnp.dot(data_wide, coeffs, precision=HIGHEST)
    mode_image = jnp.dot(data_image, coeffs, precision=HIGHEST)
    inner = jnp.dot(cross_total / total_cells, coeffs, precision=HIGHEST)
    reduced = jnp.dot(coeffs.T, inner, precision=HIGHEST)
    mode_fields = mode_basis.reshape(EDGE, EDGE, EDGE * MODES).astype(jnp.bfloat16)
    diffused = mode_image.reshape(EDGE, EDGE, EDGE * MODES).astype(jnp.bfloat16)
    return (gram_matrix, mode_fields, diffused, reduced)


def solution(mesh):
    split = Mesh(
        mesh.devices.reshape(mesh.shape["gx"], mesh.shape["gy"], 4, 2), ("gx", "gy", "gz_0", "gz_1")
    )
    in_specs = (P(GX_GY_GZ, None, None), P(GX_GY_GZ), P(GX_GY_GZ), P())
    out_specs = (P(), P("gx", "gy", GZ), P("gx", "gy", GZ), P())
    return jax.shard_map(
        shards, mesh=split, in_specs=in_specs, out_specs=out_specs, check_vma=False
    )
```

```python
import functools

import jax
import jax.numpy as jnp
from jax import lax
from jax.sharding import Mesh
from jax.sharding import PartitionSpec as P
from jax.experimental import pallas as pl
from jax.experimental.pallas import tpu as pltpu

SNAPS = 16
FIELDS = 4
PATCH = 32
MODES = 32
EDGE = 16
CELLS = 4096
COLS = 64
GZ = ("gz_0", "gz_1")
GX_GY_GZ = ("gx", "gy", "gz_0", "gz_1")


HIGHEST = lax.Precision.HIGHEST


def extended(value, sides, width):
    edges = {}
    for axis, dim in sides:
        devices, length = (lax.axis_size(axis), value.shape[dim])
        up = [(i, (i + 1) % devices) for i in range(devices - 1)]
        last = lax.slice_in_dim(value, length - width, length, axis=dim)
        first = lax.slice_in_dim(value, 0, width, axis=dim)
        edges[dim] = (
            lax.ppermute(last, axis, up),
            lax.ppermute(first, axis, [(b, a) for a, b in up]),
        )
    done = []
    for _, dim in sides:
        low, high = edges[dim]
        around = [(width, width) if d in done else (0, 0) for d in range(value.ndim)]
        value = jnp.concatenate([jnp.pad(low, around), value, jnp.pad(high, around)], axis=dim)
        done.append(dim)
    return value


def extended_2(value, sides, width):
    for axis, dim in sides:
        devices, length = (lax.axis_size(axis), value.shape[dim])
        up = [(i, (i + 1) % devices) for i in range(devices - 1)]
        down = [(j, i) for i, j in up]
        last = lax.slice_in_dim(value, length - width, length, axis=dim)
        first = lax.slice_in_dim(value, 0, width, axis=dim)
        before = lax.ppermute(last, axis, up)
        after = lax.ppermute(first, axis, down)
        value = jnp.concatenate([before, value, after], axis=dim)
    return value


def over_axes(value, axes):
    for axis in axes:
        value = lax.psum(value, axis)
    return value


def pairing_matrix():
    fine = jnp.arange(2 * PATCH * PATCH, dtype=jnp.int32)
    fine_y = fine % (PATCH * PATCH) // PATCH
    fine_z = fine % PATCH
    coarse = jnp.arange(EDGE * EDGE, dtype=jnp.int32)
    hit = ((fine_y // 2 * EDGE + fine_z // 2)[:, None] == coarse[None, :])
    return jnp.where(hit, 0.125, 0.0).astype(jnp.bfloat16)


PAIRS_PER_STEP = 4


def average_kernel(fine_ref, pairing_ref, out_ref):
    rows = fine_ref.shape[0]
    span = 2 * PATCH * PATCH
    stacked = jnp.concatenate(
        [fine_ref[:, i * span : (i + 1) * span] for i in range(PAIRS_PER_STEP)], axis=0
    )
    means = jnp.dot(stacked, pairing_ref[...], preferred_element_type=jnp.float32)
    width = EDGE * EDGE
    for i in range(PAIRS_PER_STEP):
        out_ref[:, i * width : (i + 1) * width] = means[i * rows : (i + 1) * rows].astype(out_ref.dtype)


def average_cells(fine_data):
    row_count = fine_data.shape[0]
    rows = row_count * FIELDS
    flat = fine_data.reshape(rows, PATCH * PATCH * PATCH)
    span = 2 * PATCH * PATCH * PAIRS_PER_STEP
    width = EDGE * EDGE * PAIRS_PER_STEP
    steps = EDGE // PAIRS_PER_STEP
    means = pl.pallas_call(
        average_kernel,
        grid=(steps,),
        in_specs=[
            pl.BlockSpec((rows, span), lambda g: (0, g)),
            pl.BlockSpec((2 * PATCH * PATCH, EDGE * EDGE), lambda g: (0, 0)),
        ],
        out_specs=pl.BlockSpec((rows, width), lambda g: (0, g)),
        out_shape=jax.ShapeDtypeStruct((rows, CELLS), jnp.bfloat16),
    )(flat, pairing_matrix())
    return means.reshape(row_count, FIELDS, CELLS)


def seven_point(center, around_xy, around_z, stride):
    total = around_xy[2:, 1:-1] + around_xy[:-2, 1:-1] + around_xy[1:-1, 2:] + around_xy[1:-1, :-2]
    total = total + around_z[:, :, 2 * stride :] + around_z[:, :, : -2 * stride]
    return total - 6.0 * center


def factor_basis(gram_matrix, prior_basis):
    lower_factor = jnp.linalg.cholesky(gram_matrix)
    return lax.linalg.triangular_solve(
        lower_factor, prior_basis, left_side=True, lower=True, transpose_a=True
    )


def tree_sum(values):
    while len(values) > 1:
        values = [values[i] + values[i + 1] for i in range(0, len(values), 2)]
    return values[0]


def allreduce_kernel(sizes, part_ref, out_ref, acc, *rest):
    bufs, (send_sems, recv_sems) = rest[: len(sizes)], rest[len(sizes) :]
    me = [lax.axis_index(axis) for axis in GX_GY_GZ]

    def peer(dim, step):
        device = list(me)
        device[dim] = lax.rem(me[dim] + step, sizes[dim])
        return tuple(device)

    barrier = pltpu.get_barrier_semaphore()
    count = 0
    for dim, size in enumerate(sizes):
        for step in range(1, size):
            pl.semaphore_signal(
                barrier, inc=1, device_id=peer(dim, step), device_id_type=pl.DeviceIdType.MESH
            )
            count += 1
    pl.semaphore_wait(barrier, count)
    acc[...] = part_ref[...]
    slot = 0
    for dim, size in enumerate(sizes):
        if size == 1:
            continue
        buf = bufs[dim]
        copies = []
        for step in range(1, size):
            copy = pltpu.make_async_remote_copy(
                src_ref=acc,
                dst_ref=buf.at[step - 1],
                send_sem=send_sems.at[slot],
                recv_sem=recv_sems.at[slot],
                device_id=peer(dim, step),
                device_id_type=pl.DeviceIdType.MESH,
            )
            copy.start()
            copies.append(copy)
            slot += 1
        for copy in copies:
            copy.wait()
        own = acc[...]
        values = []
        for source in range(size):
            held = jnp.maximum(lax.rem(me[dim] - source + size, size) - 1, 0)
            values.append(jnp.where(me[dim] == source, own, buf[held]))
        acc[...] = tree_sum(values)
    out_ref[...] = acc[...]


def allreduce(part):
    sizes = tuple(lax.axis_size(axis) for axis in GX_GY_GZ)
    copies = sum(size - 1 for size in sizes)
    return pl.pallas_call(
        functools.partial(allreduce_kernel, sizes),
        out_shape=jax.ShapeDtypeStruct(part.shape, part.dtype),
        in_specs=[pl.BlockSpec(memory_space=pltpu.VMEM)],
        out_specs=pl.BlockSpec(memory_space=pltpu.VMEM),
        scratch_shapes=[pltpu.VMEM(part.shape, part.dtype)]
        + [pltpu.VMEM((max(size - 1, 1),) + part.shape, part.dtype) for size in sizes]
        + [pltpu.SemaphoreType.DMA((copies,)), pltpu.SemaphoreType.DMA((copies,))],
        compiler_params=pltpu.CompilerParams(collective_id=0, has_side_effects=True),
    )(part)


def shards(patch_fields, slot_snapshot, slot_brick, prior_basis):
    size_x = lax.axis_size("gx")
    size_y = lax.axis_size("gy")
    size_z = lax.axis_size(GZ)
    plane_size = size_x * size_y
    slot_count = slot_snapshot.shape[0]
    pair_depth = slot_count // plane_size
    total_cells = CELLS * plane_size * size_z
    is_live = slot_snapshot >= 0
    slot_ids = jnp.arange(slot_count, dtype=jnp.int32)
    target_peer = jnp.where(is_live, slot_brick // size_z, plane_size)
    earlier = (target_peer[:, None] == target_peer[None, :]) & (
        slot_ids[None, :] < slot_ids[:, None]
    )
    pair_rank = jnp.sum(earlier.astype(jnp.int32), axis=1)
    position = jnp.where(is_live, target_peer * pair_depth + pair_rank, slot_count)
    slot_hits = position[:, None] == slot_ids[None, :]
    filled = jnp.any(slot_hits, axis=0)
    source = jnp.sum(jnp.where(slot_hits, slot_ids[:, None], 0), axis=0)
    sent_snapshot = jnp.where(filled, jnp.take(slot_snapshot, source), -1)
    payload = jnp.take(average_cells(patch_fields), source, axis=0)
    received, received_snapshot = (
        lax.all_to_all(payload, ("gx", "gy"), split_axis=0, concat_axis=0, tiled=True),
        lax.all_to_all(sent_snapshot, ("gx", "gy"), split_axis=0, concat_axis=0, tiled=True),
    )
    snapshots = jnp.arange(SNAPS, dtype=jnp.int32)
    chosen = jnp.sum(
        jnp.where(received_snapshot[None, :] == snapshots[:, None], slot_ids[None, :], 0), axis=1
    )
    arrived = jnp.take(received, chosen, axis=0)
    columns = arrived.reshape(COLS, CELLS)
    partial_gram = jnp.dot(columns, columns.T, preferred_element_type=jnp.float32)
    data_wide = columns.astype(jnp.float32).T
    data_block = columns.T.reshape(EDGE, EDGE, EDGE * COLS)
    data_xy = extended(data_block, (("gx", 0), ("gy", 1)), 1).astype(jnp.float32)
    data_z = extended_2(data_block, ((GZ, 2),), COLS).astype(jnp.float32)
    data_image = seven_point(data_block.astype(jnp.float32), data_xy, data_z, COLS).reshape(
        CELLS, COLS
    )
    partial_cross = jnp.dot(data_wide.T, data_image, precision=HIGHEST)
    totals = allreduce(jnp.concatenate([partial_gram, partial_cross], axis=1))
    gram_total, cross_total = totals[:, :COLS], totals[:, COLS:]
    gram_matrix = gram_total / total_cells
    coeffs = factor_basis(gram_matrix, prior_basis)
    mode_basis = jnp.dot(data_wide, coeffs, precision=HIGHEST)
    mode_image = jnp.dot(data_image, coeffs, precision=HIGHEST)
    inner = jnp.dot(cross_total / total_cells, coeffs, precision=HIGHEST)
    reduced = jnp.dot(coeffs.T, inner, precision=HIGHEST)
    mode_fields = mode_basis.reshape(EDGE, EDGE, EDGE * MODES).astype(jnp.bfloat16)
    diffused = mode_image.reshape(EDGE, EDGE, EDGE * MODES).astype(jnp.bfloat16)
    return (gram_matrix, mode_fields, diffused, reduced)


def solution(mesh):
    split = Mesh(
        mesh.devices.reshape(mesh.shape["gx"], mesh.shape["gy"], 4, 2), ("gx", "gy", "gz_0", "gz_1")
    )
    in_specs = (P(GX_GY_GZ, None, None), P(GX_GY_GZ), P(GX_GY_GZ), P())
    out_specs = (P(), P("gx", "gy", GZ), P("gx", "gy", GZ), P())
    return jax.shard_map(
        shards, mesh=split, in_specs=in_specs, out_specs=out_specs, check_vma=False
    )
```

```python
import functools

import jax
import jax.numpy as jnp
from jax import lax
from jax.sharding import Mesh
from jax.sharding import PartitionSpec as P
from jax.experimental import pallas as pl
from jax.experimental.pallas import tpu as pltpu

SNAPS = 16
FIELDS = 4
PATCH = 32
MODES = 32
EDGE = 16
CELLS = 4096
COLS = 64
GZ = ("gz_0", "gz_1")
GX_GY_GZ = ("gx", "gy", "gz_0", "gz_1")


HIGHEST = lax.Precision.HIGHEST


def extended(value, sides, width):
    edges = {}
    for axis, dim in sides:
        devices, length = (lax.axis_size(axis), value.shape[dim])
        up = [(i, (i + 1) % devices) for i in range(devices - 1)]
        last = lax.slice_in_dim(value, length - width, length, axis=dim)
        first = lax.slice_in_dim(value, 0, width, axis=dim)
        edges[dim] = (
            lax.ppermute(last, axis, up),
            lax.ppermute(first, axis, [(b, a) for a, b in up]),
        )
    done = []
    for _, dim in sides:
        low, high = edges[dim]
        around = [(width, width) if d in done else (0, 0) for d in range(value.ndim)]
        value = jnp.concatenate([jnp.pad(low, around), value, jnp.pad(high, around)], axis=dim)
        done.append(dim)
    return value


def extended_2(value, sides, width):
    for axis, dim in sides:
        devices, length = (lax.axis_size(axis), value.shape[dim])
        up = [(i, (i + 1) % devices) for i in range(devices - 1)]
        down = [(j, i) for i, j in up]
        last = lax.slice_in_dim(value, length - width, length, axis=dim)
        first = lax.slice_in_dim(value, 0, width, axis=dim)
        before = lax.ppermute(last, axis, up)
        after = lax.ppermute(first, axis, down)
        value = jnp.concatenate([before, value, after], axis=dim)
    return value


def over_axes(value, axes):
    for axis in axes:
        value = lax.psum(value, axis)
    return value


def pairing_matrix():
    fine = jnp.arange(2 * PATCH * PATCH, dtype=jnp.int32)
    fine_y = fine % (PATCH * PATCH) // PATCH
    fine_z = fine % PATCH
    coarse = jnp.arange(EDGE * EDGE, dtype=jnp.int32)
    hit = ((fine_y // 2 * EDGE + fine_z // 2)[:, None] == coarse[None, :])
    return jnp.where(hit, 0.125, 0.0).astype(jnp.bfloat16)


PAIRS_PER_STEP = 4


def average_kernel(fine_ref, pairing_ref, out_ref):
    rows = fine_ref.shape[0]
    span = 2 * PATCH * PATCH
    stacked = jnp.concatenate(
        [fine_ref[:, i * span : (i + 1) * span] for i in range(PAIRS_PER_STEP)], axis=0
    )
    means = jnp.dot(stacked, pairing_ref[...], preferred_element_type=jnp.float32)
    width = EDGE * EDGE
    for i in range(PAIRS_PER_STEP):
        out_ref[:, i * width : (i + 1) * width] = means[i * rows : (i + 1) * rows].astype(out_ref.dtype)


def average_cells(fine_data):
    row_count = fine_data.shape[0]
    rows = row_count * FIELDS
    flat = fine_data.reshape(rows, PATCH * PATCH * PATCH)
    span = 2 * PATCH * PATCH * PAIRS_PER_STEP
    width = EDGE * EDGE * PAIRS_PER_STEP
    steps = EDGE // PAIRS_PER_STEP
    means = pl.pallas_call(
        average_kernel,
        grid=(steps,),
        in_specs=[
            pl.BlockSpec((rows, span), lambda g: (0, g)),
            pl.BlockSpec((2 * PATCH * PATCH, EDGE * EDGE), lambda g: (0, 0)),
        ],
        out_specs=pl.BlockSpec((rows, width), lambda g: (0, g)),
        out_shape=jax.ShapeDtypeStruct((rows, CELLS), jnp.bfloat16),
    )(flat, pairing_matrix())
    return means.reshape(row_count, FIELDS, CELLS)


def seven_point(center, around_xy, around_z, stride):
    total = around_xy[2:, 1:-1] + around_xy[:-2, 1:-1] + around_xy[1:-1, 2:] + around_xy[1:-1, :-2]
    total = total + around_z[:, :, 2 * stride :] + around_z[:, :, : -2 * stride]
    return total - 6.0 * center


def factor_basis(gram_matrix, prior_basis):
    lower_factor = jnp.linalg.cholesky(gram_matrix)
    return lax.linalg.triangular_solve(
        lower_factor, prior_basis, left_side=True, lower=True, transpose_a=True
    )


def tree_sum(values):
    while len(values) > 1:
        values = [values[i] + values[i + 1] for i in range(0, len(values), 2)]
    return values[0]


def allreduce_kernel(sizes, part_ref, out_ref, acc, *rest):
    bufs, (send_sems, recv_sems) = rest[: len(sizes)], rest[len(sizes) :]
    me = [lax.axis_index(axis) for axis in GX_GY_GZ]

    def peer(dim, step):
        device = list(me)
        device[dim] = lax.rem(me[dim] + step, sizes[dim])
        return tuple(device)

    barrier = pltpu.get_barrier_semaphore()
    count = 0
    for dim, size in enumerate(sizes):
        for step in range(1, size):
            pl.semaphore_signal(
                barrier, inc=1, device_id=peer(dim, step), device_id_type=pl.DeviceIdType.MESH
            )
            count += 1
    pl.semaphore_wait(barrier, count)
    acc[...] = part_ref[...]
    slot = 0
    for dim, size in enumerate(sizes):
        if size == 1:
            continue
        buf = bufs[dim]
        copies = []
        for step in range(1, size):
            copy = pltpu.make_async_remote_copy(
                src_ref=acc,
                dst_ref=buf.at[step - 1],
                send_sem=send_sems.at[slot],
                recv_sem=recv_sems.at[slot],
                device_id=peer(dim, step),
                device_id_type=pl.DeviceIdType.MESH,
            )
            copy.start()
            copies.append(copy)
            slot += 1
        for copy in copies:
            copy.wait()
        own = acc[...]
        values = []
        for source in range(size):
            held = jnp.maximum(lax.rem(me[dim] - source + size, size) - 1, 0)
            values.append(jnp.where(me[dim] == source, own, buf[held]))
        acc[...] = tree_sum(values)
    out_ref[...] = acc[...]


def allreduce(part):
    sizes = tuple(lax.axis_size(axis) for axis in GX_GY_GZ)
    copies = sum(size - 1 for size in sizes)
    return pl.pallas_call(
        functools.partial(allreduce_kernel, sizes),
        out_shape=jax.ShapeDtypeStruct(part.shape, part.dtype),
        in_specs=[pl.BlockSpec(memory_space=pltpu.VMEM)],
        out_specs=pl.BlockSpec(memory_space=pltpu.VMEM),
        scratch_shapes=[pltpu.VMEM(part.shape, part.dtype)]
        + [pltpu.VMEM((max(size - 1, 1),) + part.shape, part.dtype) for size in sizes]
        + [pltpu.SemaphoreType.DMA((copies,)), pltpu.SemaphoreType.DMA((copies,))],
        compiler_params=pltpu.CompilerParams(collective_id=0, has_side_effects=True),
    )(part)


def exchange_kernel(plane, size_y, payload_ref, ids_ref, out_ref, out_ids_ref, send_sems, recv_sems, local_sems):
    me = lax.axis_index("gx") * size_y + lax.axis_index("gy")
    rest = tuple(lax.axis_index(axis) for axis in GZ)

    def device(step):
        target = lax.rem(me + step, plane)
        return (target // size_y, lax.rem(target, size_y)) + rest

    barrier = pltpu.get_barrier_semaphore()
    for step in range(1, plane):
        pl.semaphore_signal(barrier, inc=1, device_id=device(step), device_id_type=pl.DeviceIdType.MESH)
    pl.semaphore_wait(barrier, plane - 1)
    pairs = ((payload_ref, out_ref), (ids_ref, out_ids_ref))
    copies = []
    for index, (src, dst) in enumerate(pairs):
        copy = pltpu.make_async_copy(src.at[me], dst.at[me], local_sems.at[index])
        copy.start()
        copies.append(copy)
    for step in range(1, plane):
        target = lax.rem(me + step, plane)
        for index, (src, dst) in enumerate(pairs):
            slot = 2 * (step - 1) + index
            copy = pltpu.make_async_remote_copy(
                src_ref=src.at[target],
                dst_ref=dst.at[me],
                send_sem=send_sems.at[slot],
                recv_sem=recv_sems.at[slot],
                device_id=device(step),
                device_id_type=pl.DeviceIdType.MESH,
            )
            copy.start()
            copies.append(copy)
    for copy in copies:
        copy.wait()


def exchange(payload, ids):
    size_y = lax.axis_size("gy")
    plane = lax.axis_size("gx") * size_y
    vmem = pl.BlockSpec(memory_space=pltpu.VMEM)
    return pl.pallas_call(
        functools.partial(exchange_kernel, plane, size_y),
        out_shape=(
            jax.ShapeDtypeStruct(payload.shape, payload.dtype),
            jax.ShapeDtypeStruct(ids.shape, ids.dtype),
        ),
        in_specs=[vmem, vmem],
        out_specs=(vmem, vmem),
        scratch_shapes=[
            pltpu.SemaphoreType.DMA((2 * (plane - 1),)),
            pltpu.SemaphoreType.DMA((2 * (plane - 1),)),
            pltpu.SemaphoreType.DMA((2,)),
        ],
        compiler_params=pltpu.CompilerParams(collective_id=1, has_side_effects=True),
    )(payload, ids)


def shards(patch_fields, slot_snapshot, slot_brick, prior_basis):
    size_x = lax.axis_size("gx")
    size_y = lax.axis_size("gy")
    size_z = lax.axis_size(GZ)
    plane_size = size_x * size_y
    slot_count = slot_snapshot.shape[0]
    pair_depth = slot_count // plane_size
    total_cells = CELLS * plane_size * size_z
    is_live = slot_snapshot >= 0
    slot_ids = jnp.arange(slot_count, dtype=jnp.int32)
    target_peer = jnp.where(is_live, slot_brick // size_z, plane_size)
    earlier = (target_peer[:, None] == target_peer[None, :]) & (
        slot_ids[None, :] < slot_ids[:, None]
    )
    pair_rank = jnp.sum(earlier.astype(jnp.int32), axis=1)
    position = jnp.where(is_live, target_peer * pair_depth + pair_rank, slot_count)
    slot_hits = position[:, None] == slot_ids[None, :]
    filled = jnp.any(slot_hits, axis=0)
    source = jnp.sum(jnp.where(slot_hits, slot_ids[:, None], 0), axis=0)
    sent_snapshot = jnp.where(filled, jnp.take(slot_snapshot, source), -1)
    payload = jnp.take(average_cells(patch_fields), source, axis=0)
    sent_ids = jnp.broadcast_to(sent_snapshot[:, None, None], (slot_count, 8, 128))
    received, received_ids = exchange(payload, sent_ids)
    received_snapshot = received_ids[:, 0, 0]
    snapshots = jnp.arange(SNAPS, dtype=jnp.int32)
    chosen = jnp.sum(
        jnp.where(received_snapshot[None, :] == snapshots[:, None], slot_ids[None, :], 0), axis=1
    )
    arrived = jnp.take(received, chosen, axis=0)
    columns = arrived.reshape(COLS, CELLS)
    partial_gram = jnp.dot(columns, columns.T, preferred_element_type=jnp.float32)
    data_wide = columns.astype(jnp.float32).T
    data_block = columns.T.reshape(EDGE, EDGE, EDGE * COLS)
    data_xy = extended(data_block, (("gx", 0), ("gy", 1)), 1).astype(jnp.float32)
    data_z = extended_2(data_block, ((GZ, 2),), COLS).astype(jnp.float32)
    data_image = seven_point(data_block.astype(jnp.float32), data_xy, data_z, COLS).reshape(
        CELLS, COLS
    )
    partial_cross = jnp.dot(data_wide.T, data_image, precision=HIGHEST)
    totals = allreduce(jnp.concatenate([partial_gram, partial_cross], axis=1))
    gram_total, cross_total = totals[:, :COLS], totals[:, COLS:]
    gram_matrix = gram_total / total_cells
    coeffs = factor_basis(gram_matrix, prior_basis)
    mode_basis = jnp.dot(data_wide, coeffs, precision=HIGHEST)
    mode_image = jnp.dot(data_image, coeffs, precision=HIGHEST)
    inner = jnp.dot(cross_total / total_cells, coeffs, precision=HIGHEST)
    reduced = jnp.dot(coeffs.T, inner, precision=HIGHEST)
    mode_fields = mode_basis.reshape(EDGE, EDGE, EDGE * MODES).astype(jnp.bfloat16)
    diffused = mode_image.reshape(EDGE, EDGE, EDGE * MODES).astype(jnp.bfloat16)
    return (gram_matrix, mode_fields, diffused, reduced)


def solution(mesh):
    split = Mesh(
        mesh.devices.reshape(mesh.shape["gx"], mesh.shape["gy"], 4, 2), ("gx", "gy", "gz_0", "gz_1")
    )
    in_specs = (P(GX_GY_GZ, None, None), P(GX_GY_GZ), P(GX_GY_GZ), P())
    out_specs = (P(), P("gx", "gy", GZ), P("gx", "gy", GZ), P())
    return jax.shard_map(
        shards, mesh=split, in_specs=in_specs, out_specs=out_specs, check_vma=False
    )
```

```python
import functools

import jax
import jax.numpy as jnp
from jax import lax
from jax.sharding import Mesh
from jax.sharding import PartitionSpec as P
from jax.experimental import pallas as pl
from jax.experimental.pallas import tpu as pltpu

SNAPS = 16
FIELDS = 4
PATCH = 32
MODES = 32
EDGE = 16
CELLS = 4096
COLS = 64
GZ = ("gz_0", "gz_1")
GX_GY_GZ = ("gx", "gy", "gz_0", "gz_1")


HIGHEST = lax.Precision.HIGHEST


def extended(value, sides, width):
    edges = {}
    for axis, dim in sides:
        devices, length = (lax.axis_size(axis), value.shape[dim])
        up = [(i, (i + 1) % devices) for i in range(devices - 1)]
        last = lax.slice_in_dim(value, length - width, length, axis=dim)
        first = lax.slice_in_dim(value, 0, width, axis=dim)
        edges[dim] = (
            lax.ppermute(last, axis, up),
            lax.ppermute(first, axis, [(b, a) for a, b in up]),
        )
    done = []
    for _, dim in sides:
        low, high = edges[dim]
        around = [(width, width) if d in done else (0, 0) for d in range(value.ndim)]
        value = jnp.concatenate([jnp.pad(low, around), value, jnp.pad(high, around)], axis=dim)
        done.append(dim)
    return value


def extended_2(value, sides, width):
    for axis, dim in sides:
        devices, length = (lax.axis_size(axis), value.shape[dim])
        up = [(i, (i + 1) % devices) for i in range(devices - 1)]
        down = [(j, i) for i, j in up]
        last = lax.slice_in_dim(value, length - width, length, axis=dim)
        first = lax.slice_in_dim(value, 0, width, axis=dim)
        before = lax.ppermute(last, axis, up)
        after = lax.ppermute(first, axis, down)
        value = jnp.concatenate([before, value, after], axis=dim)
    return value


def over_axes(value, axes):
    for axis in axes:
        value = lax.psum(value, axis)
    return value


def pairing_matrix():
    fine = jnp.arange(2 * PATCH * PATCH, dtype=jnp.int32)
    fine_y = fine % (PATCH * PATCH) // PATCH
    fine_z = fine % PATCH
    coarse = jnp.arange(EDGE * EDGE, dtype=jnp.int32)
    hit = ((fine_y // 2 * EDGE + fine_z // 2)[:, None] == coarse[None, :])
    return jnp.where(hit, 0.125, 0.0).astype(jnp.bfloat16)


PAIRS_PER_STEP = 4


def average_kernel(fine_ref, pairing_ref, out_ref):
    slots = fine_ref.shape[0]
    rows = slots * FIELDS
    span = 2 * PATCH * PATCH
    stacked = jnp.concatenate(
        [fine_ref[:, :, i * span : (i + 1) * span].reshape(rows, span) for i in range(PAIRS_PER_STEP)],
        axis=0,
    )
    means = jnp.dot(stacked, pairing_ref[...], preferred_element_type=jnp.float32)
    width = EDGE * EDGE
    for i in range(PAIRS_PER_STEP):
        out_ref[:, :, i * width : (i + 1) * width] = (
            means[i * rows : (i + 1) * rows].reshape(slots, FIELDS, width).astype(out_ref.dtype)
        )


def average_cells(fine_data):
    row_count = fine_data.shape[0]
    span = 2 * PATCH * PATCH * PAIRS_PER_STEP
    width = EDGE * EDGE * PAIRS_PER_STEP
    steps = EDGE // PAIRS_PER_STEP
    return pl.pallas_call(
        average_kernel,
        grid=(steps,),
        in_specs=[
            pl.BlockSpec((row_count, FIELDS, span), lambda g: (0, 0, g)),
            pl.BlockSpec((2 * PATCH * PATCH, EDGE * EDGE), lambda g: (0, 0)),
        ],
        out_specs=pl.BlockSpec((row_count, FIELDS, width), lambda g: (0, 0, g)),
        out_shape=jax.ShapeDtypeStruct((row_count, FIELDS, CELLS), jnp.bfloat16),
    )(fine_data, pairing_matrix())


def seven_point(center, around_xy, around_z, stride):
    total = around_xy[2:, 1:-1] + around_xy[:-2, 1:-1] + around_xy[1:-1, 2:] + around_xy[1:-1, :-2]
    total = total + around_z[:, :, 2 * stride :] + around_z[:, :, : -2 * stride]
    return total - 6.0 * center


def factor_basis(gram_matrix, prior_basis):
    lower_factor = jnp.linalg.cholesky(gram_matrix)
    return lax.linalg.triangular_solve(
        lower_factor, prior_basis, left_side=True, lower=True, transpose_a=True
    )


def tree_sum(values):
    while len(values) > 1:
        values = [values[i] + values[i + 1] for i in range(0, len(values), 2)]
    return values[0]


REDUCE_GROUPS = (("gx", "gz_1"), ("gy",), ("gz_0",))


def allreduce_kernel(groups, part_ref, out_ref, acc, *rest):
    bufs, (send_sems, recv_sems) = rest[: len(groups)], rest[len(groups) :]
    me = {axis: lax.axis_index(axis) for group in groups for axis, _ in group}

    def linear(group):
        index = 0
        for axis, size in group:
            index = index * size + me[axis]
        return index

    def peer(group, step):
        count = 1
        for _, size in group:
            count *= size
        target = lax.rem(linear(group) + step, count)
        device = dict(me)
        for axis, size in reversed(group):
            device[axis] = lax.rem(target, size)
            target = target // size
        return tuple(device[axis] for axis in GX_GY_GZ)

    counts = []
    for group in groups:
        count = 1
        for _, size in group:
            count *= size
        counts.append(count)
    barrier = pltpu.get_barrier_semaphore()
    for group, count in zip(groups, counts):
        for step in range(1, count):
            pl.semaphore_signal(
                barrier, inc=1, device_id=peer(group, step), device_id_type=pl.DeviceIdType.MESH
            )
    pl.semaphore_wait(barrier, sum(counts) - len(counts))
    acc[...] = part_ref[...]
    slot = 0
    for group, count, buf in zip(groups, counts, bufs):
        copies = []
        for step in range(1, count):
            copy = pltpu.make_async_remote_copy(
                src_ref=acc,
                dst_ref=buf.at[step - 1],
                send_sem=send_sems.at[slot],
                recv_sem=recv_sems.at[slot],
                device_id=peer(group, step),
                device_id_type=pl.DeviceIdType.MESH,
            )
            copy.start()
            copies.append(copy)
            slot += 1
        for copy in copies:
            copy.wait()
        own = acc[...]
        mine = linear(group)
        values = []
        for source in range(count):
            held = jnp.maximum(lax.rem(mine - source + count, count) - 1, 0)
            values.append(jnp.where(mine == source, own, buf[held]))
        acc[...] = tree_sum(values)
    out_ref[...] = acc[...]


def allreduce(part):
    groups = tuple(
        tuple((axis, lax.axis_size(axis)) for axis in group) for group in REDUCE_GROUPS
    )
    counts = [functools.reduce(lambda a, b: a * b, [size for _, size in group]) for group in groups]
    copies = sum(count - 1 for count in counts)
    return pl.pallas_call(
        functools.partial(allreduce_kernel, groups),
        out_shape=jax.ShapeDtypeStruct(part.shape, part.dtype),
        in_specs=[pl.BlockSpec(memory_space=pltpu.VMEM)],
        out_specs=pl.BlockSpec(memory_space=pltpu.VMEM),
        scratch_shapes=[pltpu.VMEM(part.shape, part.dtype)]
        + [pltpu.VMEM((max(count - 1, 1),) + part.shape, part.dtype) for count in counts]
        + [pltpu.SemaphoreType.DMA((copies,)), pltpu.SemaphoreType.DMA((copies,))],
        compiler_params=pltpu.CompilerParams(collective_id=0, has_side_effects=True),
    )(part)


def exchange_kernel(plane, size_y, payload_ref, ids_ref, out_ref, out_ids_ref, send_sems, recv_sems, local_sems):
    me = lax.axis_index("gx") * size_y + lax.axis_index("gy")
    rest = tuple(lax.axis_index(axis) for axis in GZ)

    def device(step):
        target = lax.rem(me + step, plane)
        return (target // size_y, lax.rem(target, size_y)) + rest

    barrier = pltpu.get_barrier_semaphore()
    for step in range(1, plane):
        pl.semaphore_signal(barrier, inc=1, device_id=device(step), device_id_type=pl.DeviceIdType.MESH)
    pl.semaphore_wait(barrier, plane - 1)
    pairs = ((payload_ref, out_ref), (ids_ref, out_ids_ref))
    copies = []
    for index, (src, dst) in enumerate(pairs):
        copy = pltpu.make_async_copy(src.at[me], dst.at[me], local_sems.at[index])
        copy.start()
        copies.append(copy)
    for step in range(1, plane):
        target = lax.rem(me + step, plane)
        for index, (src, dst) in enumerate(pairs):
            slot = 2 * (step - 1) + index
            copy = pltpu.make_async_remote_copy(
                src_ref=src.at[target],
                dst_ref=dst.at[me],
                send_sem=send_sems.at[slot],
                recv_sem=recv_sems.at[slot],
                device_id=device(step),
                device_id_type=pl.DeviceIdType.MESH,
            )
            copy.start()
            copies.append(copy)
    for copy in copies:
        copy.wait()


def exchange(payload, ids):
    size_y = lax.axis_size("gy")
    plane = lax.axis_size("gx") * size_y
    vmem = pl.BlockSpec(memory_space=pltpu.VMEM)
    return pl.pallas_call(
        functools.partial(exchange_kernel, plane, size_y),
        out_shape=(
            jax.ShapeDtypeStruct(payload.shape, payload.dtype),
            jax.ShapeDtypeStruct(ids.shape, ids.dtype),
        ),
        in_specs=[vmem, vmem],
        out_specs=(vmem, vmem),
        scratch_shapes=[
            pltpu.SemaphoreType.DMA((2 * (plane - 1),)),
            pltpu.SemaphoreType.DMA((2 * (plane - 1),)),
            pltpu.SemaphoreType.DMA((2,)),
        ],
        compiler_params=pltpu.CompilerParams(collective_id=1, has_side_effects=True),
    )(payload, ids)


def shards(patch_fields, slot_snapshot, slot_brick, prior_basis):
    size_x = lax.axis_size("gx")
    size_y = lax.axis_size("gy")
    size_z = lax.axis_size(GZ)
    plane_size = size_x * size_y
    slot_count = slot_snapshot.shape[0]
    pair_depth = slot_count // plane_size
    total_cells = CELLS * plane_size * size_z
    is_live = slot_snapshot >= 0
    slot_ids = jnp.arange(slot_count, dtype=jnp.int32)
    target_peer = jnp.where(is_live, slot_brick // size_z, plane_size)
    earlier = (target_peer[:, None] == target_peer[None, :]) & (
        slot_ids[None, :] < slot_ids[:, None]
    )
    pair_rank = jnp.sum(earlier.astype(jnp.int32), axis=1)
    position = jnp.where(is_live, target_peer * pair_depth + pair_rank, slot_count)
    slot_hits = position[:, None] == slot_ids[None, :]
    filled = jnp.any(slot_hits, axis=0)
    source = jnp.sum(jnp.where(slot_hits, slot_ids[:, None], 0), axis=0)
    sent_snapshot = jnp.where(filled, jnp.take(slot_snapshot, source), -1)
    payload = jnp.take(average_cells(patch_fields), source, axis=0)
    sent_ids = jnp.broadcast_to(sent_snapshot[:, None, None], (slot_count, 8, 128))
    received, received_ids = exchange(payload, sent_ids)
    received_snapshot = received_ids[:, 0, 0]
    snapshots = jnp.arange(SNAPS, dtype=jnp.int32)
    chosen = jnp.sum(
        jnp.where(received_snapshot[None, :] == snapshots[:, None], slot_ids[None, :], 0), axis=1
    )
    arrived = jnp.take(received, chosen, axis=0)
    columns = arrived.reshape(COLS, CELLS)
    partial_gram = jnp.dot(columns, columns.T, preferred_element_type=jnp.float32)
    data_wide = columns.astype(jnp.float32).T
    data_block = columns.T.reshape(EDGE, EDGE, EDGE * COLS)
    data_xy = extended(data_block, (("gx", 0), ("gy", 1)), 1).astype(jnp.float32)
    data_z = extended_2(data_block, ((GZ, 2),), COLS).astype(jnp.float32)
    data_image = seven_point(data_block.astype(jnp.float32), data_xy, data_z, COLS).reshape(
        CELLS, COLS
    )
    partial_cross = jnp.dot(data_wide.T, data_image, precision=HIGHEST)
    totals = allreduce(jnp.concatenate([partial_gram, partial_cross], axis=1))
    gram_total, cross_total = totals[:, :COLS], totals[:, COLS:]
    gram_matrix = gram_total / total_cells
    coeffs = factor_basis(gram_matrix, prior_basis)
    mode_basis = jnp.dot(data_wide, coeffs, precision=HIGHEST)
    mode_image = jnp.dot(data_image, coeffs, precision=HIGHEST)
    inner = jnp.dot(cross_total / total_cells, coeffs, precision=HIGHEST)
    reduced = jnp.dot(coeffs.T, inner, precision=HIGHEST)
    mode_fields = mode_basis.reshape(EDGE, EDGE, EDGE * MODES).astype(jnp.bfloat16)
    diffused = mode_image.reshape(EDGE, EDGE, EDGE * MODES).astype(jnp.bfloat16)
    return (gram_matrix, mode_fields, diffused, reduced)


def solution(mesh):
    split = Mesh(
        mesh.devices.reshape(mesh.shape["gx"], mesh.shape["gy"], 4, 2), ("gx", "gy", "gz_0", "gz_1")
    )
    in_specs = (P(GX_GY_GZ, None, None), P(GX_GY_GZ), P(GX_GY_GZ), P())
    out_specs = (P(), P("gx", "gy", GZ), P("gx", "gy", GZ), P())
    return jax.shard_map(
        shards, mesh=split, in_specs=in_specs, out_specs=out_specs, check_vma=False
    )
```

```python
import functools

import jax
import jax.numpy as jnp
from jax import lax
from jax.sharding import Mesh
from jax.sharding import PartitionSpec as P
from jax.experimental import pallas as pl
from jax.experimental.pallas import tpu as pltpu

SNAPS = 16
FIELDS = 4
PATCH = 32
MODES = 32
EDGE = 16
CELLS = 4096
COLS = 64
GZ = ("gz_0", "gz_1")
GX_GY_GZ = ("gx", "gy", "gz_0", "gz_1")


HIGHEST = lax.Precision.HIGHEST


def extended(value, sides, width):
    edges = {}
    for axis, dim in sides:
        devices, length = (lax.axis_size(axis), value.shape[dim])
        up = [(i, (i + 1) % devices) for i in range(devices - 1)]
        last = lax.slice_in_dim(value, length - width, length, axis=dim)
        first = lax.slice_in_dim(value, 0, width, axis=dim)
        edges[dim] = (
            lax.ppermute(last, axis, up),
            lax.ppermute(first, axis, [(b, a) for a, b in up]),
        )
    done = []
    for _, dim in sides:
        low, high = edges[dim]
        around = [(width, width) if d in done else (0, 0) for d in range(value.ndim)]
        value = jnp.concatenate([jnp.pad(low, around), value, jnp.pad(high, around)], axis=dim)
        done.append(dim)
    return value


def extended_2(value, sides, width):
    for axis, dim in sides:
        devices, length = (lax.axis_size(axis), value.shape[dim])
        up = [(i, (i + 1) % devices) for i in range(devices - 1)]
        down = [(j, i) for i, j in up]
        last = lax.slice_in_dim(value, length - width, length, axis=dim)
        first = lax.slice_in_dim(value, 0, width, axis=dim)
        before = lax.ppermute(last, axis, up)
        after = lax.ppermute(first, axis, down)
        value = jnp.concatenate([before, value, after], axis=dim)
    return value


def over_axes(value, axes):
    for axis in axes:
        value = lax.psum(value, axis)
    return value


def pairing_matrix():
    fine = jnp.arange(2 * PATCH * PATCH, dtype=jnp.int32)
    fine_y = fine % (PATCH * PATCH) // PATCH
    fine_z = fine % PATCH
    coarse = jnp.arange(EDGE * EDGE, dtype=jnp.int32)
    hit = ((fine_y // 2 * EDGE + fine_z // 2)[:, None] == coarse[None, :])
    return jnp.where(hit, 0.125, 0.0).astype(jnp.bfloat16)


PAIRS_PER_STEP = 4


def average_kernel(fine_ref, pairing_ref, out_ref):
    slots = fine_ref.shape[0]
    rows = slots * FIELDS
    span = 2 * PATCH * PATCH
    stacked = jnp.concatenate(
        [fine_ref[:, :, i * span : (i + 1) * span].reshape(rows, span) for i in range(PAIRS_PER_STEP)],
        axis=0,
    )
    means = jnp.dot(stacked, pairing_ref[...], preferred_element_type=jnp.float32)
    width = EDGE * EDGE
    for i in range(PAIRS_PER_STEP):
        out_ref[:, :, i * width : (i + 1) * width] = (
            means[i * rows : (i + 1) * rows].reshape(slots, FIELDS, width).astype(out_ref.dtype)
        )


def average_cells(fine_data):
    row_count = fine_data.shape[0]
    span = 2 * PATCH * PATCH * PAIRS_PER_STEP
    width = EDGE * EDGE * PAIRS_PER_STEP
    steps = EDGE // PAIRS_PER_STEP
    return pl.pallas_call(
        average_kernel,
        grid=(steps,),
        in_specs=[
            pl.BlockSpec((row_count, FIELDS, span), lambda g: (0, 0, g)),
            pl.BlockSpec((2 * PATCH * PATCH, EDGE * EDGE), lambda g: (0, 0)),
        ],
        out_specs=pl.BlockSpec((row_count, FIELDS, width), lambda g: (0, 0, g)),
        out_shape=jax.ShapeDtypeStruct((row_count, FIELDS, CELLS), jnp.bfloat16),
    )(fine_data, pairing_matrix())


def seven_point(center, around_xy, around_z, stride):
    total = around_xy[2:, 1:-1] + around_xy[:-2, 1:-1] + around_xy[1:-1, 2:] + around_xy[1:-1, :-2]
    total = total + around_z[:, :, 2 * stride :] + around_z[:, :, : -2 * stride]
    return total - 6.0 * center


def factor_basis(gram_matrix, prior_basis):
    lower_factor = jnp.linalg.cholesky(gram_matrix)
    return lax.linalg.triangular_solve(
        lower_factor, prior_basis, left_side=True, lower=True, transpose_a=True
    )


def tree_sum(values):
    while len(values) > 1:
        values = [values[i] + values[i + 1] for i in range(0, len(values), 2)]
    return values[0]


REDUCE_GROUPS = (("gx", "gz_1"), ("gy",), ("gz_0",))


def allreduce_kernel(groups, part_ref, out_ref, acc, *rest):
    bufs, (send_sems, recv_sems) = rest[: len(groups)], rest[len(groups) :]
    me = {axis: lax.axis_index(axis) for group in groups for axis, _ in group}

    def linear(group):
        index = 0
        for axis, size in group:
            index = index * size + me[axis]
        return index

    def peer(group, step):
        count = 1
        for _, size in group:
            count *= size
        target = lax.rem(linear(group) + step, count)
        device = dict(me)
        for axis, size in reversed(group):
            device[axis] = lax.rem(target, size)
            target = target // size
        return tuple(device[axis] for axis in GX_GY_GZ)

    counts = []
    for group in groups:
        count = 1
        for _, size in group:
            count *= size
        counts.append(count)
    barrier = pltpu.get_barrier_semaphore()
    for group, count in zip(groups, counts):
        for step in range(1, count):
            pl.semaphore_signal(
                barrier, inc=1, device_id=peer(group, step), device_id_type=pl.DeviceIdType.MESH
            )
    pl.semaphore_wait(barrier, sum(counts) - len(counts))
    acc[...] = part_ref[...]
    slot = 0
    for group, count, buf in zip(groups, counts, bufs):
        copies = []
        for step in range(1, count):
            copy = pltpu.make_async_remote_copy(
                src_ref=acc,
                dst_ref=buf.at[step - 1],
                send_sem=send_sems.at[slot],
                recv_sem=recv_sems.at[slot],
                device_id=peer(group, step),
                device_id_type=pl.DeviceIdType.MESH,
            )
            copy.start()
            copies.append(copy)
            slot += 1
        for copy in copies:
            copy.wait()
        own = acc[...]
        mine = linear(group)
        values = []
        for source in range(count):
            held = jnp.maximum(lax.rem(mine - source + count, count) - 1, 0)
            values.append(jnp.where(mine == source, own, buf[held]))
        acc[...] = tree_sum(values)
    out_ref[...] = acc[...]


def allreduce(part):
    groups = tuple(
        tuple((axis, lax.axis_size(axis)) for axis in group) for group in REDUCE_GROUPS
    )
    counts = [functools.reduce(lambda a, b: a * b, [size for _, size in group]) for group in groups]
    copies = sum(count - 1 for count in counts)
    return pl.pallas_call(
        functools.partial(allreduce_kernel, groups),
        out_shape=jax.ShapeDtypeStruct(part.shape, part.dtype),
        in_specs=[pl.BlockSpec(memory_space=pltpu.VMEM)],
        out_specs=pl.BlockSpec(memory_space=pltpu.VMEM),
        scratch_shapes=[pltpu.VMEM(part.shape, part.dtype)]
        + [pltpu.VMEM((max(count - 1, 1),) + part.shape, part.dtype) for count in counts]
        + [pltpu.SemaphoreType.DMA((copies,)), pltpu.SemaphoreType.DMA((copies,))],
        compiler_params=pltpu.CompilerParams(collective_id=0, has_side_effects=True),
    )(part)


def exchange_kernel(plane, size_y, payload_ref, ids_ref, out_ref, out_ids_ref, send_sems, recv_sems, local_sems):
    me = lax.axis_index("gx") * size_y + lax.axis_index("gy")
    rest = tuple(lax.axis_index(axis) for axis in GZ)

    def device(step):
        target = lax.rem(me + step, plane)
        return (target // size_y, lax.rem(target, size_y)) + rest

    barrier = pltpu.get_barrier_semaphore()
    for step in range(1, plane):
        pl.semaphore_signal(barrier, inc=1, device_id=device(step), device_id_type=pl.DeviceIdType.MESH)
    pl.semaphore_wait(barrier, plane - 1)
    pairs = ((payload_ref, out_ref), (ids_ref, out_ids_ref))
    copies = []
    for index, (src, dst) in enumerate(pairs):
        copy = pltpu.make_async_copy(src.at[me], dst.at[me], local_sems.at[index])
        copy.start()
        copies.append(copy)
    for step in range(1, plane):
        target = lax.rem(me + step, plane)
        for index, (src, dst) in enumerate(pairs):
            slot = 2 * (step - 1) + index
            copy = pltpu.make_async_remote_copy(
                src_ref=src.at[target],
                dst_ref=dst.at[me],
                send_sem=send_sems.at[slot],
                recv_sem=recv_sems.at[slot],
                device_id=device(step),
                device_id_type=pl.DeviceIdType.MESH,
            )
            copy.start()
            copies.append(copy)
    for copy in copies:
        copy.wait()


def exchange(payload, ids):
    size_y = lax.axis_size("gy")
    plane = lax.axis_size("gx") * size_y
    vmem = pl.BlockSpec(memory_space=pltpu.VMEM)
    return pl.pallas_call(
        functools.partial(exchange_kernel, plane, size_y),
        out_shape=(
            jax.ShapeDtypeStruct(payload.shape, payload.dtype),
            jax.ShapeDtypeStruct(ids.shape, ids.dtype),
        ),
        in_specs=[vmem, vmem],
        out_specs=(vmem, vmem),
        scratch_shapes=[
            pltpu.SemaphoreType.DMA((2 * (plane - 1),)),
            pltpu.SemaphoreType.DMA((2 * (plane - 1),)),
            pltpu.SemaphoreType.DMA((2,)),
        ],
        compiler_params=pltpu.CompilerParams(collective_id=1, has_side_effects=True),
    )(payload, ids)


def halo_kernel(sizes, faces_ref, out_ref, send_sems, recv_sems):
    me = [lax.axis_index(axis) for axis in GX_GY_GZ]
    size_z1 = sizes[3]
    size_z = sizes[2] * size_z1

    def device(dim, step):
        if dim < 2:
            place = list(me)
            place[dim] = lax.rem(me[dim] + step + sizes[dim], sizes[dim])
            return tuple(place)
        z = lax.rem(me[2] * size_z1 + me[3] + step + size_z, size_z)
        return (me[0], me[1], z // size_z1, lax.rem(z, size_z1))

    targets = [device(dim, step) for dim in range(3) for step in (-1, 1)]
    barrier = pltpu.get_barrier_semaphore()
    for target in targets:
        pl.semaphore_signal(barrier, inc=1, device_id=target, device_id_type=pl.DeviceIdType.MESH)
    pl.semaphore_wait(barrier, len(targets))
    copies = []
    for index, target in enumerate(targets):
        copy = pltpu.make_async_remote_copy(
            src_ref=faces_ref.at[index],
            dst_ref=out_ref.at[index],
            send_sem=send_sems.at[index],
            recv_sem=recv_sems.at[index],
            device_id=target,
            device_id_type=pl.DeviceIdType.MESH,
        )
        copy.start()
        copies.append(copy)
    for copy in copies:
        copy.wait()


def halo(faces):
    sizes = tuple(lax.axis_size(axis) for axis in GX_GY_GZ)
    vmem = pl.BlockSpec(memory_space=pltpu.VMEM)
    return pl.pallas_call(
        functools.partial(halo_kernel, sizes),
        out_shape=jax.ShapeDtypeStruct(faces.shape, faces.dtype),
        in_specs=[vmem],
        out_specs=vmem,
        scratch_shapes=[
            pltpu.SemaphoreType.DMA((faces.shape[0],)),
            pltpu.SemaphoreType.DMA((faces.shape[0],)),
        ],
        compiler_params=pltpu.CompilerParams(collective_id=2, has_side_effects=True),
    )(faces)


def diffusion(data_block):
    edge = data_block.shape[0]
    cells = edge * COLS
    faces = jnp.stack(
        [
            data_block[0],
            data_block[-1],
            data_block[:, 0],
            data_block[:, -1],
            data_block[:, :, :COLS].reshape(edge, cells),
            data_block[:, :, -COLS:].reshape(edge, cells),
        ]
    )
    got = halo(faces).astype(jnp.float32)
    gx, gy, gz = lax.axis_index("gx"), lax.axis_index("gy"), lax.axis_index(GZ)
    last = (lax.axis_size("gx") - 1, lax.axis_size("gy") - 1, lax.axis_size(GZ) - 1)
    above_x = jnp.where(gx < last[0], got[0], 0.0)
    below_x = jnp.where(gx > 0, got[1], 0.0)
    above_y = jnp.where(gy < last[1], got[2], 0.0)
    below_y = jnp.where(gy > 0, got[3], 0.0)
    above_z = jnp.where(gz < last[2], got[4], 0.0).reshape(edge, edge, COLS)
    below_z = jnp.where(gz > 0, got[5], 0.0).reshape(edge, edge, COLS)
    center = data_block.astype(jnp.float32)
    along_x = jnp.concatenate([below_x[None], center, above_x[None]], axis=0)
    along_y = jnp.concatenate([below_y[:, None], center, above_y[:, None]], axis=1)
    along_z = jnp.concatenate([below_z, center, above_z], axis=2)
    total = along_x[2:] + along_x[:-2] + along_y[:, 2:] + along_y[:, :-2]
    total = total + along_z[:, :, 2 * COLS :] + along_z[:, :, : -2 * COLS]
    return total - 6.0 * center


def shards(patch_fields, slot_snapshot, slot_brick, prior_basis):
    size_x = lax.axis_size("gx")
    size_y = lax.axis_size("gy")
    size_z = lax.axis_size(GZ)
    plane_size = size_x * size_y
    slot_count = slot_snapshot.shape[0]
    pair_depth = slot_count // plane_size
    total_cells = CELLS * plane_size * size_z
    is_live = slot_snapshot >= 0
    slot_ids = jnp.arange(slot_count, dtype=jnp.int32)
    target_peer = jnp.where(is_live, slot_brick // size_z, plane_size)
    earlier = (target_peer[:, None] == target_peer[None, :]) & (
        slot_ids[None, :] < slot_ids[:, None]
    )
    pair_rank = jnp.sum(earlier.astype(jnp.int32), axis=1)
    position = jnp.where(is_live, target_peer * pair_depth + pair_rank, slot_count)
    slot_hits = position[:, None] == slot_ids[None, :]
    filled = jnp.any(slot_hits, axis=0)
    source = jnp.sum(jnp.where(slot_hits, slot_ids[:, None], 0), axis=0)
    sent_snapshot = jnp.where(filled, jnp.take(slot_snapshot, source, mode="clip"), -1)
    payload = jnp.take(average_cells(patch_fields), source, axis=0, mode="clip")
    sent_ids = jnp.broadcast_to(sent_snapshot[:, None, None], (slot_count, 8, 128))
    received, received_ids = exchange(payload, sent_ids)
    received_snapshot = received_ids[:, 0, 0]
    snapshots = jnp.arange(SNAPS, dtype=jnp.int32)
    chosen = jnp.sum(
        jnp.where(received_snapshot[None, :] == snapshots[:, None], slot_ids[None, :], 0), axis=1
    )
    arrived = jnp.take(received, chosen, axis=0, mode="clip")
    columns = arrived.reshape(COLS, CELLS)
    partial_gram = jnp.dot(columns, columns.T, preferred_element_type=jnp.float32)
    data_wide = columns.astype(jnp.float32).T
    data_block = columns.T.reshape(EDGE, EDGE, EDGE * COLS)
    data_image = diffusion(data_block).reshape(CELLS, COLS)
    partial_cross = jnp.dot(data_wide.T, data_image, precision=HIGHEST)
    totals = allreduce(jnp.concatenate([partial_gram, partial_cross], axis=1))
    gram_total, cross_total = totals[:, :COLS], totals[:, COLS:]
    gram_matrix = gram_total / total_cells
    coeffs = factor_basis(gram_matrix, prior_basis)
    mode_basis = jnp.dot(data_wide, coeffs, precision=HIGHEST)
    mode_image = jnp.dot(data_image, coeffs, precision=HIGHEST)
    inner = jnp.dot(cross_total / total_cells, coeffs, precision=HIGHEST)
    reduced = jnp.dot(coeffs.T, inner, precision=HIGHEST)
    mode_fields = mode_basis.reshape(EDGE, EDGE, EDGE * MODES).astype(jnp.bfloat16)
    diffused = mode_image.reshape(EDGE, EDGE, EDGE * MODES).astype(jnp.bfloat16)
    return (gram_matrix, mode_fields, diffused, reduced)


def solution(mesh):
    split = Mesh(
        mesh.devices.reshape(mesh.shape["gx"], mesh.shape["gy"], 4, 2), ("gx", "gy", "gz_0", "gz_1")
    )
    in_specs = (P(GX_GY_GZ, None, None), P(GX_GY_GZ), P(GX_GY_GZ), P())
    out_specs = (P(), P("gx", "gy", GZ), P("gx", "gy", GZ), P())
    return jax.shard_map(
        shards, mesh=split, in_specs=in_specs, out_specs=out_specs, check_vma=False
    )
```

```python
import functools

import jax
import jax.numpy as jnp
from jax import lax
from jax.sharding import Mesh
from jax.sharding import PartitionSpec as P
from jax.experimental import pallas as pl
from jax.experimental.pallas import tpu as pltpu

SNAPS = 16
FIELDS = 4
PATCH = 32
MODES = 32
EDGE = 16
CELLS = 4096
COLS = 64
GZ = ("gz_0", "gz_1")
GX_GY_GZ = ("gx", "gy", "gz_0", "gz_1")


HIGHEST = lax.Precision.HIGHEST


def extended(value, sides, width):
    edges = {}
    for axis, dim in sides:
        devices, length = (lax.axis_size(axis), value.shape[dim])
        up = [(i, (i + 1) % devices) for i in range(devices - 1)]
        last = lax.slice_in_dim(value, length - width, length, axis=dim)
        first = lax.slice_in_dim(value, 0, width, axis=dim)
        edges[dim] = (
            lax.ppermute(last, axis, up),
            lax.ppermute(first, axis, [(b, a) for a, b in up]),
        )
    done = []
    for _, dim in sides:
        low, high = edges[dim]
        around = [(width, width) if d in done else (0, 0) for d in range(value.ndim)]
        value = jnp.concatenate([jnp.pad(low, around), value, jnp.pad(high, around)], axis=dim)
        done.append(dim)
    return value


def extended_2(value, sides, width):
    for axis, dim in sides:
        devices, length = (lax.axis_size(axis), value.shape[dim])
        up = [(i, (i + 1) % devices) for i in range(devices - 1)]
        down = [(j, i) for i, j in up]
        last = lax.slice_in_dim(value, length - width, length, axis=dim)
        first = lax.slice_in_dim(value, 0, width, axis=dim)
        before = lax.ppermute(last, axis, up)
        after = lax.ppermute(first, axis, down)
        value = jnp.concatenate([before, value, after], axis=dim)
    return value


def over_axes(value, axes):
    for axis in axes:
        value = lax.psum(value, axis)
    return value


def pairing_matrix():
    fine = jnp.arange(2 * PATCH * PATCH, dtype=jnp.int32)
    fine_y = fine % (PATCH * PATCH) // PATCH
    fine_z = fine % PATCH
    coarse = jnp.arange(EDGE * EDGE, dtype=jnp.int32)
    hit = ((fine_y // 2 * EDGE + fine_z // 2)[:, None] == coarse[None, :])
    return jnp.where(hit, 0.125, 0.0).astype(jnp.bfloat16)


PAIRS_PER_STEP = 4


def average_kernel(fine_ref, pairing_ref, out_ref):
    slots = fine_ref.shape[0]
    rows = slots * FIELDS
    span = 2 * PATCH * PATCH
    stacked = jnp.concatenate(
        [fine_ref[:, :, i * span : (i + 1) * span].reshape(rows, span) for i in range(PAIRS_PER_STEP)],
        axis=0,
    )
    means = jnp.dot(stacked, pairing_ref[...], preferred_element_type=jnp.float32)
    width = EDGE * EDGE
    for i in range(PAIRS_PER_STEP):
        out_ref[:, :, i * width : (i + 1) * width] = (
            means[i * rows : (i + 1) * rows].reshape(slots, FIELDS, width).astype(out_ref.dtype)
        )


def average_cells(fine_data):
    row_count = fine_data.shape[0]
    span = 2 * PATCH * PATCH * PAIRS_PER_STEP
    width = EDGE * EDGE * PAIRS_PER_STEP
    steps = EDGE // PAIRS_PER_STEP
    return pl.pallas_call(
        average_kernel,
        grid=(steps,),
        in_specs=[
            pl.BlockSpec((row_count, FIELDS, span), lambda g: (0, 0, g)),
            pl.BlockSpec((2 * PATCH * PATCH, EDGE * EDGE), lambda g: (0, 0)),
        ],
        out_specs=pl.BlockSpec((row_count, FIELDS, width), lambda g: (0, 0, g)),
        out_shape=jax.ShapeDtypeStruct((row_count, FIELDS, CELLS), jnp.bfloat16),
    )(fine_data, pairing_matrix())


def seven_point(center, around_xy, around_z, stride):
    total = around_xy[2:, 1:-1] + around_xy[:-2, 1:-1] + around_xy[1:-1, 2:] + around_xy[1:-1, :-2]
    total = total + around_z[:, :, 2 * stride :] + around_z[:, :, : -2 * stride]
    return total - 6.0 * center


def factor_kernel(gram_ref, prior_ref, out_ref):
    size = gram_ref.shape[0]
    rows = lax.broadcasted_iota(jnp.int32, (size, size), 0)
    cols = lax.broadcasted_iota(jnp.int32, (size, size), 1)
    work = gram_ref[...]
    upper = jnp.zeros_like(work)
    for j in range(size):
        pivot = jnp.sqrt(work[j : j + 1, j : j + 1])
        column = jnp.where(rows[:, j : j + 1] >= j, work[:, j : j + 1] / pivot, 0.0)
        row = jnp.sum(jnp.where(rows == cols, column, 0.0), axis=0, keepdims=True)
        upper = jnp.where(rows == j, row, upper)
        work = work - column * row
    solved = prior_ref[...]
    result = jnp.zeros_like(solved)
    picks = lax.broadcasted_iota(jnp.int32, solved.shape, 0)
    for i in reversed(range(size)):
        value = solved[i : i + 1, :] / upper[i : i + 1, i : i + 1]
        result = jnp.where(picks == i, value, result)
        solved = solved - upper[:, i : i + 1] * value
    out_ref[...] = result


def factor_basis(gram_matrix, prior_basis):
    vmem = pl.BlockSpec(memory_space=pltpu.VMEM)
    return pl.pallas_call(
        factor_kernel,
        out_shape=jax.ShapeDtypeStruct(prior_basis.shape, prior_basis.dtype),
        in_specs=[vmem, vmem],
        out_specs=vmem,
    )(gram_matrix, prior_basis)


def tree_sum(values):
    while len(values) > 1:
        values = [values[i] + values[i + 1] for i in range(0, len(values), 2)]
    return values[0]


REDUCE_GROUPS = (("gx", "gz_1"), ("gy",), ("gz_0",))


def allreduce_kernel(groups, part_ref, out_ref, acc, *rest):
    bufs, (send_sems, recv_sems) = rest[: len(groups)], rest[len(groups) :]
    me = {axis: lax.axis_index(axis) for group in groups for axis, _ in group}

    def linear(group):
        index = 0
        for axis, size in group:
            index = index * size + me[axis]
        return index

    def peer(group, step):
        count = 1
        for _, size in group:
            count *= size
        target = lax.rem(linear(group) + step, count)
        device = dict(me)
        for axis, size in reversed(group):
            device[axis] = lax.rem(target, size)
            target = target // size
        return tuple(device[axis] for axis in GX_GY_GZ)

    counts = []
    for group in groups:
        count = 1
        for _, size in group:
            count *= size
        counts.append(count)
    barrier = pltpu.get_barrier_semaphore()
    for group, count in zip(groups, counts):
        for step in range(1, count):
            pl.semaphore_signal(
                barrier, inc=1, device_id=peer(group, step), device_id_type=pl.DeviceIdType.MESH
            )
    pl.semaphore_wait(barrier, sum(counts) - len(counts))
    acc[...] = part_ref[...]
    slot = 0
    for group, count, buf in zip(groups, counts, bufs):
        copies = []
        for step in range(1, count):
            copy = pltpu.make_async_remote_copy(
                src_ref=acc,
                dst_ref=buf.at[step - 1],
                send_sem=send_sems.at[slot],
                recv_sem=recv_sems.at[slot],
                device_id=peer(group, step),
                device_id_type=pl.DeviceIdType.MESH,
            )
            copy.start()
            copies.append(copy)
            slot += 1
        for copy in copies:
            copy.wait()
        own = acc[...]
        mine = linear(group)
        values = []
        for source in range(count):
            held = jnp.maximum(lax.rem(mine - source + count, count) - 1, 0)
            values.append(jnp.where(mine == source, own, buf[held]))
        acc[...] = tree_sum(values)
    out_ref[...] = acc[...]


def allreduce(part):
    groups = tuple(
        tuple((axis, lax.axis_size(axis)) for axis in group) for group in REDUCE_GROUPS
    )
    counts = [functools.reduce(lambda a, b: a * b, [size for _, size in group]) for group in groups]
    copies = sum(count - 1 for count in counts)
    return pl.pallas_call(
        functools.partial(allreduce_kernel, groups),
        out_shape=jax.ShapeDtypeStruct(part.shape, part.dtype),
        in_specs=[pl.BlockSpec(memory_space=pltpu.VMEM)],
        out_specs=pl.BlockSpec(memory_space=pltpu.VMEM),
        scratch_shapes=[pltpu.VMEM(part.shape, part.dtype)]
        + [pltpu.VMEM((max(count - 1, 1),) + part.shape, part.dtype) for count in counts]
        + [pltpu.SemaphoreType.DMA((copies,)), pltpu.SemaphoreType.DMA((copies,))],
        compiler_params=pltpu.CompilerParams(collective_id=0, has_side_effects=True),
    )(part)


def exchange_kernel(plane, size_y, payload_ref, ids_ref, out_ref, out_ids_ref, send_sems, recv_sems, local_sems):
    me = lax.axis_index("gx") * size_y + lax.axis_index("gy")
    rest = tuple(lax.axis_index(axis) for axis in GZ)

    def device(step):
        target = lax.rem(me + step, plane)
        return (target // size_y, lax.rem(target, size_y)) + rest

    barrier = pltpu.get_barrier_semaphore()
    for step in range(1, plane):
        pl.semaphore_signal(barrier, inc=1, device_id=device(step), device_id_type=pl.DeviceIdType.MESH)
    pl.semaphore_wait(barrier, plane - 1)
    pairs = ((payload_ref, out_ref), (ids_ref, out_ids_ref))
    copies = []
    for index, (src, dst) in enumerate(pairs):
        copy = pltpu.make_async_copy(src.at[me], dst.at[me], local_sems.at[index])
        copy.start()
        copies.append(copy)
    for step in range(1, plane):
        target = lax.rem(me + step, plane)
        for index, (src, dst) in enumerate(pairs):
            slot = 2 * (step - 1) + index
            copy = pltpu.make_async_remote_copy(
                src_ref=src.at[target],
                dst_ref=dst.at[me],
                send_sem=send_sems.at[slot],
                recv_sem=recv_sems.at[slot],
                device_id=device(step),
                device_id_type=pl.DeviceIdType.MESH,
            )
            copy.start()
            copies.append(copy)
    for copy in copies:
        copy.wait()


def exchange(payload, ids):
    size_y = lax.axis_size("gy")
    plane = lax.axis_size("gx") * size_y
    vmem = pl.BlockSpec(memory_space=pltpu.VMEM)
    return pl.pallas_call(
        functools.partial(exchange_kernel, plane, size_y),
        out_shape=(
            jax.ShapeDtypeStruct(payload.shape, payload.dtype),
            jax.ShapeDtypeStruct(ids.shape, ids.dtype),
        ),
        in_specs=[vmem, vmem],
        out_specs=(vmem, vmem),
        scratch_shapes=[
            pltpu.SemaphoreType.DMA((2 * (plane - 1),)),
            pltpu.SemaphoreType.DMA((2 * (plane - 1),)),
            pltpu.SemaphoreType.DMA((2,)),
        ],
        compiler_params=pltpu.CompilerParams(collective_id=1, has_side_effects=True),
    )(payload, ids)


def halo_kernel(sizes, faces_ref, out_ref, send_sems, recv_sems):
    me = [lax.axis_index(axis) for axis in GX_GY_GZ]
    size_z1 = sizes[3]
    size_z = sizes[2] * size_z1

    def device(dim, step):
        if dim < 2:
            place = list(me)
            place[dim] = lax.rem(me[dim] + step + sizes[dim], sizes[dim])
            return tuple(place)
        z = lax.rem(me[2] * size_z1 + me[3] + step + size_z, size_z)
        return (me[0], me[1], z // size_z1, lax.rem(z, size_z1))

    targets = [device(dim, step) for dim in range(3) for step in (-1, 1)]
    barrier = pltpu.get_barrier_semaphore()
    for target in targets:
        pl.semaphore_signal(barrier, inc=1, device_id=target, device_id_type=pl.DeviceIdType.MESH)
    pl.semaphore_wait(barrier, len(targets))
    copies = []
    for index, target in enumerate(targets):
        copy = pltpu.make_async_remote_copy(
            src_ref=faces_ref.at[index],
            dst_ref=out_ref.at[index],
            send_sem=send_sems.at[index],
            recv_sem=recv_sems.at[index],
            device_id=target,
            device_id_type=pl.DeviceIdType.MESH,
        )
        copy.start()
        copies.append(copy)
    for copy in copies:
        copy.wait()


def halo(faces):
    sizes = tuple(lax.axis_size(axis) for axis in GX_GY_GZ)
    vmem = pl.BlockSpec(memory_space=pltpu.VMEM)
    return pl.pallas_call(
        functools.partial(halo_kernel, sizes),
        out_shape=jax.ShapeDtypeStruct(faces.shape, faces.dtype),
        in_specs=[vmem],
        out_specs=vmem,
        scratch_shapes=[
            pltpu.SemaphoreType.DMA((faces.shape[0],)),
            pltpu.SemaphoreType.DMA((faces.shape[0],)),
        ],
        compiler_params=pltpu.CompilerParams(collective_id=2, has_side_effects=True),
    )(faces)


def diffusion(data_block):
    edge = data_block.shape[0]
    cells = edge * COLS
    faces = jnp.stack(
        [
            data_block[0],
            data_block[-1],
            data_block[:, 0],
            data_block[:, -1],
            data_block[:, :, :COLS].reshape(edge, cells),
            data_block[:, :, -COLS:].reshape(edge, cells),
        ]
    )
    got = halo(faces).astype(jnp.float32)
    gx, gy, gz = lax.axis_index("gx"), lax.axis_index("gy"), lax.axis_index(GZ)
    last = (lax.axis_size("gx") - 1, lax.axis_size("gy") - 1, lax.axis_size(GZ) - 1)
    above_x = jnp.where(gx < last[0], got[0], 0.0)
    below_x = jnp.where(gx > 0, got[1], 0.0)
    above_y = jnp.where(gy < last[1], got[2], 0.0)
    below_y = jnp.where(gy > 0, got[3], 0.0)
    above_z = jnp.where(gz < last[2], got[4], 0.0).reshape(edge, edge, COLS)
    below_z = jnp.where(gz > 0, got[5], 0.0).reshape(edge, edge, COLS)
    center = data_block.astype(jnp.float32)
    along_x = jnp.concatenate([below_x[None], center, above_x[None]], axis=0)
    along_y = jnp.concatenate([below_y[:, None], center, above_y[:, None]], axis=1)
    along_z = jnp.concatenate([below_z, center, above_z], axis=2)
    total = along_x[2:] + along_x[:-2] + along_y[:, 2:] + along_y[:, :-2]
    total = total + along_z[:, :, 2 * COLS :] + along_z[:, :, : -2 * COLS]
    return total - 6.0 * center


def shards(patch_fields, slot_snapshot, slot_brick, prior_basis):
    size_x = lax.axis_size("gx")
    size_y = lax.axis_size("gy")
    size_z = lax.axis_size(GZ)
    plane_size = size_x * size_y
    slot_count = slot_snapshot.shape[0]
    pair_depth = slot_count // plane_size
    total_cells = CELLS * plane_size * size_z
    is_live = slot_snapshot >= 0
    slot_ids = jnp.arange(slot_count, dtype=jnp.int32)
    target_peer = jnp.where(is_live, slot_brick // size_z, plane_size)
    earlier = (target_peer[:, None] == target_peer[None, :]) & (
        slot_ids[None, :] < slot_ids[:, None]
    )
    pair_rank = jnp.sum(earlier.astype(jnp.int32), axis=1)
    position = jnp.where(is_live, target_peer * pair_depth + pair_rank, slot_count)
    slot_hits = position[:, None] == slot_ids[None, :]
    filled = jnp.any(slot_hits, axis=0)
    source = jnp.sum(jnp.where(slot_hits, slot_ids[:, None], 0), axis=0)
    sent_snapshot = jnp.where(filled, jnp.take(slot_snapshot, source, mode="clip"), -1)
    payload = jnp.take(average_cells(patch_fields), source, axis=0, mode="clip")
    sent_ids = jnp.broadcast_to(sent_snapshot[:, None, None], (slot_count, 8, 128))
    received, received_ids = exchange(payload, sent_ids)
    received_snapshot = received_ids[:, 0, 0]
    snapshots = jnp.arange(SNAPS, dtype=jnp.int32)
    chosen = jnp.sum(
        jnp.where(received_snapshot[None, :] == snapshots[:, None], slot_ids[None, :], 0), axis=1
    )
    arrived = jnp.take(received, chosen, axis=0, mode="clip")
    columns = arrived.reshape(COLS, CELLS)
    partial_gram = jnp.dot(columns, columns.T, preferred_element_type=jnp.float32)
    data_wide = columns.astype(jnp.float32).T
    data_block = columns.T.reshape(EDGE, EDGE, EDGE * COLS)
    data_block_image = diffusion(data_block)
    data_image = data_block_image.reshape(CELLS, COLS)
    partial_cross = jnp.dot(data_wide.T, data_image, precision=HIGHEST)
    totals = allreduce(jnp.concatenate([partial_gram, partial_cross], axis=1))
    gram_total, cross_total = totals[:, :COLS], totals[:, COLS:]
    gram_matrix = gram_total / total_cells
    coeffs = factor_basis(gram_matrix, prior_basis)
    inner = jnp.dot(cross_total / total_cells, coeffs, precision=HIGHEST)
    reduced = jnp.dot(coeffs.T, inner, precision=HIGHEST)
    depth = data_block.shape[2] // COLS
    per_cell = jnp.eye(depth, dtype=jnp.float32)[:, None, :, None] * coeffs[None, :, None, :]
    per_cell = per_cell.reshape(depth * COLS, depth * MODES)
    plane = data_block.shape[0] * data_block.shape[1]
    mode_fields = jnp.dot(
        data_block.reshape(plane, depth * COLS).astype(jnp.float32), per_cell, precision=HIGHEST
    )
    diffused = jnp.dot(data_block_image.reshape(plane, depth * COLS), per_cell, precision=HIGHEST)
    mode_fields = mode_fields.reshape(EDGE, EDGE, EDGE * MODES).astype(jnp.bfloat16)
    diffused = diffused.reshape(EDGE, EDGE, EDGE * MODES).astype(jnp.bfloat16)
    return (gram_matrix, mode_fields, diffused, reduced)


def solution(mesh):
    split = Mesh(
        mesh.devices.reshape(mesh.shape["gx"], mesh.shape["gy"], 4, 2), ("gx", "gy", "gz_0", "gz_1")
    )
    in_specs = (P(GX_GY_GZ, None, None), P(GX_GY_GZ), P(GX_GY_GZ), P())
    out_specs = (P(), P("gx", "gy", GZ), P("gx", "gy", GZ), P())
    return jax.shard_map(
        shards, mesh=split, in_specs=in_specs, out_specs=out_specs, check_vma=False
    )
```

```python
import functools

import jax
import jax.numpy as jnp
from jax import lax
from jax.sharding import Mesh
from jax.sharding import PartitionSpec as P
from jax.experimental import pallas as pl
from jax.experimental.pallas import tpu as pltpu

SNAPS = 16
FIELDS = 4
PATCH = 32
MODES = 32
EDGE = 16
CELLS = 4096
COLS = 64
GZ = ("gz_0", "gz_1")
GX_GY_GZ = ("gx", "gy", "gz_0", "gz_1")


HIGHEST = lax.Precision.HIGHEST


def extended(value, sides, width):
    edges = {}
    for axis, dim in sides:
        devices, length = (lax.axis_size(axis), value.shape[dim])
        up = [(i, (i + 1) % devices) for i in range(devices - 1)]
        last = lax.slice_in_dim(value, length - width, length, axis=dim)
        first = lax.slice_in_dim(value, 0, width, axis=dim)
        edges[dim] = (
            lax.ppermute(last, axis, up),
            lax.ppermute(first, axis, [(b, a) for a, b in up]),
        )
    done = []
    for _, dim in sides:
        low, high = edges[dim]
        around = [(width, width) if d in done else (0, 0) for d in range(value.ndim)]
        value = jnp.concatenate([jnp.pad(low, around), value, jnp.pad(high, around)], axis=dim)
        done.append(dim)
    return value


def extended_2(value, sides, width):
    for axis, dim in sides:
        devices, length = (lax.axis_size(axis), value.shape[dim])
        up = [(i, (i + 1) % devices) for i in range(devices - 1)]
        down = [(j, i) for i, j in up]
        last = lax.slice_in_dim(value, length - width, length, axis=dim)
        first = lax.slice_in_dim(value, 0, width, axis=dim)
        before = lax.ppermute(last, axis, up)
        after = lax.ppermute(first, axis, down)
        value = jnp.concatenate([before, value, after], axis=dim)
    return value


def over_axes(value, axes):
    for axis in axes:
        value = lax.psum(value, axis)
    return value


def pairing_matrix():
    fine = jnp.arange(2 * PATCH * PATCH, dtype=jnp.int32)
    fine_y = fine % (PATCH * PATCH) // PATCH
    fine_z = fine % PATCH
    coarse = jnp.arange(EDGE * EDGE, dtype=jnp.int32)
    hit = ((fine_y // 2 * EDGE + fine_z // 2)[:, None] == coarse[None, :])
    return jnp.where(hit, 0.125, 0.0).astype(jnp.bfloat16)


PAIRS_PER_STEP = 4


def average_kernel(fine_ref, pairing_ref, out_ref):
    slots = fine_ref.shape[0]
    rows = slots * FIELDS
    span = 2 * PATCH * PATCH
    stacked = jnp.concatenate(
        [fine_ref[:, :, i * span : (i + 1) * span].reshape(rows, span) for i in range(PAIRS_PER_STEP)],
        axis=0,
    )
    means = jnp.dot(stacked, pairing_ref[...], preferred_element_type=jnp.float32)
    width = EDGE * EDGE
    for i in range(PAIRS_PER_STEP):
        out_ref[:, :, i * width : (i + 1) * width] = (
            means[i * rows : (i + 1) * rows].reshape(slots, FIELDS, width).astype(out_ref.dtype)
        )


def average_cells(fine_data):
    row_count = fine_data.shape[0]
    span = 2 * PATCH * PATCH * PAIRS_PER_STEP
    width = EDGE * EDGE * PAIRS_PER_STEP
    steps = EDGE // PAIRS_PER_STEP
    return pl.pallas_call(
        average_kernel,
        grid=(steps,),
        in_specs=[
            pl.BlockSpec((row_count, FIELDS, span), lambda g: (0, 0, g)),
            pl.BlockSpec((2 * PATCH * PATCH, EDGE * EDGE), lambda g: (0, 0)),
        ],
        out_specs=pl.BlockSpec((row_count, FIELDS, width), lambda g: (0, 0, g)),
        out_shape=jax.ShapeDtypeStruct((row_count, FIELDS, CELLS), jnp.bfloat16),
    )(fine_data, pairing_matrix())


def seven_point(center, around_xy, around_z, stride):
    total = around_xy[2:, 1:-1] + around_xy[:-2, 1:-1] + around_xy[1:-1, 2:] + around_xy[1:-1, :-2]
    total = total + around_z[:, :, 2 * stride :] + around_z[:, :, : -2 * stride]
    return total - 6.0 * center


def factor_kernel(gram_ref, prior_ref, out_ref):
    size = gram_ref.shape[0]
    rows = lax.broadcasted_iota(jnp.int32, (size, size), 0)
    cols = lax.broadcasted_iota(jnp.int32, (size, size), 1)
    work = gram_ref[...]
    upper = jnp.zeros_like(work)
    for j in range(size):
        pivot = jnp.sqrt(work[j : j + 1, j : j + 1])
        column = jnp.where(rows[:, j : j + 1] >= j, work[:, j : j + 1] / pivot, 0.0)
        row = jnp.where(cols[j : j + 1, :] >= j, work[j : j + 1, :] / pivot, 0.0)
        upper = jnp.where(rows == j, row, upper)
        work = work - column * row
    solved = prior_ref[...]
    result = jnp.zeros_like(solved)
    picks = lax.broadcasted_iota(jnp.int32, solved.shape, 0)
    for i in reversed(range(size)):
        value = solved[i : i + 1, :] / upper[i : i + 1, i : i + 1]
        result = jnp.where(picks == i, value, result)
        solved = solved - upper[:, i : i + 1] * value
    out_ref[...] = result


def factor_basis(gram_matrix, prior_basis):
    vmem = pl.BlockSpec(memory_space=pltpu.VMEM)
    return pl.pallas_call(
        factor_kernel,
        out_shape=jax.ShapeDtypeStruct(prior_basis.shape, prior_basis.dtype),
        in_specs=[vmem, vmem],
        out_specs=vmem,
    )((gram_matrix + gram_matrix.T) * 0.5, prior_basis)


def tree_sum(values):
    while len(values) > 1:
        values = [values[i] + values[i + 1] for i in range(0, len(values), 2)]
    return values[0]


REDUCE_GROUPS = (("gx", "gz_1"), ("gy",), ("gz_0",))


def allreduce_kernel(groups, part_ref, out_ref, acc, *rest):
    bufs, (send_sems, recv_sems) = rest[: len(groups)], rest[len(groups) :]
    me = {axis: lax.axis_index(axis) for group in groups for axis, _ in group}

    def linear(group):
        index = 0
        for axis, size in group:
            index = index * size + me[axis]
        return index

    def peer(group, step):
        count = 1
        for _, size in group:
            count *= size
        target = lax.rem(linear(group) + step, count)
        device = dict(me)
        for axis, size in reversed(group):
            device[axis] = lax.rem(target, size)
            target = target // size
        return tuple(device[axis] for axis in GX_GY_GZ)

    counts = []
    for group in groups:
        count = 1
        for _, size in group:
            count *= size
        counts.append(count)
    barrier = pltpu.get_barrier_semaphore()
    for group, count in zip(groups, counts):
        for step in range(1, count):
            pl.semaphore_signal(
                barrier, inc=1, device_id=peer(group, step), device_id_type=pl.DeviceIdType.MESH
            )
    pl.semaphore_wait(barrier, sum(counts) - len(counts))
    acc[...] = part_ref[...]
    slot = 0
    for group, count, buf in zip(groups, counts, bufs):
        copies = []
        for step in range(1, count):
            copy = pltpu.make_async_remote_copy(
                src_ref=acc,
                dst_ref=buf.at[step - 1],
                send_sem=send_sems.at[slot],
                recv_sem=recv_sems.at[slot],
                device_id=peer(group, step),
                device_id_type=pl.DeviceIdType.MESH,
            )
            copy.start()
            copies.append(copy)
            slot += 1
        for copy in copies:
            copy.wait()
        own = acc[...]
        mine = linear(group)
        values = []
        for source in range(count):
            held = jnp.maximum(lax.rem(mine - source + count, count) - 1, 0)
            values.append(jnp.where(mine == source, own, buf[held]))
        acc[...] = tree_sum(values)
    out_ref[...] = acc[...]


def allreduce(part):
    groups = tuple(
        tuple((axis, lax.axis_size(axis)) for axis in group) for group in REDUCE_GROUPS
    )
    counts = [functools.reduce(lambda a, b: a * b, [size for _, size in group]) for group in groups]
    copies = sum(count - 1 for count in counts)
    return pl.pallas_call(
        functools.partial(allreduce_kernel, groups),
        out_shape=jax.ShapeDtypeStruct(part.shape, part.dtype),
        in_specs=[pl.BlockSpec(memory_space=pltpu.VMEM)],
        out_specs=pl.BlockSpec(memory_space=pltpu.VMEM),
        scratch_shapes=[pltpu.VMEM(part.shape, part.dtype)]
        + [pltpu.VMEM((max(count - 1, 1),) + part.shape, part.dtype) for count in counts]
        + [pltpu.SemaphoreType.DMA((copies,)), pltpu.SemaphoreType.DMA((copies,))],
        compiler_params=pltpu.CompilerParams(collective_id=0, has_side_effects=True),
    )(part)


def exchange_kernel(plane, size_y, payload_ref, ids_ref, out_ref, out_ids_ref, send_sems, recv_sems, local_sems):
    me = lax.axis_index("gx") * size_y + lax.axis_index("gy")
    rest = tuple(lax.axis_index(axis) for axis in GZ)

    def device(step):
        target = lax.rem(me + step, plane)
        return (target // size_y, lax.rem(target, size_y)) + rest

    barrier = pltpu.get_barrier_semaphore()
    for step in range(1, plane):
        pl.semaphore_signal(barrier, inc=1, device_id=device(step), device_id_type=pl.DeviceIdType.MESH)
    pl.semaphore_wait(barrier, plane - 1)
    pairs = ((payload_ref, out_ref), (ids_ref, out_ids_ref))
    copies = []
    for index, (src, dst) in enumerate(pairs):
        copy = pltpu.make_async_copy(src.at[me], dst.at[me], local_sems.at[index])
        copy.start()
        copies.append(copy)
    for step in range(1, plane):
        target = lax.rem(me + step, plane)
        for index, (src, dst) in enumerate(pairs):
            slot = 2 * (step - 1) + index
            copy = pltpu.make_async_remote_copy(
                src_ref=src.at[target],
                dst_ref=dst.at[me],
                send_sem=send_sems.at[slot],
                recv_sem=recv_sems.at[slot],
                device_id=device(step),
                device_id_type=pl.DeviceIdType.MESH,
            )
            copy.start()
            copies.append(copy)
    for copy in copies:
        copy.wait()


def exchange(payload, ids):
    size_y = lax.axis_size("gy")
    plane = lax.axis_size("gx") * size_y
    vmem = pl.BlockSpec(memory_space=pltpu.VMEM)
    return pl.pallas_call(
        functools.partial(exchange_kernel, plane, size_y),
        out_shape=(
            jax.ShapeDtypeStruct(payload.shape, payload.dtype),
            jax.ShapeDtypeStruct(ids.shape, ids.dtype),
        ),
        in_specs=[vmem, vmem],
        out_specs=(vmem, vmem),
        scratch_shapes=[
            pltpu.SemaphoreType.DMA((2 * (plane - 1),)),
            pltpu.SemaphoreType.DMA((2 * (plane - 1),)),
            pltpu.SemaphoreType.DMA((2,)),
        ],
        compiler_params=pltpu.CompilerParams(collective_id=1, has_side_effects=True),
    )(payload, ids)


def halo_kernel(sizes, faces_ref, out_ref, send_sems, recv_sems):
    me = [lax.axis_index(axis) for axis in GX_GY_GZ]
    size_z1 = sizes[3]
    size_z = sizes[2] * size_z1

    def device(dim, step):
        if dim < 2:
            place = list(me)
            place[dim] = lax.rem(me[dim] + step + sizes[dim], sizes[dim])
            return tuple(place)
        z = lax.rem(me[2] * size_z1 + me[3] + step + size_z, size_z)
        return (me[0], me[1], z // size_z1, lax.rem(z, size_z1))

    targets = [device(dim, step) for dim in range(3) for step in (-1, 1)]
    barrier = pltpu.get_barrier_semaphore()
    for target in targets:
        pl.semaphore_signal(barrier, inc=1, device_id=target, device_id_type=pl.DeviceIdType.MESH)
    pl.semaphore_wait(barrier, len(targets))
    copies = []
    for index, target in enumerate(targets):
        copy = pltpu.make_async_remote_copy(
            src_ref=faces_ref.at[index],
            dst_ref=out_ref.at[index],
            send_sem=send_sems.at[index],
            recv_sem=recv_sems.at[index],
            device_id=target,
            device_id_type=pl.DeviceIdType.MESH,
        )
        copy.start()
        copies.append(copy)
    for copy in copies:
        copy.wait()


def halo(faces):
    sizes = tuple(lax.axis_size(axis) for axis in GX_GY_GZ)
    vmem = pl.BlockSpec(memory_space=pltpu.VMEM)
    return pl.pallas_call(
        functools.partial(halo_kernel, sizes),
        out_shape=jax.ShapeDtypeStruct(faces.shape, faces.dtype),
        in_specs=[vmem],
        out_specs=vmem,
        scratch_shapes=[
            pltpu.SemaphoreType.DMA((faces.shape[0],)),
            pltpu.SemaphoreType.DMA((faces.shape[0],)),
        ],
        compiler_params=pltpu.CompilerParams(collective_id=2, has_side_effects=True),
    )(faces)


def diffusion(data_block):
    edge = data_block.shape[0]
    cells = edge * COLS
    faces = jnp.stack(
        [
            data_block[0],
            data_block[-1],
            data_block[:, 0],
            data_block[:, -1],
            data_block[:, :, :COLS].reshape(edge, cells),
            data_block[:, :, -COLS:].reshape(edge, cells),
        ]
    )
    got = halo(faces).astype(jnp.float32)
    gx, gy, gz = lax.axis_index("gx"), lax.axis_index("gy"), lax.axis_index(GZ)
    last = (lax.axis_size("gx") - 1, lax.axis_size("gy") - 1, lax.axis_size(GZ) - 1)
    above_x = jnp.where(gx < last[0], got[0], 0.0)
    below_x = jnp.where(gx > 0, got[1], 0.0)
    above_y = jnp.where(gy < last[1], got[2], 0.0)
    below_y = jnp.where(gy > 0, got[3], 0.0)
    above_z = jnp.where(gz < last[2], got[4], 0.0).reshape(edge, edge, COLS)
    below_z = jnp.where(gz > 0, got[5], 0.0).reshape(edge, edge, COLS)
    center = data_block.astype(jnp.float32)
    along_x = jnp.concatenate([below_x[None], center, above_x[None]], axis=0)
    along_y = jnp.concatenate([below_y[:, None], center, above_y[:, None]], axis=1)
    along_z = jnp.concatenate([below_z, center, above_z], axis=2)
    total = along_x[2:] + along_x[:-2] + along_y[:, 2:] + along_y[:, :-2]
    total = total + along_z[:, :, 2 * COLS :] + along_z[:, :, : -2 * COLS]
    return total - 6.0 * center


def shards(patch_fields, slot_snapshot, slot_brick, prior_basis):
    size_x = lax.axis_size("gx")
    size_y = lax.axis_size("gy")
    size_z = lax.axis_size(GZ)
    plane_size = size_x * size_y
    slot_count = slot_snapshot.shape[0]
    pair_depth = slot_count // plane_size
    total_cells = CELLS * plane_size * size_z
    is_live = slot_snapshot >= 0
    slot_ids = jnp.arange(slot_count, dtype=jnp.int32)
    target_peer = jnp.where(is_live, slot_brick // size_z, plane_size)
    earlier = (target_peer[:, None] == target_peer[None, :]) & (
        slot_ids[None, :] < slot_ids[:, None]
    )
    pair_rank = jnp.sum(earlier.astype(jnp.int32), axis=1)
    position = jnp.where(is_live, target_peer * pair_depth + pair_rank, slot_count)
    slot_hits = position[:, None] == slot_ids[None, :]
    filled = jnp.any(slot_hits, axis=0)
    source = jnp.sum(jnp.where(slot_hits, slot_ids[:, None], 0), axis=0)
    sent_snapshot = jnp.where(filled, jnp.take(slot_snapshot, source, mode="clip"), -1)
    payload = jnp.take(average_cells(patch_fields), source, axis=0, mode="clip")
    sent_ids = jnp.broadcast_to(sent_snapshot[:, None, None], (slot_count, 8, 128))
    received, received_ids = exchange(payload, sent_ids)
    received_snapshot = received_ids[:, 0, 0]
    snapshots = jnp.arange(SNAPS, dtype=jnp.int32)
    chosen = jnp.sum(
        jnp.where(received_snapshot[None, :] == snapshots[:, None], slot_ids[None, :], 0), axis=1
    )
    arrived = jnp.take(received, chosen, axis=0, mode="clip")
    columns = arrived.reshape(COLS, CELLS)
    partial_gram = jnp.dot(columns, columns.T, preferred_element_type=jnp.float32)
    data_wide = columns.astype(jnp.float32).T
    data_block = columns.T.reshape(EDGE, EDGE, EDGE * COLS)
    data_image = diffusion(data_block).reshape(CELLS, COLS)
    partial_cross = jnp.dot(data_wide.T, data_image, precision=HIGHEST)
    totals = allreduce(jnp.concatenate([partial_gram, partial_cross], axis=1))
    gram_total, cross_total = totals[:, :COLS], totals[:, COLS:]
    gram_matrix = gram_total / total_cells
    coeffs = factor_basis(gram_matrix, prior_basis)
    mode_basis = jnp.dot(data_wide, coeffs, precision=HIGHEST)
    mode_image = jnp.dot(data_image, coeffs, precision=HIGHEST)
    inner = jnp.dot(cross_total / total_cells, coeffs, precision=HIGHEST)
    reduced = jnp.dot(coeffs.T, inner, precision=HIGHEST)
    mode_fields = mode_basis.reshape(EDGE, EDGE, EDGE * MODES).astype(jnp.bfloat16)
    diffused = mode_image.reshape(EDGE, EDGE, EDGE * MODES).astype(jnp.bfloat16)
    return (gram_matrix, mode_fields, diffused, reduced)


def solution(mesh):
    split = Mesh(
        mesh.devices.reshape(mesh.shape["gx"], mesh.shape["gy"], 4, 2), ("gx", "gy", "gz_0", "gz_1")
    )
    in_specs = (P(GX_GY_GZ, None, None), P(GX_GY_GZ), P(GX_GY_GZ), P())
    out_specs = (P(), P("gx", "gy", GZ), P("gx", "gy", GZ), P())
    return jax.shard_map(
        shards, mesh=split, in_specs=in_specs, out_specs=out_specs, check_vma=False
    )
```

```python
import functools

import jax
import jax.numpy as jnp
from jax import lax
from jax.sharding import Mesh
from jax.sharding import PartitionSpec as P
from jax.experimental import pallas as pl
from jax.experimental.pallas import tpu as pltpu

SNAPS = 16
FIELDS = 4
PATCH = 32
MODES = 32
EDGE = 16
CELLS = 4096
COLS = 64
GZ = ("gz_0", "gz_1")
GX_GY_GZ = ("gx", "gy", "gz_0", "gz_1")


HIGHEST = lax.Precision.HIGHEST


def extended(value, sides, width):
    edges = {}
    for axis, dim in sides:
        devices, length = (lax.axis_size(axis), value.shape[dim])
        up = [(i, (i + 1) % devices) for i in range(devices - 1)]
        last = lax.slice_in_dim(value, length - width, length, axis=dim)
        first = lax.slice_in_dim(value, 0, width, axis=dim)
        edges[dim] = (
            lax.ppermute(last, axis, up),
            lax.ppermute(first, axis, [(b, a) for a, b in up]),
        )
    done = []
    for _, dim in sides:
        low, high = edges[dim]
        around = [(width, width) if d in done else (0, 0) for d in range(value.ndim)]
        value = jnp.concatenate([jnp.pad(low, around), value, jnp.pad(high, around)], axis=dim)
        done.append(dim)
    return value


def extended_2(value, sides, width):
    for axis, dim in sides:
        devices, length = (lax.axis_size(axis), value.shape[dim])
        up = [(i, (i + 1) % devices) for i in range(devices - 1)]
        down = [(j, i) for i, j in up]
        last = lax.slice_in_dim(value, length - width, length, axis=dim)
        first = lax.slice_in_dim(value, 0, width, axis=dim)
        before = lax.ppermute(last, axis, up)
        after = lax.ppermute(first, axis, down)
        value = jnp.concatenate([before, value, after], axis=dim)
    return value


def over_axes(value, axes):
    for axis in axes:
        value = lax.psum(value, axis)
    return value


def pairing_matrix():
    fine = jnp.arange(2 * PATCH * PATCH, dtype=jnp.int32)
    fine_y = fine % (PATCH * PATCH) // PATCH
    fine_z = fine % PATCH
    coarse = jnp.arange(EDGE * EDGE, dtype=jnp.int32)
    hit = ((fine_y // 2 * EDGE + fine_z // 2)[:, None] == coarse[None, :])
    return jnp.where(hit, 0.125, 0.0).astype(jnp.bfloat16)


PAIRS_PER_STEP = 4


def average_kernel(source_ref, fine_ref, pairing_ref, out_ref, means_ref):
    slots = fine_ref.shape[0]
    rows = slots * FIELDS
    span = 2 * PATCH * PATCH
    stacked = jnp.concatenate(
        [fine_ref[:, :, i * span : (i + 1) * span].reshape(rows, span) for i in range(PAIRS_PER_STEP)],
        axis=0,
    )
    means = jnp.dot(stacked, pairing_ref[...], preferred_element_type=jnp.float32)
    width = EDGE * EDGE
    for i in range(PAIRS_PER_STEP):
        means_ref[:, :, i * width : (i + 1) * width] = (
            means[i * rows : (i + 1) * rows].reshape(slots, FIELDS, width).astype(means_ref.dtype)
        )
    for slot in range(slots):
        out_ref[slot] = means_ref[source_ref[slot]]


def average_cells(fine_data, source):
    row_count = fine_data.shape[0]
    span = 2 * PATCH * PATCH * PAIRS_PER_STEP
    width = EDGE * EDGE * PAIRS_PER_STEP
    steps = EDGE // PAIRS_PER_STEP
    grid_spec = pltpu.PrefetchScalarGridSpec(
        num_scalar_prefetch=1,
        grid=(steps,),
        in_specs=[
            pl.BlockSpec((row_count, FIELDS, span), lambda g, order: (0, 0, g)),
            pl.BlockSpec((2 * PATCH * PATCH, EDGE * EDGE), lambda g, order: (0, 0)),
        ],
        out_specs=pl.BlockSpec((row_count, FIELDS, width), lambda g, order: (0, 0, g)),
        scratch_shapes=[pltpu.VMEM((row_count, FIELDS, width), jnp.bfloat16)],
    )
    return pl.pallas_call(
        average_kernel,
        grid_spec=grid_spec,
        out_shape=jax.ShapeDtypeStruct((row_count, FIELDS, CELLS), jnp.bfloat16),
    )(source, fine_data, pairing_matrix())


def modes_kernel(data_ref, image_ref, coeffs_ref, fields_ref, diffused_ref):
    coeffs = coeffs_ref[...]
    high = coeffs.astype(jnp.bfloat16)
    low = (coeffs - high.astype(jnp.float32)).astype(jnp.bfloat16)
    cols, modes = coeffs.shape
    for z in range(data_ref.shape[1] // cols):
        data = data_ref[:, z * cols : (z + 1) * cols]
        fields = jnp.dot(data, high, preferred_element_type=jnp.float32)
        fields = fields + jnp.dot(data, low, preferred_element_type=jnp.float32)
        fields_ref[:, z * modes : (z + 1) * modes] = fields.astype(fields_ref.dtype)
        image = image_ref[:, z * cols : (z + 1) * cols]
        image_high = image.astype(jnp.bfloat16)
        image_low = (image - image_high.astype(jnp.float32)).astype(jnp.bfloat16)
        diffused = jnp.dot(image_high, high, preferred_element_type=jnp.float32)
        diffused = diffused + jnp.dot(image_high, low, preferred_element_type=jnp.float32)
        diffused = diffused + jnp.dot(image_low, high, preferred_element_type=jnp.float32)
        diffused_ref[:, z * modes : (z + 1) * modes] = diffused.astype(diffused_ref.dtype)


def project_modes(data, image, coeffs):
    rows, width = data.shape
    out_width = width // coeffs.shape[0] * coeffs.shape[1]
    vmem = pl.BlockSpec(memory_space=pltpu.VMEM)
    shape = jax.ShapeDtypeStruct((rows, out_width), jnp.bfloat16)
    return pl.pallas_call(
        modes_kernel,
        out_shape=(shape, shape),
        in_specs=[vmem, vmem, vmem],
        out_specs=(vmem, vmem),
    )(data, image, coeffs)


def seven_point(center, around_xy, around_z, stride):
    total = around_xy[2:, 1:-1] + around_xy[:-2, 1:-1] + around_xy[1:-1, 2:] + around_xy[1:-1, :-2]
    total = total + around_z[:, :, 2 * stride :] + around_z[:, :, : -2 * stride]
    return total - 6.0 * center


def factor_kernel(gram_ref, prior_ref, out_ref):
    size = gram_ref.shape[0]
    rows = lax.broadcasted_iota(jnp.int32, (size, size), 0)
    cols = lax.broadcasted_iota(jnp.int32, (size, size), 1)
    work = gram_ref[...]
    upper = jnp.zeros_like(work)
    for j in range(size):
        pivot = jnp.sqrt(work[j : j + 1, j : j + 1])
        column = jnp.where(rows[:, j : j + 1] >= j, work[:, j : j + 1] / pivot, 0.0)
        row = jnp.where(cols[j : j + 1, :] >= j, work[j : j + 1, :] / pivot, 0.0)
        upper = jnp.where(rows == j, row, upper)
        work = work - column * row
    solved = prior_ref[...]
    result = jnp.zeros_like(solved)
    picks = lax.broadcasted_iota(jnp.int32, solved.shape, 0)
    for i in reversed(range(size)):
        value = solved[i : i + 1, :] / upper[i : i + 1, i : i + 1]
        result = jnp.where(picks == i, value, result)
        solved = solved - upper[:, i : i + 1] * value
    out_ref[...] = result


def factor_basis(gram_matrix, prior_basis):
    vmem = pl.BlockSpec(memory_space=pltpu.VMEM)
    return pl.pallas_call(
        factor_kernel,
        out_shape=jax.ShapeDtypeStruct(prior_basis.shape, prior_basis.dtype),
        in_specs=[vmem, vmem],
        out_specs=vmem,
    )((gram_matrix + gram_matrix.T) * 0.5, prior_basis)


def tree_sum(values):
    while len(values) > 1:
        values = [values[i] + values[i + 1] for i in range(0, len(values), 2)]
    return values[0]


REDUCE_GROUPS = (("gx", "gz_1"), ("gy",), ("gz_0",))


def allreduce_kernel(groups, part_ref, out_ref, acc, *rest):
    bufs, (send_sems, recv_sems) = rest[: len(groups)], rest[len(groups) :]
    me = {axis: lax.axis_index(axis) for group in groups for axis, _ in group}

    def linear(group):
        index = 0
        for axis, size in group:
            index = index * size + me[axis]
        return index

    def peer(group, step):
        count = 1
        for _, size in group:
            count *= size
        target = lax.rem(linear(group) + step, count)
        device = dict(me)
        for axis, size in reversed(group):
            device[axis] = lax.rem(target, size)
            target = target // size
        return tuple(device[axis] for axis in GX_GY_GZ)

    counts = []
    for group in groups:
        count = 1
        for _, size in group:
            count *= size
        counts.append(count)
    barrier = pltpu.get_barrier_semaphore()
    for group, count in zip(groups, counts):
        for step in range(1, count):
            pl.semaphore_signal(
                barrier, inc=1, device_id=peer(group, step), device_id_type=pl.DeviceIdType.MESH
            )
    pl.semaphore_wait(barrier, sum(counts) - len(counts))
    acc[...] = part_ref[...]
    slot = 0
    for group, count, buf in zip(groups, counts, bufs):
        copies = []
        for step in range(1, count):
            copy = pltpu.make_async_remote_copy(
                src_ref=acc,
                dst_ref=buf.at[step - 1],
                send_sem=send_sems.at[slot],
                recv_sem=recv_sems.at[slot],
                device_id=peer(group, step),
                device_id_type=pl.DeviceIdType.MESH,
            )
            copy.start()
            copies.append(copy)
            slot += 1
        for copy in copies:
            copy.wait()
        own = acc[...]
        mine = linear(group)
        values = []
        for source in range(count):
            held = jnp.maximum(lax.rem(mine - source + count, count) - 1, 0)
            values.append(jnp.where(mine == source, own, buf[held]))
        acc[...] = tree_sum(values)
    out_ref[...] = acc[...]


def allreduce(part):
    groups = tuple(
        tuple((axis, lax.axis_size(axis)) for axis in group) for group in REDUCE_GROUPS
    )
    counts = [functools.reduce(lambda a, b: a * b, [size for _, size in group]) for group in groups]
    copies = sum(count - 1 for count in counts)
    return pl.pallas_call(
        functools.partial(allreduce_kernel, groups),
        out_shape=jax.ShapeDtypeStruct(part.shape, part.dtype),
        in_specs=[pl.BlockSpec(memory_space=pltpu.VMEM)],
        out_specs=pl.BlockSpec(memory_space=pltpu.VMEM),
        scratch_shapes=[pltpu.VMEM(part.shape, part.dtype)]
        + [pltpu.VMEM((max(count - 1, 1),) + part.shape, part.dtype) for count in counts]
        + [pltpu.SemaphoreType.DMA((copies,)), pltpu.SemaphoreType.DMA((copies,))],
        compiler_params=pltpu.CompilerParams(collective_id=0, has_side_effects=True),
    )(part)


def exchange_kernel(plane, size_y, payload_ref, ids_ref, out_ref, out_ids_ref, send_sems, recv_sems, local_sems):
    me = lax.axis_index("gx") * size_y + lax.axis_index("gy")
    rest = tuple(lax.axis_index(axis) for axis in GZ)

    def device(step):
        target = lax.rem(me + step, plane)
        return (target // size_y, lax.rem(target, size_y)) + rest

    barrier = pltpu.get_barrier_semaphore()
    for step in range(1, plane):
        pl.semaphore_signal(barrier, inc=1, device_id=device(step), device_id_type=pl.DeviceIdType.MESH)
    pl.semaphore_wait(barrier, plane - 1)
    pairs = ((payload_ref, out_ref), (ids_ref, out_ids_ref))
    copies = []
    for index, (src, dst) in enumerate(pairs):
        copy = pltpu.make_async_copy(src.at[me], dst.at[me], local_sems.at[index])
        copy.start()
        copies.append(copy)
    for step in range(1, plane):
        target = lax.rem(me + step, plane)
        for index, (src, dst) in enumerate(pairs):
            slot = 2 * (step - 1) + index
            copy = pltpu.make_async_remote_copy(
                src_ref=src.at[target],
                dst_ref=dst.at[me],
                send_sem=send_sems.at[slot],
                recv_sem=recv_sems.at[slot],
                device_id=device(step),
                device_id_type=pl.DeviceIdType.MESH,
            )
            copy.start()
            copies.append(copy)
    for copy in copies:
        copy.wait()


def exchange(payload, ids):
    size_y = lax.axis_size("gy")
    plane = lax.axis_size("gx") * size_y
    vmem = pl.BlockSpec(memory_space=pltpu.VMEM)
    return pl.pallas_call(
        functools.partial(exchange_kernel, plane, size_y),
        out_shape=(
            jax.ShapeDtypeStruct(payload.shape, payload.dtype),
            jax.ShapeDtypeStruct(ids.shape, ids.dtype),
        ),
        in_specs=[vmem, vmem],
        out_specs=(vmem, vmem),
        scratch_shapes=[
            pltpu.SemaphoreType.DMA((2 * (plane - 1),)),
            pltpu.SemaphoreType.DMA((2 * (plane - 1),)),
            pltpu.SemaphoreType.DMA((2,)),
        ],
        compiler_params=pltpu.CompilerParams(collective_id=1, has_side_effects=True),
    )(payload, ids)


def halo_kernel(sizes, faces_ref, out_ref, send_sems, recv_sems):
    me = [lax.axis_index(axis) for axis in GX_GY_GZ]
    size_z1 = sizes[3]
    size_z = sizes[2] * size_z1

    def device(dim, step):
        if dim < 2:
            place = list(me)
            place[dim] = lax.rem(me[dim] + step + sizes[dim], sizes[dim])
            return tuple(place)
        z = lax.rem(me[2] * size_z1 + me[3] + step + size_z, size_z)
        return (me[0], me[1], z // size_z1, lax.rem(z, size_z1))

    targets = [device(dim, step) for dim in range(3) for step in (-1, 1)]
    barrier = pltpu.get_barrier_semaphore()
    for target in targets:
        pl.semaphore_signal(barrier, inc=1, device_id=target, device_id_type=pl.DeviceIdType.MESH)
    pl.semaphore_wait(barrier, len(targets))
    copies = []
    for index, target in enumerate(targets):
        copy = pltpu.make_async_remote_copy(
            src_ref=faces_ref.at[index],
            dst_ref=out_ref.at[index],
            send_sem=send_sems.at[index],
            recv_sem=recv_sems.at[index],
            device_id=target,
            device_id_type=pl.DeviceIdType.MESH,
        )
        copy.start()
        copies.append(copy)
    for copy in copies:
        copy.wait()


def halo(faces):
    sizes = tuple(lax.axis_size(axis) for axis in GX_GY_GZ)
    vmem = pl.BlockSpec(memory_space=pltpu.VMEM)
    return pl.pallas_call(
        functools.partial(halo_kernel, sizes),
        out_shape=jax.ShapeDtypeStruct(faces.shape, faces.dtype),
        in_specs=[vmem],
        out_specs=vmem,
        scratch_shapes=[
            pltpu.SemaphoreType.DMA((faces.shape[0],)),
            pltpu.SemaphoreType.DMA((faces.shape[0],)),
        ],
        compiler_params=pltpu.CompilerParams(collective_id=2, has_side_effects=True),
    )(faces)


def diffusion(data_block):
    edge = data_block.shape[0]
    cells = edge * COLS
    faces = jnp.stack(
        [
            data_block[0],
            data_block[-1],
            data_block[:, 0],
            data_block[:, -1],
            data_block[:, :, :COLS].reshape(edge, cells),
            data_block[:, :, -COLS:].reshape(edge, cells),
        ]
    )
    got = halo(faces).astype(jnp.float32)
    gx, gy, gz = lax.axis_index("gx"), lax.axis_index("gy"), lax.axis_index(GZ)
    last = (lax.axis_size("gx") - 1, lax.axis_size("gy") - 1, lax.axis_size(GZ) - 1)
    above_x = jnp.where(gx < last[0], got[0], 0.0)
    below_x = jnp.where(gx > 0, got[1], 0.0)
    above_y = jnp.where(gy < last[1], got[2], 0.0)
    below_y = jnp.where(gy > 0, got[3], 0.0)
    above_z = jnp.where(gz < last[2], got[4], 0.0).reshape(edge, edge, COLS)
    below_z = jnp.where(gz > 0, got[5], 0.0).reshape(edge, edge, COLS)
    center = data_block.astype(jnp.float32)
    along_x = jnp.concatenate([below_x[None], center, above_x[None]], axis=0)
    along_y = jnp.concatenate([below_y[:, None], center, above_y[:, None]], axis=1)
    along_z = jnp.concatenate([below_z, center, above_z], axis=2)
    total = along_x[2:] + along_x[:-2] + along_y[:, 2:] + along_y[:, :-2]
    total = total + along_z[:, :, 2 * COLS :] + along_z[:, :, : -2 * COLS]
    return total - 6.0 * center


def shards(patch_fields, slot_snapshot, slot_brick, prior_basis):
    size_x = lax.axis_size("gx")
    size_y = lax.axis_size("gy")
    size_z = lax.axis_size(GZ)
    plane_size = size_x * size_y
    slot_count = slot_snapshot.shape[0]
    pair_depth = slot_count // plane_size
    total_cells = CELLS * plane_size * size_z
    is_live = slot_snapshot >= 0
    slot_ids = jnp.arange(slot_count, dtype=jnp.int32)
    target_peer = jnp.where(is_live, slot_brick // size_z, plane_size)
    earlier = (target_peer[:, None] == target_peer[None, :]) & (
        slot_ids[None, :] < slot_ids[:, None]
    )
    pair_rank = jnp.sum(earlier.astype(jnp.int32), axis=1)
    position = jnp.where(is_live, target_peer * pair_depth + pair_rank, slot_count)
    slot_hits = position[:, None] == slot_ids[None, :]
    filled = jnp.any(slot_hits, axis=0)
    source = jnp.sum(jnp.where(slot_hits, slot_ids[:, None], 0), axis=0)
    sent_snapshot = jnp.where(filled, jnp.take(slot_snapshot, source, mode="clip"), -1)
    payload = average_cells(patch_fields, source)
    sent_ids = jnp.broadcast_to(sent_snapshot[:, None, None], (slot_count, 8, 128))
    received, received_ids = exchange(payload, sent_ids)
    received_snapshot = received_ids[:, 0, 0]
    snapshots = jnp.arange(SNAPS, dtype=jnp.int32)
    chosen = jnp.sum(
        jnp.where(received_snapshot[None, :] == snapshots[:, None], slot_ids[None, :], 0), axis=1
    )
    arrived = jnp.take(received, chosen, axis=0, mode="clip")
    columns = arrived.reshape(COLS, CELLS)
    partial_gram = jnp.dot(columns, columns.T, preferred_element_type=jnp.float32)
    data_wide = columns.astype(jnp.float32).T
    data_block = columns.T.reshape(EDGE, EDGE, EDGE * COLS)
    data_block_image = diffusion(data_block)
    data_image = data_block_image.reshape(CELLS, COLS)
    partial_cross = jnp.dot(data_wide.T, data_image, precision=HIGHEST)
    totals = allreduce(jnp.concatenate([partial_gram, partial_cross], axis=1))
    gram_total, cross_total = totals[:, :COLS], totals[:, COLS:]
    gram_matrix = gram_total / total_cells
    coeffs = factor_basis(gram_matrix, prior_basis)
    inner = jnp.dot(cross_total / total_cells, coeffs, precision=HIGHEST)
    reduced = jnp.dot(coeffs.T, inner, precision=HIGHEST)
    plane = data_block.shape[0] * data_block.shape[1]
    mode_fields, diffused = project_modes(
        data_block.reshape(plane, -1), data_block_image.reshape(plane, -1), coeffs
    )
    mode_fields = mode_fields.reshape(EDGE, EDGE, EDGE * MODES)
    diffused = diffused.reshape(EDGE, EDGE, EDGE * MODES)
    return (gram_matrix, mode_fields, diffused, reduced)


def solution(mesh):
    split = Mesh(
        mesh.devices.reshape(mesh.shape["gx"], mesh.shape["gy"], 4, 2), ("gx", "gy", "gz_0", "gz_1")
    )
    in_specs = (P(GX_GY_GZ, None, None), P(GX_GY_GZ), P(GX_GY_GZ), P())
    out_specs = (P(), P("gx", "gy", GZ), P("gx", "gy", GZ), P())
    return jax.shard_map(
        shards, mesh=split, in_specs=in_specs, out_specs=out_specs, check_vma=False
    )
```

```python
import functools

import jax
import jax.numpy as jnp
from jax import lax
from jax.sharding import Mesh
from jax.sharding import PartitionSpec as P
from jax.experimental import pallas as pl
from jax.experimental.pallas import tpu as pltpu

SNAPS = 16
FIELDS = 4
PATCH = 32
MODES = 32
EDGE = 16
CELLS = 4096
COLS = 64
GZ = ("gz_0", "gz_1")
GX_GY_GZ = ("gx", "gy", "gz_0", "gz_1")


HIGHEST = lax.Precision.HIGHEST


def extended(value, sides, width):
    edges = {}
    for axis, dim in sides:
        devices, length = (lax.axis_size(axis), value.shape[dim])
        up = [(i, (i + 1) % devices) for i in range(devices - 1)]
        last = lax.slice_in_dim(value, length - width, length, axis=dim)
        first = lax.slice_in_dim(value, 0, width, axis=dim)
        edges[dim] = (
            lax.ppermute(last, axis, up),
            lax.ppermute(first, axis, [(b, a) for a, b in up]),
        )
    done = []
    for _, dim in sides:
        low, high = edges[dim]
        around = [(width, width) if d in done else (0, 0) for d in range(value.ndim)]
        value = jnp.concatenate([jnp.pad(low, around), value, jnp.pad(high, around)], axis=dim)
        done.append(dim)
    return value


def extended_2(value, sides, width):
    for axis, dim in sides:
        devices, length = (lax.axis_size(axis), value.shape[dim])
        up = [(i, (i + 1) % devices) for i in range(devices - 1)]
        down = [(j, i) for i, j in up]
        last = lax.slice_in_dim(value, length - width, length, axis=dim)
        first = lax.slice_in_dim(value, 0, width, axis=dim)
        before = lax.ppermute(last, axis, up)
        after = lax.ppermute(first, axis, down)
        value = jnp.concatenate([before, value, after], axis=dim)
    return value


def over_axes(value, axes):
    for axis in axes:
        value = lax.psum(value, axis)
    return value


def pairing_matrix():
    fine = jnp.arange(2 * PATCH * PATCH, dtype=jnp.int32)
    fine_y = fine % (PATCH * PATCH) // PATCH
    fine_z = fine % PATCH
    coarse = jnp.arange(EDGE * EDGE, dtype=jnp.int32)
    hit = ((fine_y // 2 * EDGE + fine_z // 2)[:, None] == coarse[None, :])
    return jnp.where(hit, 0.125, 0.0).astype(jnp.bfloat16)


PAIRS_PER_STEP = 4


def average_kernel(source_ref, fine_ref, pairing_ref, out_ref, means_ref):
    slots = fine_ref.shape[0]
    rows = slots * FIELDS
    span = 2 * PATCH * PATCH
    stacked = jnp.concatenate(
        [fine_ref[:, :, i * span : (i + 1) * span].reshape(rows, span) for i in range(PAIRS_PER_STEP)],
        axis=0,
    )
    means = jnp.dot(stacked, pairing_ref[...], preferred_element_type=jnp.float32)
    width = EDGE * EDGE
    for i in range(PAIRS_PER_STEP):
        means_ref[:, :, i * width : (i + 1) * width] = (
            means[i * rows : (i + 1) * rows].reshape(slots, FIELDS, width).astype(means_ref.dtype)
        )
    for slot in range(slots):
        out_ref[slot] = means_ref[source_ref[slot]]


def average_cells(fine_data, source):
    row_count = fine_data.shape[0]
    span = 2 * PATCH * PATCH * PAIRS_PER_STEP
    width = EDGE * EDGE * PAIRS_PER_STEP
    steps = EDGE // PAIRS_PER_STEP
    grid_spec = pltpu.PrefetchScalarGridSpec(
        num_scalar_prefetch=1,
        grid=(steps,),
        in_specs=[
            pl.BlockSpec((row_count, FIELDS, span), lambda g, order: (0, 0, g)),
            pl.BlockSpec((2 * PATCH * PATCH, EDGE * EDGE), lambda g, order: (0, 0)),
        ],
        out_specs=pl.BlockSpec((row_count, FIELDS, width), lambda g, order: (0, 0, g)),
        scratch_shapes=[pltpu.VMEM((row_count, FIELDS, width), jnp.bfloat16)],
    )
    return pl.pallas_call(
        average_kernel,
        grid_spec=grid_spec,
        out_shape=jax.ShapeDtypeStruct((row_count, FIELDS, CELLS), jnp.bfloat16),
    )(source, fine_data, pairing_matrix())


def modes_kernel(data_ref, image_ref, coeffs_ref, fields_ref, diffused_ref):
    coeffs = coeffs_ref[...]
    high = coeffs.astype(jnp.bfloat16)
    low = (coeffs - high.astype(jnp.float32)).astype(jnp.bfloat16)
    cols, modes = coeffs.shape
    for z in range(data_ref.shape[1] // cols):
        data = data_ref[:, z * cols : (z + 1) * cols]
        fields = jnp.dot(data, high, preferred_element_type=jnp.float32)
        fields = fields + jnp.dot(data, low, preferred_element_type=jnp.float32)
        fields_ref[:, z * modes : (z + 1) * modes] = fields.astype(fields_ref.dtype)
        image = image_ref[:, z * cols : (z + 1) * cols]
        image_high = image.astype(jnp.bfloat16)
        image_low = (image - image_high.astype(jnp.float32)).astype(jnp.bfloat16)
        diffused = jnp.dot(image_high, high, preferred_element_type=jnp.float32)
        diffused = diffused + jnp.dot(image_high, low, preferred_element_type=jnp.float32)
        diffused = diffused + jnp.dot(image_low, high, preferred_element_type=jnp.float32)
        diffused_ref[:, z * modes : (z + 1) * modes] = diffused.astype(diffused_ref.dtype)


def project_modes(data, image, coeffs):
    rows, width = data.shape
    out_width = width // coeffs.shape[0] * coeffs.shape[1]
    vmem = pl.BlockSpec(memory_space=pltpu.VMEM)
    shape = jax.ShapeDtypeStruct((rows, out_width), jnp.bfloat16)
    return pl.pallas_call(
        modes_kernel,
        out_shape=(shape, shape),
        in_specs=[vmem, vmem, vmem],
        out_specs=(vmem, vmem),
    )(data, image, coeffs)


def seven_point(center, around_xy, around_z, stride):
    total = around_xy[2:, 1:-1] + around_xy[:-2, 1:-1] + around_xy[1:-1, 2:] + around_xy[1:-1, :-2]
    total = total + around_z[:, :, 2 * stride :] + around_z[:, :, : -2 * stride]
    return total - 6.0 * center


def split(value):
    high = value.astype(jnp.bfloat16)
    return high, (value - high.astype(jnp.float32)).astype(jnp.bfloat16)


def exact_dot(left, right, contract=1):
    numbers = (((contract,), (0,)), ((), ()))
    left_high, left_low = split(left)
    right_high, right_low = split(right)
    total = lax.dot_general(left_high, right_high, numbers, preferred_element_type=jnp.float32)
    total = total + lax.dot_general(left_high, right_low, numbers, preferred_element_type=jnp.float32)
    return total + lax.dot_general(left_low, right_high, numbers, preferred_element_type=jnp.float32)


def factor_kernel(gram_ref, prior_ref, cross_ref, out_ref, reduced_ref):
    size = gram_ref.shape[0]
    rows = lax.broadcasted_iota(jnp.int32, (size, size), 0)
    cols = lax.broadcasted_iota(jnp.int32, (size, size), 1)
    work = gram_ref[...]
    upper = jnp.zeros_like(work)
    for j in range(size):
        pivot = jnp.sqrt(work[j : j + 1, j : j + 1])
        column = jnp.where(rows[:, j : j + 1] >= j, work[:, j : j + 1] / pivot, 0.0)
        row = jnp.where(cols[j : j + 1, :] >= j, work[j : j + 1, :] / pivot, 0.0)
        upper = jnp.where(rows == j, row, upper)
        work = work - column * row
    solved = prior_ref[...]
    result = jnp.zeros_like(solved)
    picks = lax.broadcasted_iota(jnp.int32, solved.shape, 0)
    for i in reversed(range(size)):
        value = solved[i : i + 1, :] / upper[i : i + 1, i : i + 1]
        result = jnp.where(picks == i, value, result)
        solved = solved - upper[:, i : i + 1] * value
    out_ref[...] = result
    inner = exact_dot(cross_ref[...], result)
    reduced_ref[...] = exact_dot(result, inner, contract=0)


def factor_basis(gram_matrix, prior_basis, cross):
    vmem = pl.BlockSpec(memory_space=pltpu.VMEM)
    modes = prior_basis.shape[1]
    return pl.pallas_call(
        factor_kernel,
        out_shape=(
            jax.ShapeDtypeStruct(prior_basis.shape, prior_basis.dtype),
            jax.ShapeDtypeStruct((modes, modes), prior_basis.dtype),
        ),
        in_specs=[vmem, vmem, vmem],
        out_specs=(vmem, vmem),
    )((gram_matrix + gram_matrix.T) * 0.5, prior_basis, cross)


def cross_kernel(data_ref, image_ref, out_ref):
    cols = out_ref.shape[0]
    total = jnp.zeros(out_ref.shape, jnp.float32)
    for z in range(data_ref.shape[1] // cols):
        data = data_ref[:, z * cols : (z + 1) * cols]
        high, low = split(image_ref[:, z * cols : (z + 1) * cols])
        numbers = (((0,), (0,)), ((), ()))
        total = total + lax.dot_general(data, high, numbers, preferred_element_type=jnp.float32)
        total = total + lax.dot_general(data, low, numbers, preferred_element_type=jnp.float32)
    out_ref[...] = total


def cross_products(data, image):
    vmem = pl.BlockSpec(memory_space=pltpu.VMEM)
    return pl.pallas_call(
        cross_kernel,
        out_shape=jax.ShapeDtypeStruct((COLS, COLS), jnp.float32),
        in_specs=[vmem, vmem],
        out_specs=vmem,
    )(data, image)


def tree_sum(values):
    while len(values) > 1:
        values = [values[i] + values[i + 1] for i in range(0, len(values), 2)]
    return values[0]


REDUCE_GROUPS = (("gx", "gz_1"), ("gy",), ("gz_0",))


def allreduce_kernel(groups, part_ref, out_ref, acc, *rest):
    bufs, (send_sems, recv_sems) = rest[: len(groups)], rest[len(groups) :]
    me = {axis: lax.axis_index(axis) for group in groups for axis, _ in group}

    def linear(group):
        index = 0
        for axis, size in group:
            index = index * size + me[axis]
        return index

    def peer(group, step):
        count = 1
        for _, size in group:
            count *= size
        target = lax.rem(linear(group) + step, count)
        device = dict(me)
        for axis, size in reversed(group):
            device[axis] = lax.rem(target, size)
            target = target // size
        return tuple(device[axis] for axis in GX_GY_GZ)

    counts = []
    for group in groups:
        count = 1
        for _, size in group:
            count *= size
        counts.append(count)
    barrier = pltpu.get_barrier_semaphore()
    for group, count in zip(groups, counts):
        for step in range(1, count):
            pl.semaphore_signal(
                barrier, inc=1, device_id=peer(group, step), device_id_type=pl.DeviceIdType.MESH
            )
    pl.semaphore_wait(barrier, sum(counts) - len(counts))
    acc[...] = part_ref[...]
    slot = 0
    for group, count, buf in zip(groups, counts, bufs):
        copies = []
        for step in range(1, count):
            copy = pltpu.make_async_remote_copy(
                src_ref=acc,
                dst_ref=buf.at[step - 1],
                send_sem=send_sems.at[slot],
                recv_sem=recv_sems.at[slot],
                device_id=peer(group, step),
                device_id_type=pl.DeviceIdType.MESH,
            )
            copy.start()
            copies.append(copy)
            slot += 1
        for copy in copies:
            copy.wait()
        own = acc[...]
        mine = linear(group)
        values = []
        for source in range(count):
            held = jnp.maximum(lax.rem(mine - source + count, count) - 1, 0)
            values.append(jnp.where(mine == source, own, buf[held]))
        acc[...] = tree_sum(values)
    out_ref[...] = acc[...]


def allreduce(part):
    groups = tuple(
        tuple((axis, lax.axis_size(axis)) for axis in group) for group in REDUCE_GROUPS
    )
    counts = [functools.reduce(lambda a, b: a * b, [size for _, size in group]) for group in groups]
    copies = sum(count - 1 for count in counts)
    return pl.pallas_call(
        functools.partial(allreduce_kernel, groups),
        out_shape=jax.ShapeDtypeStruct(part.shape, part.dtype),
        in_specs=[pl.BlockSpec(memory_space=pltpu.VMEM)],
        out_specs=pl.BlockSpec(memory_space=pltpu.VMEM),
        scratch_shapes=[pltpu.VMEM(part.shape, part.dtype)]
        + [pltpu.VMEM((max(count - 1, 1),) + part.shape, part.dtype) for count in counts]
        + [pltpu.SemaphoreType.DMA((copies,)), pltpu.SemaphoreType.DMA((copies,))],
        compiler_params=pltpu.CompilerParams(collective_id=0, has_side_effects=True),
    )(part)


def exchange_kernel(plane, size_y, payload_ref, ids_ref, out_ref, out_ids_ref, send_sems, recv_sems, local_sems):
    me = lax.axis_index("gx") * size_y + lax.axis_index("gy")
    rest = tuple(lax.axis_index(axis) for axis in GZ)

    def device(step):
        target = lax.rem(me + step, plane)
        return (target // size_y, lax.rem(target, size_y)) + rest

    barrier = pltpu.get_barrier_semaphore()
    for step in range(1, plane):
        pl.semaphore_signal(barrier, inc=1, device_id=device(step), device_id_type=pl.DeviceIdType.MESH)
    pl.semaphore_wait(barrier, plane - 1)
    pairs = ((payload_ref, out_ref), (ids_ref, out_ids_ref))
    copies = []
    for index, (src, dst) in enumerate(pairs):
        copy = pltpu.make_async_copy(src.at[me], dst.at[me], local_sems.at[index])
        copy.start()
        copies.append(copy)
    for step in range(1, plane):
        target = lax.rem(me + step, plane)
        for index, (src, dst) in enumerate(pairs):
            slot = 2 * (step - 1) + index
            copy = pltpu.make_async_remote_copy(
                src_ref=src.at[target],
                dst_ref=dst.at[me],
                send_sem=send_sems.at[slot],
                recv_sem=recv_sems.at[slot],
                device_id=device(step),
                device_id_type=pl.DeviceIdType.MESH,
            )
            copy.start()
            copies.append(copy)
    for copy in copies:
        copy.wait()


def exchange(payload, ids):
    size_y = lax.axis_size("gy")
    plane = lax.axis_size("gx") * size_y
    vmem = pl.BlockSpec(memory_space=pltpu.VMEM)
    return pl.pallas_call(
        functools.partial(exchange_kernel, plane, size_y),
        out_shape=(
            jax.ShapeDtypeStruct(payload.shape, payload.dtype),
            jax.ShapeDtypeStruct(ids.shape, ids.dtype),
        ),
        in_specs=[vmem, vmem],
        out_specs=(vmem, vmem),
        scratch_shapes=[
            pltpu.SemaphoreType.DMA((2 * (plane - 1),)),
            pltpu.SemaphoreType.DMA((2 * (plane - 1),)),
            pltpu.SemaphoreType.DMA((2,)),
        ],
        compiler_params=pltpu.CompilerParams(collective_id=1, has_side_effects=True),
    )(payload, ids)


def halo_kernel(sizes, faces_ref, out_ref, send_sems, recv_sems):
    me = [lax.axis_index(axis) for axis in GX_GY_GZ]
    size_z1 = sizes[3]
    size_z = sizes[2] * size_z1

    def device(dim, step):
        if dim < 2:
            place = list(me)
            place[dim] = lax.rem(me[dim] + step + sizes[dim], sizes[dim])
            return tuple(place)
        z = lax.rem(me[2] * size_z1 + me[3] + step + size_z, size_z)
        return (me[0], me[1], z // size_z1, lax.rem(z, size_z1))

    targets = [device(dim, step) for dim in range(3) for step in (-1, 1)]
    barrier = pltpu.get_barrier_semaphore()
    for target in targets:
        pl.semaphore_signal(barrier, inc=1, device_id=target, device_id_type=pl.DeviceIdType.MESH)
    pl.semaphore_wait(barrier, len(targets))
    copies = []
    for index, target in enumerate(targets):
        copy = pltpu.make_async_remote_copy(
            src_ref=faces_ref.at[index],
            dst_ref=out_ref.at[index],
            send_sem=send_sems.at[index],
            recv_sem=recv_sems.at[index],
            device_id=target,
            device_id_type=pl.DeviceIdType.MESH,
        )
        copy.start()
        copies.append(copy)
    for copy in copies:
        copy.wait()


def halo(faces):
    sizes = tuple(lax.axis_size(axis) for axis in GX_GY_GZ)
    vmem = pl.BlockSpec(memory_space=pltpu.VMEM)
    return pl.pallas_call(
        functools.partial(halo_kernel, sizes),
        out_shape=jax.ShapeDtypeStruct(faces.shape, faces.dtype),
        in_specs=[vmem],
        out_specs=vmem,
        scratch_shapes=[
            pltpu.SemaphoreType.DMA((faces.shape[0],)),
            pltpu.SemaphoreType.DMA((faces.shape[0],)),
        ],
        compiler_params=pltpu.CompilerParams(collective_id=2, has_side_effects=True),
    )(faces)


def diffusion(data_block):
    edge = data_block.shape[0]
    cells = edge * COLS
    faces = jnp.stack(
        [
            data_block[0],
            data_block[-1],
            data_block[:, 0],
            data_block[:, -1],
            data_block[:, :, :COLS].reshape(edge, cells),
            data_block[:, :, -COLS:].reshape(edge, cells),
        ]
    )
    got = halo(faces).astype(jnp.float32)
    gx, gy, gz = lax.axis_index("gx"), lax.axis_index("gy"), lax.axis_index(GZ)
    last = (lax.axis_size("gx") - 1, lax.axis_size("gy") - 1, lax.axis_size(GZ) - 1)
    above_x = jnp.where(gx < last[0], got[0], 0.0)
    below_x = jnp.where(gx > 0, got[1], 0.0)
    above_y = jnp.where(gy < last[1], got[2], 0.0)
    below_y = jnp.where(gy > 0, got[3], 0.0)
    above_z = jnp.where(gz < last[2], got[4], 0.0).reshape(edge, edge, COLS)
    below_z = jnp.where(gz > 0, got[5], 0.0).reshape(edge, edge, COLS)
    center = data_block.astype(jnp.float32)
    along_x = jnp.concatenate([below_x[None], center, above_x[None]], axis=0)
    along_y = jnp.concatenate([below_y[:, None], center, above_y[:, None]], axis=1)
    along_z = jnp.concatenate([below_z, center, above_z], axis=2)
    total = along_x[2:] + along_x[:-2] + along_y[:, 2:] + along_y[:, :-2]
    total = total + along_z[:, :, 2 * COLS :] + along_z[:, :, : -2 * COLS]
    return total - 6.0 * center


def shards(patch_fields, slot_snapshot, slot_brick, prior_basis):
    size_x = lax.axis_size("gx")
    size_y = lax.axis_size("gy")
    size_z = lax.axis_size(GZ)
    plane_size = size_x * size_y
    slot_count = slot_snapshot.shape[0]
    pair_depth = slot_count // plane_size
    total_cells = CELLS * plane_size * size_z
    is_live = slot_snapshot >= 0
    slot_ids = jnp.arange(slot_count, dtype=jnp.int32)
    target_peer = jnp.where(is_live, slot_brick // size_z, plane_size)
    earlier = (target_peer[:, None] == target_peer[None, :]) & (
        slot_ids[None, :] < slot_ids[:, None]
    )
    pair_rank = jnp.sum(earlier.astype(jnp.int32), axis=1)
    position = jnp.where(is_live, target_peer * pair_depth + pair_rank, slot_count)
    slot_hits = position[:, None] == slot_ids[None, :]
    filled = jnp.any(slot_hits, axis=0)
    source = jnp.sum(jnp.where(slot_hits, slot_ids[:, None], 0), axis=0)
    sent_snapshot = jnp.where(filled, jnp.take(slot_snapshot, source, mode="clip"), -1)
    payload = average_cells(patch_fields, source)
    sent_ids = jnp.broadcast_to(sent_snapshot[:, None, None], (slot_count, 8, 128))
    received, received_ids = exchange(payload, sent_ids)
    received_snapshot = received_ids[:, 0, 0]
    snapshots = jnp.arange(SNAPS, dtype=jnp.int32)
    chosen = jnp.sum(
        jnp.where(received_snapshot[None, :] == snapshots[:, None], slot_ids[None, :], 0), axis=1
    )
    arrived = jnp.take(received, chosen, axis=0, mode="clip")
    columns = arrived.reshape(COLS, CELLS)
    partial_gram = jnp.dot(columns, columns.T, preferred_element_type=jnp.float32)
    data_block = columns.T.reshape(EDGE, EDGE, EDGE * COLS)
    data_block_image = diffusion(data_block)
    plane = data_block.shape[0] * data_block.shape[1]
    partial_cross = cross_products(data_block.reshape(plane, -1), data_block_image.reshape(plane, -1))
    totals = allreduce(jnp.concatenate([partial_gram, partial_cross], axis=1))
    gram_total, cross_total = totals[:, :COLS], totals[:, COLS:]
    gram_matrix = gram_total / total_cells
    coeffs, reduced = factor_basis(gram_matrix, prior_basis, cross_total / total_cells)
    mode_fields, diffused = project_modes(
        data_block.reshape(plane, -1), data_block_image.reshape(plane, -1), coeffs
    )
    mode_fields = mode_fields.reshape(EDGE, EDGE, EDGE * MODES)
    diffused = diffused.reshape(EDGE, EDGE, EDGE * MODES)
    return (gram_matrix, mode_fields, diffused, reduced)


def solution(mesh):
    split = Mesh(
        mesh.devices.reshape(mesh.shape["gx"], mesh.shape["gy"], 4, 2), ("gx", "gy", "gz_0", "gz_1")
    )
    in_specs = (P(GX_GY_GZ, None, None), P(GX_GY_GZ), P(GX_GY_GZ), P())
    out_specs = (P(), P("gx", "gy", GZ), P("gx", "gy", GZ), P())
    return jax.shard_map(
        shards, mesh=split, in_specs=in_specs, out_specs=out_specs, check_vma=False
    )
```

```python
import functools

import jax
import jax.numpy as jnp
from jax import lax
from jax.sharding import Mesh
from jax.sharding import PartitionSpec as P
from jax.experimental import pallas as pl
from jax.experimental.pallas import tpu as pltpu

SNAPS = 16
FIELDS = 4
PATCH = 32
MODES = 32
EDGE = 16
CELLS = 4096
COLS = 64
GZ = ("gz_0", "gz_1")
GX_GY_GZ = ("gx", "gy", "gz_0", "gz_1")


HIGHEST = lax.Precision.HIGHEST


def extended(value, sides, width):
    edges = {}
    for axis, dim in sides:
        devices, length = (lax.axis_size(axis), value.shape[dim])
        up = [(i, (i + 1) % devices) for i in range(devices - 1)]
        last = lax.slice_in_dim(value, length - width, length, axis=dim)
        first = lax.slice_in_dim(value, 0, width, axis=dim)
        edges[dim] = (
            lax.ppermute(last, axis, up),
            lax.ppermute(first, axis, [(b, a) for a, b in up]),
        )
    done = []
    for _, dim in sides:
        low, high = edges[dim]
        around = [(width, width) if d in done else (0, 0) for d in range(value.ndim)]
        value = jnp.concatenate([jnp.pad(low, around), value, jnp.pad(high, around)], axis=dim)
        done.append(dim)
    return value


def extended_2(value, sides, width):
    for axis, dim in sides:
        devices, length = (lax.axis_size(axis), value.shape[dim])
        up = [(i, (i + 1) % devices) for i in range(devices - 1)]
        down = [(j, i) for i, j in up]
        last = lax.slice_in_dim(value, length - width, length, axis=dim)
        first = lax.slice_in_dim(value, 0, width, axis=dim)
        before = lax.ppermute(last, axis, up)
        after = lax.ppermute(first, axis, down)
        value = jnp.concatenate([before, value, after], axis=dim)
    return value


def over_axes(value, axes):
    for axis in axes:
        value = lax.psum(value, axis)
    return value


def pairing_matrix():
    fine = jnp.arange(2 * PATCH * PATCH, dtype=jnp.int32)
    fine_y = fine % (PATCH * PATCH) // PATCH
    fine_z = fine % PATCH
    coarse = jnp.arange(EDGE * EDGE, dtype=jnp.int32)
    hit = ((fine_y // 2 * EDGE + fine_z // 2)[:, None] == coarse[None, :])
    return jnp.where(hit, 0.125, 0.0).astype(jnp.bfloat16)


PAIRS_PER_STEP = 4


def average_kernel(source_ref, fine_ref, pairing_ref, out_ref, means_ref):
    slots = fine_ref.shape[0]
    rows = slots * FIELDS
    span = 2 * PATCH * PATCH
    stacked = jnp.concatenate(
        [fine_ref[:, :, i * span : (i + 1) * span].reshape(rows, span) for i in range(PAIRS_PER_STEP)],
        axis=0,
    )
    means = jnp.dot(stacked, pairing_ref[...], preferred_element_type=jnp.float32)
    width = EDGE * EDGE
    for i in range(PAIRS_PER_STEP):
        means_ref[:, :, i * width : (i + 1) * width] = (
            means[i * rows : (i + 1) * rows].reshape(slots, FIELDS, width).astype(means_ref.dtype)
        )
    for slot in range(slots):
        out_ref[slot] = means_ref[source_ref[slot]]


def average_cells(fine_data, source):
    row_count = fine_data.shape[0]
    span = 2 * PATCH * PATCH * PAIRS_PER_STEP
    width = EDGE * EDGE * PAIRS_PER_STEP
    steps = EDGE // PAIRS_PER_STEP
    grid_spec = pltpu.PrefetchScalarGridSpec(
        num_scalar_prefetch=1,
        grid=(steps,),
        in_specs=[
            pl.BlockSpec((row_count, FIELDS, span), lambda g, order: (0, 0, g)),
            pl.BlockSpec((2 * PATCH * PATCH, EDGE * EDGE), lambda g, order: (0, 0)),
        ],
        out_specs=pl.BlockSpec((row_count, FIELDS, width), lambda g, order: (0, 0, g)),
        scratch_shapes=[pltpu.VMEM((row_count, FIELDS, width), jnp.bfloat16)],
    )
    return pl.pallas_call(
        average_kernel,
        grid_spec=grid_spec,
        out_shape=jax.ShapeDtypeStruct((row_count, FIELDS, CELLS), jnp.bfloat16),
    )(source, fine_data, pairing_matrix())


def modes_kernel(data_ref, image_ref, coeffs_ref, fields_ref, diffused_ref):
    coeffs = coeffs_ref[...]
    high = coeffs.astype(jnp.bfloat16)
    low = (coeffs - high.astype(jnp.float32)).astype(jnp.bfloat16)
    cols, modes = coeffs.shape
    for z in range(data_ref.shape[1] // cols):
        data = data_ref[:, z * cols : (z + 1) * cols]
        fields = jnp.dot(data, high, preferred_element_type=jnp.float32)
        fields = fields + jnp.dot(data, low, preferred_element_type=jnp.float32)
        fields_ref[:, z * modes : (z + 1) * modes] = fields.astype(fields_ref.dtype)
        image = image_ref[:, z * cols : (z + 1) * cols]
        image_high = image.astype(jnp.bfloat16)
        image_low = (image - image_high.astype(jnp.float32)).astype(jnp.bfloat16)
        diffused = jnp.dot(image_high, high, preferred_element_type=jnp.float32)
        diffused = diffused + jnp.dot(image_high, low, preferred_element_type=jnp.float32)
        diffused = diffused + jnp.dot(image_low, high, preferred_element_type=jnp.float32)
        diffused_ref[:, z * modes : (z + 1) * modes] = diffused.astype(diffused_ref.dtype)


def project_modes(data, image, coeffs):
    rows, width = data.shape
    out_width = width // coeffs.shape[0] * coeffs.shape[1]
    vmem = pl.BlockSpec(memory_space=pltpu.VMEM)
    shape = jax.ShapeDtypeStruct((rows, out_width), jnp.bfloat16)
    return pl.pallas_call(
        modes_kernel,
        out_shape=(shape, shape),
        in_specs=[vmem, vmem, vmem],
        out_specs=(vmem, vmem),
    )(data, image, coeffs)


def seven_point(center, around_xy, around_z, stride):
    total = around_xy[2:, 1:-1] + around_xy[:-2, 1:-1] + around_xy[1:-1, 2:] + around_xy[1:-1, :-2]
    total = total + around_z[:, :, 2 * stride :] + around_z[:, :, : -2 * stride]
    return total - 6.0 * center


def split(value):
    high = value.astype(jnp.bfloat16)
    return high, (value - high.astype(jnp.float32)).astype(jnp.bfloat16)


def exact_dot(left, right, contract=1):
    numbers = (((contract,), (0,)), ((), ()))
    left_high, left_low = split(left)
    right_high, right_low = split(right)
    total = lax.dot_general(left_high, right_high, numbers, preferred_element_type=jnp.float32)
    total = total + lax.dot_general(left_high, right_low, numbers, preferred_element_type=jnp.float32)
    return total + lax.dot_general(left_low, right_high, numbers, preferred_element_type=jnp.float32)


def factor_kernel(gram_ref, prior_ref, cross_ref, out_ref, reduced_ref):
    size = gram_ref.shape[0]
    rows = lax.broadcasted_iota(jnp.int32, (size, size), 0)
    cols = lax.broadcasted_iota(jnp.int32, (size, size), 1)
    work = gram_ref[...]
    upper = jnp.zeros_like(work)
    for j in range(size):
        pivot = jnp.sqrt(work[j : j + 1, j : j + 1])
        column = jnp.where(rows[:, j : j + 1] >= j, work[:, j : j + 1] / pivot, 0.0)
        row = jnp.where(cols[j : j + 1, :] >= j, work[j : j + 1, :] / pivot, 0.0)
        upper = jnp.where(rows == j, row, upper)
        work = work - column * row
    solved = prior_ref[...]
    result = jnp.zeros_like(solved)
    picks = lax.broadcasted_iota(jnp.int32, solved.shape, 0)
    for i in reversed(range(size)):
        value = solved[i : i + 1, :] / upper[i : i + 1, i : i + 1]
        result = jnp.where(picks == i, value, result)
        solved = solved - upper[:, i : i + 1] * value
    out_ref[...] = result
    inner = exact_dot(cross_ref[...], result)
    reduced_ref[...] = exact_dot(result, inner, contract=0)


def factor_basis(gram_matrix, prior_basis, cross):
    vmem = pl.BlockSpec(memory_space=pltpu.VMEM)
    modes = prior_basis.shape[1]
    return pl.pallas_call(
        factor_kernel,
        out_shape=(
            jax.ShapeDtypeStruct(prior_basis.shape, prior_basis.dtype),
            jax.ShapeDtypeStruct((modes, modes), prior_basis.dtype),
        ),
        in_specs=[vmem, vmem, vmem],
        out_specs=(vmem, vmem),
    )((gram_matrix + gram_matrix.T) * 0.5, prior_basis, cross)


def cross_kernel(data_ref, image_ref, out_ref):
    cols = out_ref.shape[0]
    total = jnp.zeros(out_ref.shape, jnp.float32)
    for z in range(data_ref.shape[1] // cols):
        data = data_ref[:, z * cols : (z + 1) * cols]
        high, low = split(image_ref[:, z * cols : (z + 1) * cols])
        numbers = (((0,), (0,)), ((), ()))
        total = total + lax.dot_general(data, high, numbers, preferred_element_type=jnp.float32)
        total = total + lax.dot_general(data, low, numbers, preferred_element_type=jnp.float32)
    out_ref[...] = total


def cross_products(data, image):
    vmem = pl.BlockSpec(memory_space=pltpu.VMEM)
    return pl.pallas_call(
        cross_kernel,
        out_shape=jax.ShapeDtypeStruct((COLS, COLS), jnp.float32),
        in_specs=[vmem, vmem],
        out_specs=vmem,
    )(data, image)


def tree_sum(values):
    while len(values) > 1:
        values = [values[i] + values[i + 1] for i in range(0, len(values), 2)]
    return values[0]


REDUCE_GROUPS = (("gx", "gz_1"), ("gy",), ("gz_0",))


def allreduce_kernel(groups, scale, gram_ref, cross_ref, gram_out, cross_out, acc, *rest):
    bufs, (send_sems, recv_sems) = rest[: len(groups)], rest[len(groups) :]
    me = {axis: lax.axis_index(axis) for group in groups for axis, _ in group}

    def linear(group):
        index = 0
        for axis, size in group:
            index = index * size + me[axis]
        return index

    def peer(group, step):
        count = 1
        for _, size in group:
            count *= size
        target = lax.rem(linear(group) + step, count)
        device = dict(me)
        for axis, size in reversed(group):
            device[axis] = lax.rem(target, size)
            target = target // size
        return tuple(device[axis] for axis in GX_GY_GZ)

    counts = []
    for group in groups:
        count = 1
        for _, size in group:
            count *= size
        counts.append(count)
    barrier = pltpu.get_barrier_semaphore()
    for group, count in zip(groups, counts):
        for step in range(1, count):
            pl.semaphore_signal(
                barrier, inc=1, device_id=peer(group, step), device_id_type=pl.DeviceIdType.MESH
            )
    pl.semaphore_wait(barrier, sum(counts) - len(counts))
    cols = gram_ref.shape[1]
    acc[:, :cols] = gram_ref[...]
    acc[:, cols:] = cross_ref[...]
    slot = 0
    for group, count, buf in zip(groups, counts, bufs):
        copies = []
        for step in range(1, count):
            copy = pltpu.make_async_remote_copy(
                src_ref=acc,
                dst_ref=buf.at[step - 1],
                send_sem=send_sems.at[slot],
                recv_sem=recv_sems.at[slot],
                device_id=peer(group, step),
                device_id_type=pl.DeviceIdType.MESH,
            )
            copy.start()
            copies.append(copy)
            slot += 1
        for copy in copies:
            copy.wait()
        own = acc[...]
        mine = linear(group)
        values = []
        for source in range(count):
            held = jnp.maximum(lax.rem(mine - source + count, count) - 1, 0)
            values.append(jnp.where(mine == source, own, buf[held]))
        acc[...] = tree_sum(values)
    total = acc[...]
    gram_out[...] = total[:, :cols] * scale
    cross_out[...] = total[:, cols:] * scale


def allreduce(gram, cross, scale):
    part = jax.ShapeDtypeStruct((gram.shape[0], gram.shape[1] + cross.shape[1]), gram.dtype)
    groups = tuple(
        tuple((axis, lax.axis_size(axis)) for axis in group) for group in REDUCE_GROUPS
    )
    counts = [functools.reduce(lambda a, b: a * b, [size for _, size in group]) for group in groups]
    copies = sum(count - 1 for count in counts)
    return pl.pallas_call(
        functools.partial(allreduce_kernel, groups, scale),
        out_shape=(
            jax.ShapeDtypeStruct(gram.shape, gram.dtype),
            jax.ShapeDtypeStruct(cross.shape, cross.dtype),
        ),
        in_specs=[pl.BlockSpec(memory_space=pltpu.VMEM)] * 2,
        out_specs=(pl.BlockSpec(memory_space=pltpu.VMEM),) * 2,
        scratch_shapes=[pltpu.VMEM(part.shape, part.dtype)]
        + [pltpu.VMEM((max(count - 1, 1),) + part.shape, part.dtype) for count in counts]
        + [pltpu.SemaphoreType.DMA((copies,)), pltpu.SemaphoreType.DMA((copies,))],
        compiler_params=pltpu.CompilerParams(collective_id=0, has_side_effects=True),
    )(gram, cross)


def exchange_kernel(plane, size_y, payload_ref, ids_ref, out_ref, out_ids_ref, send_sems, recv_sems, local_sems):
    me = lax.axis_index("gx") * size_y + lax.axis_index("gy")
    rest = tuple(lax.axis_index(axis) for axis in GZ)

    def device(step):
        target = lax.rem(me + step, plane)
        return (target // size_y, lax.rem(target, size_y)) + rest

    barrier = pltpu.get_barrier_semaphore()
    for step in range(1, plane):
        pl.semaphore_signal(barrier, inc=1, device_id=device(step), device_id_type=pl.DeviceIdType.MESH)
    pl.semaphore_wait(barrier, plane - 1)
    pairs = ((payload_ref, out_ref), (ids_ref, out_ids_ref))
    copies = []
    for index, (src, dst) in enumerate(pairs):
        copy = pltpu.make_async_copy(src.at[me], dst.at[me], local_sems.at[index])
        copy.start()
        copies.append(copy)
    for step in range(1, plane):
        target = lax.rem(me + step, plane)
        for index, (src, dst) in enumerate(pairs):
            slot = 2 * (step - 1) + index
            copy = pltpu.make_async_remote_copy(
                src_ref=src.at[target],
                dst_ref=dst.at[me],
                send_sem=send_sems.at[slot],
                recv_sem=recv_sems.at[slot],
                device_id=device(step),
                device_id_type=pl.DeviceIdType.MESH,
            )
            copy.start()
            copies.append(copy)
    for copy in copies:
        copy.wait()


def exchange(payload, ids):
    size_y = lax.axis_size("gy")
    plane = lax.axis_size("gx") * size_y
    vmem = pl.BlockSpec(memory_space=pltpu.VMEM)
    return pl.pallas_call(
        functools.partial(exchange_kernel, plane, size_y),
        out_shape=(
            jax.ShapeDtypeStruct(payload.shape, payload.dtype),
            jax.ShapeDtypeStruct(ids.shape, ids.dtype),
        ),
        in_specs=[vmem, vmem],
        out_specs=(vmem, vmem),
        scratch_shapes=[
            pltpu.SemaphoreType.DMA((2 * (plane - 1),)),
            pltpu.SemaphoreType.DMA((2 * (plane - 1),)),
            pltpu.SemaphoreType.DMA((2,)),
        ],
        compiler_params=pltpu.CompilerParams(collective_id=1, has_side_effects=True),
    )(payload, ids)


def halo_kernel(sizes, faces_ref, out_ref, send_sems, recv_sems):
    me = [lax.axis_index(axis) for axis in GX_GY_GZ]
    size_z1 = sizes[3]
    size_z = sizes[2] * size_z1

    def device(dim, step):
        if dim < 2:
            place = list(me)
            place[dim] = lax.rem(me[dim] + step + sizes[dim], sizes[dim])
            return tuple(place)
        z = lax.rem(me[2] * size_z1 + me[3] + step + size_z, size_z)
        return (me[0], me[1], z // size_z1, lax.rem(z, size_z1))

    targets = [device(dim, step) for dim in range(3) for step in (-1, 1)]
    barrier = pltpu.get_barrier_semaphore()
    for target in targets:
        pl.semaphore_signal(barrier, inc=1, device_id=target, device_id_type=pl.DeviceIdType.MESH)
    pl.semaphore_wait(barrier, len(targets))
    copies = []
    for index, target in enumerate(targets):
        copy = pltpu.make_async_remote_copy(
            src_ref=faces_ref.at[index],
            dst_ref=out_ref.at[index],
            send_sem=send_sems.at[index],
            recv_sem=recv_sems.at[index],
            device_id=target,
            device_id_type=pl.DeviceIdType.MESH,
        )
        copy.start()
        copies.append(copy)
    for copy in copies:
        copy.wait()


def halo(faces):
    sizes = tuple(lax.axis_size(axis) for axis in GX_GY_GZ)
    vmem = pl.BlockSpec(memory_space=pltpu.VMEM)
    return pl.pallas_call(
        functools.partial(halo_kernel, sizes),
        out_shape=jax.ShapeDtypeStruct(faces.shape, faces.dtype),
        in_specs=[vmem],
        out_specs=vmem,
        scratch_shapes=[
            pltpu.SemaphoreType.DMA((faces.shape[0],)),
            pltpu.SemaphoreType.DMA((faces.shape[0],)),
        ],
        compiler_params=pltpu.CompilerParams(collective_id=2, has_side_effects=True),
    )(faces)


def diffusion(data_block):
    edge = data_block.shape[0]
    cells = edge * COLS
    faces = jnp.stack(
        [
            data_block[0],
            data_block[-1],
            data_block[:, 0],
            data_block[:, -1],
            data_block[:, :, :COLS].reshape(edge, cells),
            data_block[:, :, -COLS:].reshape(edge, cells),
        ]
    )
    got = halo(faces).astype(jnp.float32)
    gx, gy, gz = lax.axis_index("gx"), lax.axis_index("gy"), lax.axis_index(GZ)
    last = (lax.axis_size("gx") - 1, lax.axis_size("gy") - 1, lax.axis_size(GZ) - 1)
    above_x = jnp.where(gx < last[0], got[0], 0.0)
    below_x = jnp.where(gx > 0, got[1], 0.0)
    above_y = jnp.where(gy < last[1], got[2], 0.0)
    below_y = jnp.where(gy > 0, got[3], 0.0)
    above_z = jnp.where(gz < last[2], got[4], 0.0).reshape(edge, edge, COLS)
    below_z = jnp.where(gz > 0, got[5], 0.0).reshape(edge, edge, COLS)
    center = data_block.astype(jnp.float32)
    along_x = jnp.concatenate([below_x[None], center, above_x[None]], axis=0)
    along_y = jnp.concatenate([below_y[:, None], center, above_y[:, None]], axis=1)
    along_z = jnp.concatenate([below_z, center, above_z], axis=2)
    total = along_x[2:] + along_x[:-2] + along_y[:, 2:] + along_y[:, :-2]
    total = total + along_z[:, :, 2 * COLS :] + along_z[:, :, : -2 * COLS]
    return total - 6.0 * center


def shards(patch_fields, slot_snapshot, slot_brick, prior_basis):
    size_x = lax.axis_size("gx")
    size_y = lax.axis_size("gy")
    size_z = lax.axis_size(GZ)
    plane_size = size_x * size_y
    slot_count = slot_snapshot.shape[0]
    pair_depth = slot_count // plane_size
    total_cells = CELLS * plane_size * size_z
    is_live = slot_snapshot >= 0
    slot_ids = jnp.arange(slot_count, dtype=jnp.int32)
    target_peer = jnp.where(is_live, slot_brick // size_z, plane_size)
    earlier = (target_peer[:, None] == target_peer[None, :]) & (
        slot_ids[None, :] < slot_ids[:, None]
    )
    pair_rank = jnp.sum(earlier.astype(jnp.int32), axis=1)
    position = jnp.where(is_live, target_peer * pair_depth + pair_rank, slot_count)
    slot_hits = position[:, None] == slot_ids[None, :]
    filled = jnp.any(slot_hits, axis=0)
    source = jnp.sum(jnp.where(slot_hits, slot_ids[:, None], 0), axis=0)
    sent_snapshot = jnp.where(filled, jnp.take(slot_snapshot, source, mode="clip"), -1)
    payload = average_cells(patch_fields, source)
    sent_ids = jnp.broadcast_to(sent_snapshot[:, None, None], (slot_count, 8, 128))
    received, received_ids = exchange(payload, sent_ids)
    received_snapshot = received_ids[:, 0, 0]
    snapshots = jnp.arange(SNAPS, dtype=jnp.int32)
    chosen = jnp.sum(
        jnp.where(received_snapshot[None, :] == snapshots[:, None], slot_ids[None, :], 0), axis=1
    )
    arrived = jnp.take(received, chosen, axis=0, mode="clip")
    columns = arrived.reshape(COLS, CELLS)
    partial_gram = jnp.dot(columns, columns.T, preferred_element_type=jnp.float32)
    data_block = columns.T.reshape(EDGE, EDGE, EDGE * COLS)
    data_block_image = diffusion(data_block)
    plane = data_block.shape[0] * data_block.shape[1]
    partial_cross = cross_products(data_block.reshape(plane, -1), data_block_image.reshape(plane, -1))
    gram_matrix, cross_matrix = allreduce(partial_gram, partial_cross, 1.0 / total_cells)
    coeffs, reduced = factor_basis(gram_matrix, prior_basis, cross_matrix)
    mode_fields, diffused = project_modes(
        data_block.reshape(plane, -1), data_block_image.reshape(plane, -1), coeffs
    )
    mode_fields = mode_fields.reshape(EDGE, EDGE, EDGE * MODES)
    diffused = diffused.reshape(EDGE, EDGE, EDGE * MODES)
    return (gram_matrix, mode_fields, diffused, reduced)


def solution(mesh):
    split = Mesh(
        mesh.devices.reshape(mesh.shape["gx"], mesh.shape["gy"], 4, 2), ("gx", "gy", "gz_0", "gz_1")
    )
    in_specs = (P(GX_GY_GZ, None, None), P(GX_GY_GZ), P(GX_GY_GZ), P())
    out_specs = (P(), P("gx", "gy", GZ), P("gx", "gy", GZ), P())
    return jax.shard_map(
        shards, mesh=split, in_specs=in_specs, out_specs=out_specs, check_vma=False
    )
```

```python
import functools

import jax
import jax.numpy as jnp
from jax import lax
from jax.sharding import Mesh
from jax.sharding import PartitionSpec as P
from jax.experimental import pallas as pl
from jax.experimental.pallas import tpu as pltpu

SNAPS = 16
FIELDS = 4
PATCH = 32
MODES = 32
EDGE = 16
CELLS = 4096
COLS = 64
GZ = ("gz_0", "gz_1")
GX_GY_GZ = ("gx", "gy", "gz_0", "gz_1")


HIGHEST = lax.Precision.HIGHEST


def extended(value, sides, width):
    edges = {}
    for axis, dim in sides:
        devices, length = (lax.axis_size(axis), value.shape[dim])
        up = [(i, (i + 1) % devices) for i in range(devices - 1)]
        last = lax.slice_in_dim(value, length - width, length, axis=dim)
        first = lax.slice_in_dim(value, 0, width, axis=dim)
        edges[dim] = (
            lax.ppermute(last, axis, up),
            lax.ppermute(first, axis, [(b, a) for a, b in up]),
        )
    done = []
    for _, dim in sides:
        low, high = edges[dim]
        around = [(width, width) if d in done else (0, 0) for d in range(value.ndim)]
        value = jnp.concatenate([jnp.pad(low, around), value, jnp.pad(high, around)], axis=dim)
        done.append(dim)
    return value


def extended_2(value, sides, width):
    for axis, dim in sides:
        devices, length = (lax.axis_size(axis), value.shape[dim])
        up = [(i, (i + 1) % devices) for i in range(devices - 1)]
        down = [(j, i) for i, j in up]
        last = lax.slice_in_dim(value, length - width, length, axis=dim)
        first = lax.slice_in_dim(value, 0, width, axis=dim)
        before = lax.ppermute(last, axis, up)
        after = lax.ppermute(first, axis, down)
        value = jnp.concatenate([before, value, after], axis=dim)
    return value


def over_axes(value, axes):
    for axis in axes:
        value = lax.psum(value, axis)
    return value


def pairing_matrix():
    fine = jnp.arange(2 * PATCH * PATCH, dtype=jnp.int32)
    fine_y = fine % (PATCH * PATCH) // PATCH
    fine_z = fine % PATCH
    coarse = jnp.arange(EDGE * EDGE, dtype=jnp.int32)
    hit = ((fine_y // 2 * EDGE + fine_z // 2)[:, None] == coarse[None, :])
    return jnp.where(hit, 0.125, 0.0).astype(jnp.bfloat16)


PAIRS_PER_STEP = 4


def average_kernel(source_ref, fine_ref, pairing_ref, out_ref, means_ref):
    slots = fine_ref.shape[0]
    rows = slots * FIELDS
    span = 2 * PATCH * PATCH
    stacked = jnp.concatenate(
        [fine_ref[:, :, i * span : (i + 1) * span].reshape(rows, span) for i in range(PAIRS_PER_STEP)],
        axis=0,
    )
    means = jnp.dot(stacked, pairing_ref[...], preferred_element_type=jnp.float32)
    width = EDGE * EDGE
    for i in range(PAIRS_PER_STEP):
        means_ref[:, :, i * width : (i + 1) * width] = (
            means[i * rows : (i + 1) * rows].reshape(slots, FIELDS, width).astype(means_ref.dtype)
        )
    for slot in range(slots):
        out_ref[slot] = means_ref[source_ref[slot]]


def average_cells(fine_data, source):
    row_count = fine_data.shape[0]
    span = 2 * PATCH * PATCH * PAIRS_PER_STEP
    width = EDGE * EDGE * PAIRS_PER_STEP
    steps = EDGE // PAIRS_PER_STEP
    grid_spec = pltpu.PrefetchScalarGridSpec(
        num_scalar_prefetch=1,
        grid=(steps,),
        in_specs=[
            pl.BlockSpec((row_count, FIELDS, span), lambda g, order: (0, 0, g)),
            pl.BlockSpec((2 * PATCH * PATCH, EDGE * EDGE), lambda g, order: (0, 0)),
        ],
        out_specs=pl.BlockSpec((row_count, FIELDS, width), lambda g, order: (0, 0, g)),
        scratch_shapes=[pltpu.VMEM((row_count, FIELDS, width), jnp.bfloat16)],
    )
    return pl.pallas_call(
        average_kernel,
        grid_spec=grid_spec,
        out_shape=jax.ShapeDtypeStruct((row_count, FIELDS, CELLS), jnp.bfloat16),
    )(source, fine_data, pairing_matrix())


def modes_kernel(data_ref, image_ref, coeffs_ref, fields_ref, diffused_ref):
    coeffs = coeffs_ref[...]
    high = coeffs.astype(jnp.bfloat16)
    low = (coeffs - high.astype(jnp.float32)).astype(jnp.bfloat16)
    cols, modes = coeffs.shape
    for z in range(data_ref.shape[1] // cols):
        data = data_ref[:, z * cols : (z + 1) * cols]
        fields = jnp.dot(data, high, preferred_element_type=jnp.float32)
        fields = fields + jnp.dot(data, low, preferred_element_type=jnp.float32)
        fields_ref[:, z * modes : (z + 1) * modes] = fields.astype(fields_ref.dtype)
        image = image_ref[:, z * cols : (z + 1) * cols]
        image_high = image.astype(jnp.bfloat16)
        image_low = (image - image_high.astype(jnp.float32)).astype(jnp.bfloat16)
        diffused = jnp.dot(image_high, high, preferred_element_type=jnp.float32)
        diffused = diffused + jnp.dot(image_high, low, preferred_element_type=jnp.float32)
        diffused = diffused + jnp.dot(image_low, high, preferred_element_type=jnp.float32)
        diffused_ref[:, z * modes : (z + 1) * modes] = diffused.astype(diffused_ref.dtype)


def project_modes(data, image, coeffs):
    rows, width = data.shape
    out_width = width // coeffs.shape[0] * coeffs.shape[1]
    vmem = pl.BlockSpec(memory_space=pltpu.VMEM)
    shape = jax.ShapeDtypeStruct((rows, out_width), jnp.bfloat16)
    return pl.pallas_call(
        modes_kernel,
        out_shape=(shape, shape),
        in_specs=[vmem, vmem, vmem],
        out_specs=(vmem, vmem),
    )(data, image, coeffs)


def seven_point(center, around_xy, around_z, stride):
    total = around_xy[2:, 1:-1] + around_xy[:-2, 1:-1] + around_xy[1:-1, 2:] + around_xy[1:-1, :-2]
    total = total + around_z[:, :, 2 * stride :] + around_z[:, :, : -2 * stride]
    return total - 6.0 * center


def split(value):
    high = value.astype(jnp.bfloat16)
    return high, (value - high.astype(jnp.float32)).astype(jnp.bfloat16)


def exact_dot(left, right, contract=1):
    numbers = (((contract,), (0,)), ((), ()))
    left_high, left_low = split(left)
    right_high, right_low = split(right)
    total = lax.dot_general(left_high, right_high, numbers, preferred_element_type=jnp.float32)
    total = total + lax.dot_general(left_high, right_low, numbers, preferred_element_type=jnp.float32)
    return total + lax.dot_general(left_low, right_high, numbers, preferred_element_type=jnp.float32)


def factor_kernel(gram_ref, prior_ref, cross_ref, out_ref, reduced_ref):
    size = gram_ref.shape[0]
    rows = lax.broadcasted_iota(jnp.int32, (size, size), 0)
    cols = lax.broadcasted_iota(jnp.int32, (size, size), 1)
    work = gram_ref[...]
    upper = jnp.zeros_like(work)
    for j in range(size):
        pivot = jnp.sqrt(work[j : j + 1, j : j + 1])
        column = jnp.where(rows[:, j : j + 1] >= j, work[:, j : j + 1] / pivot, 0.0)
        row = jnp.where(cols[j : j + 1, :] >= j, work[j : j + 1, :] / pivot, 0.0)
        upper = jnp.where(rows == j, row, upper)
        work = work - column * row
    solved = prior_ref[...]
    result = jnp.zeros_like(solved)
    picks = lax.broadcasted_iota(jnp.int32, solved.shape, 0)
    for i in reversed(range(size)):
        value = solved[i : i + 1, :] / upper[i : i + 1, i : i + 1]
        result = jnp.where(picks == i, value, result)
        solved = solved - upper[:, i : i + 1] * value
    out_ref[...] = result
    inner = exact_dot(cross_ref[...], result)
    reduced_ref[...] = exact_dot(result, inner, contract=0)


def factor_basis(gram_matrix, prior_basis, cross):
    vmem = pl.BlockSpec(memory_space=pltpu.VMEM)
    modes = prior_basis.shape[1]
    return pl.pallas_call(
        factor_kernel,
        out_shape=(
            jax.ShapeDtypeStruct(prior_basis.shape, prior_basis.dtype),
            jax.ShapeDtypeStruct((modes, modes), prior_basis.dtype),
        ),
        in_specs=[vmem, vmem, vmem],
        out_specs=(vmem, vmem),
    )((gram_matrix + gram_matrix.T) * 0.5, prior_basis, cross)


def cross_kernel(data_ref, image_ref, out_ref):
    cols = out_ref.shape[0]
    total = jnp.zeros(out_ref.shape, jnp.float32)
    for z in range(data_ref.shape[1] // cols):
        data = data_ref[:, z * cols : (z + 1) * cols]
        high, low = split(image_ref[:, z * cols : (z + 1) * cols])
        numbers = (((0,), (0,)), ((), ()))
        total = total + lax.dot_general(data, high, numbers, preferred_element_type=jnp.float32)
        total = total + lax.dot_general(data, low, numbers, preferred_element_type=jnp.float32)
    out_ref[...] = total


def cross_products(data, image):
    vmem = pl.BlockSpec(memory_space=pltpu.VMEM)
    return pl.pallas_call(
        cross_kernel,
        out_shape=jax.ShapeDtypeStruct((COLS, COLS), jnp.float32),
        in_specs=[vmem, vmem],
        out_specs=vmem,
    )(data, image)


def tree_sum(values):
    while len(values) > 1:
        values = [values[i] + values[i + 1] for i in range(0, len(values), 2)]
    return values[0]


REDUCE_GROUPS = (("gx", "gz_1"), ("gy",), ("gz_0",))


def allreduce_kernel(groups, part_ref, out_ref, acc, *rest):
    bufs, (send_sems, recv_sems) = rest[: len(groups)], rest[len(groups) :]
    me = {axis: lax.axis_index(axis) for group in groups for axis, _ in group}

    def linear(group):
        index = 0
        for axis, size in group:
            index = index * size + me[axis]
        return index

    def peer(group, step):
        count = 1
        for _, size in group:
            count *= size
        target = lax.rem(linear(group) + step, count)
        device = dict(me)
        for axis, size in reversed(group):
            device[axis] = lax.rem(target, size)
            target = target // size
        return tuple(device[axis] for axis in GX_GY_GZ)

    counts = []
    for group in groups:
        count = 1
        for _, size in group:
            count *= size
        counts.append(count)
    barrier = pltpu.get_barrier_semaphore()
    for group, count in zip(groups, counts):
        for step in range(1, count):
            pl.semaphore_signal(
                barrier, inc=1, device_id=peer(group, step), device_id_type=pl.DeviceIdType.MESH
            )
    pl.semaphore_wait(barrier, sum(counts) - len(counts))
    acc[...] = part_ref[...]
    slot = 0
    for group, count, buf in zip(groups, counts, bufs):
        copies = []
        for step in range(1, count):
            copy = pltpu.make_async_remote_copy(
                src_ref=acc,
                dst_ref=buf.at[step - 1],
                send_sem=send_sems.at[slot],
                recv_sem=recv_sems.at[slot],
                device_id=peer(group, step),
                device_id_type=pl.DeviceIdType.MESH,
            )
            copy.start()
            copies.append(copy)
            slot += 1
        for copy in copies:
            copy.wait()
        own = acc[...]
        mine = linear(group)
        values = []
        for source in range(count):
            held = jnp.maximum(lax.rem(mine - source + count, count) - 1, 0)
            values.append(jnp.where(mine == source, own, buf[held]))
        acc[...] = tree_sum(values)
    out_ref[...] = acc[...]


def allreduce(part):
    groups = tuple(
        tuple((axis, lax.axis_size(axis)) for axis in group) for group in REDUCE_GROUPS
    )
    counts = [functools.reduce(lambda a, b: a * b, [size for _, size in group]) for group in groups]
    copies = sum(count - 1 for count in counts)
    return pl.pallas_call(
        functools.partial(allreduce_kernel, groups),
        out_shape=jax.ShapeDtypeStruct(part.shape, part.dtype),
        in_specs=[pl.BlockSpec(memory_space=pltpu.VMEM)],
        out_specs=pl.BlockSpec(memory_space=pltpu.VMEM),
        scratch_shapes=[pltpu.VMEM(part.shape, part.dtype)]
        + [pltpu.VMEM((max(count - 1, 1),) + part.shape, part.dtype) for count in counts]
        + [pltpu.SemaphoreType.DMA((copies,)), pltpu.SemaphoreType.DMA((copies,))],
        compiler_params=pltpu.CompilerParams(collective_id=0, has_side_effects=True),
    )(part)


def exchange_kernel(plane, size_y, payload_ref, ids_ref, out_ref, out_ids_ref, send_sems, recv_sems, local_sems):
    me = lax.axis_index("gx") * size_y + lax.axis_index("gy")
    rest = tuple(lax.axis_index(axis) for axis in GZ)

    def device(step):
        target = lax.rem(me + step, plane)
        return (target // size_y, lax.rem(target, size_y)) + rest

    barrier = pltpu.get_barrier_semaphore()
    for step in range(1, plane):
        pl.semaphore_signal(barrier, inc=1, device_id=device(step), device_id_type=pl.DeviceIdType.MESH)
    pl.semaphore_wait(barrier, plane - 1)
    pairs = ((payload_ref, out_ref), (ids_ref, out_ids_ref))
    copies = []
    for index, (src, dst) in enumerate(pairs):
        copy = pltpu.make_async_copy(src.at[me], dst.at[me], local_sems.at[index])
        copy.start()
        copies.append(copy)
    for step in range(1, plane):
        target = lax.rem(me + step, plane)
        for index, (src, dst) in enumerate(pairs):
            slot = 2 * (step - 1) + index
            copy = pltpu.make_async_remote_copy(
                src_ref=src.at[target],
                dst_ref=dst.at[me],
                send_sem=send_sems.at[slot],
                recv_sem=recv_sems.at[slot],
                device_id=device(step),
                device_id_type=pl.DeviceIdType.MESH,
            )
            copy.start()
            copies.append(copy)
    for copy in copies:
        copy.wait()


def exchange(payload, ids):
    size_y = lax.axis_size("gy")
    plane = lax.axis_size("gx") * size_y
    vmem = pl.BlockSpec(memory_space=pltpu.VMEM)
    return pl.pallas_call(
        functools.partial(exchange_kernel, plane, size_y),
        out_shape=(
            jax.ShapeDtypeStruct(payload.shape, payload.dtype),
            jax.ShapeDtypeStruct(ids.shape, ids.dtype),
        ),
        in_specs=[vmem, vmem],
        out_specs=(vmem, vmem),
        scratch_shapes=[
            pltpu.SemaphoreType.DMA((2 * (plane - 1),)),
            pltpu.SemaphoreType.DMA((2 * (plane - 1),)),
            pltpu.SemaphoreType.DMA((2,)),
        ],
        compiler_params=pltpu.CompilerParams(collective_id=1, has_side_effects=True),
    )(payload, ids)


def halo_kernel(sizes, faces_ref, out_ref, send_sems, recv_sems):
    me = [lax.axis_index(axis) for axis in GX_GY_GZ]
    size_z1 = sizes[3]
    size_z = sizes[2] * size_z1

    def device(dim, step):
        if dim < 2:
            place = list(me)
            place[dim] = lax.rem(me[dim] + step + sizes[dim], sizes[dim])
            return tuple(place)
        z = lax.rem(me[2] * size_z1 + me[3] + step + size_z, size_z)
        return (me[0], me[1], z // size_z1, lax.rem(z, size_z1))

    targets = [device(dim, step) for dim in range(3) for step in (-1, 1)]
    barrier = pltpu.get_barrier_semaphore()
    for target in targets:
        pl.semaphore_signal(barrier, inc=1, device_id=target, device_id_type=pl.DeviceIdType.MESH)
    pl.semaphore_wait(barrier, len(targets))
    copies = []
    for index, target in enumerate(targets):
        copy = pltpu.make_async_remote_copy(
            src_ref=faces_ref.at[index],
            dst_ref=out_ref.at[index],
            send_sem=send_sems.at[index],
            recv_sem=recv_sems.at[index],
            device_id=target,
            device_id_type=pl.DeviceIdType.MESH,
        )
        copy.start()
        copies.append(copy)
    for copy in copies:
        copy.wait()


def halo(faces):
    sizes = tuple(lax.axis_size(axis) for axis in GX_GY_GZ)
    vmem = pl.BlockSpec(memory_space=pltpu.VMEM)
    return pl.pallas_call(
        functools.partial(halo_kernel, sizes),
        out_shape=jax.ShapeDtypeStruct(faces.shape, faces.dtype),
        in_specs=[vmem],
        out_specs=vmem,
        scratch_shapes=[
            pltpu.SemaphoreType.DMA((faces.shape[0],)),
            pltpu.SemaphoreType.DMA((faces.shape[0],)),
        ],
        compiler_params=pltpu.CompilerParams(collective_id=2, has_side_effects=True),
    )(faces)


def diffusion(data_block):
    edge = data_block.shape[0]
    cells = edge * COLS
    faces = jnp.stack(
        [
            data_block[0],
            data_block[-1],
            data_block[:, 0],
            data_block[:, -1],
            data_block[:, :, :COLS].reshape(edge, cells),
            data_block[:, :, -COLS:].reshape(edge, cells),
        ]
    )
    got = halo(faces).astype(jnp.float32)
    gx, gy, gz = lax.axis_index("gx"), lax.axis_index("gy"), lax.axis_index(GZ)
    last = (lax.axis_size("gx") - 1, lax.axis_size("gy") - 1, lax.axis_size(GZ) - 1)
    above_x = jnp.where(gx < last[0], got[0], 0.0)
    below_x = jnp.where(gx > 0, got[1], 0.0)
    above_y = jnp.where(gy < last[1], got[2], 0.0)
    below_y = jnp.where(gy > 0, got[3], 0.0)
    above_z = jnp.where(gz < last[2], got[4], 0.0).reshape(edge, edge, COLS)
    below_z = jnp.where(gz > 0, got[5], 0.0).reshape(edge, edge, COLS)
    center = data_block.astype(jnp.float32)
    along_x = jnp.concatenate([below_x[None], center, above_x[None]], axis=0)
    along_y = jnp.concatenate([below_y[:, None], center, above_y[:, None]], axis=1)
    along_z = jnp.concatenate([below_z, center, above_z], axis=2)
    total = along_x[2:] + along_x[:-2] + along_y[:, 2:] + along_y[:, :-2]
    total = total + along_z[:, :, 2 * COLS :] + along_z[:, :, : -2 * COLS]
    return total - 6.0 * center


def shards(patch_fields, slot_snapshot, slot_brick, prior_basis):
    size_x = lax.axis_size("gx")
    size_y = lax.axis_size("gy")
    size_z = lax.axis_size(GZ)
    plane_size = size_x * size_y
    slot_count = slot_snapshot.shape[0]
    pair_depth = slot_count // plane_size
    total_cells = CELLS * plane_size * size_z
    is_live = slot_snapshot >= 0
    slot_ids = jnp.arange(slot_count, dtype=jnp.int32)
    target_peer = jnp.where(is_live, slot_brick // size_z, plane_size)
    earlier = (target_peer[:, None] == target_peer[None, :]) & (
        slot_ids[None, :] < slot_ids[:, None]
    )
    pair_rank = jnp.sum(earlier.astype(jnp.int32), axis=1)
    position = jnp.where(is_live, target_peer * pair_depth + pair_rank, slot_count)
    slot_hits = position[:, None] == slot_ids[None, :]
    filled = jnp.any(slot_hits, axis=0)
    source = jnp.sum(jnp.where(slot_hits, slot_ids[:, None], 0), axis=0)
    sent_snapshot = jnp.where(filled, jnp.take(slot_snapshot, source, mode="clip"), -1)
    payload = average_cells(patch_fields, source)
    sent_ids = jnp.broadcast_to(sent_snapshot[:, None, None], (slot_count, 8, 128))
    received, received_ids = exchange(payload, sent_ids)
    received_snapshot = received_ids[:, 0, 0]
    snapshots = jnp.arange(SNAPS, dtype=jnp.int32)
    picks = (received_snapshot[None, :] == snapshots[:, None]).astype(received.dtype)
    arrived = jnp.dot(
        picks, received.reshape(slot_count, FIELDS * CELLS), preferred_element_type=jnp.float32
    )
    columns = arrived.astype(received.dtype).reshape(COLS, CELLS)
    partial_gram = jnp.dot(columns, columns.T, preferred_element_type=jnp.float32)
    data_block = columns.T.reshape(EDGE, EDGE, EDGE * COLS)
    data_block_image = diffusion(data_block)
    plane = data_block.shape[0] * data_block.shape[1]
    partial_cross = cross_products(data_block.reshape(plane, -1), data_block_image.reshape(plane, -1))
    totals = allreduce(jnp.concatenate([partial_gram, partial_cross], axis=1))
    gram_total, cross_total = totals[:, :COLS], totals[:, COLS:]
    gram_matrix = gram_total / total_cells
    coeffs, reduced = factor_basis(gram_matrix, prior_basis, cross_total / total_cells)
    mode_fields, diffused = project_modes(
        data_block.reshape(plane, -1), data_block_image.reshape(plane, -1), coeffs
    )
    mode_fields = mode_fields.reshape(EDGE, EDGE, EDGE * MODES)
    diffused = diffused.reshape(EDGE, EDGE, EDGE * MODES)
    return (gram_matrix, mode_fields, diffused, reduced)


def solution(mesh):
    split = Mesh(
        mesh.devices.reshape(mesh.shape["gx"], mesh.shape["gy"], 4, 2), ("gx", "gy", "gz_0", "gz_1")
    )
    in_specs = (P(GX_GY_GZ, None, None), P(GX_GY_GZ), P(GX_GY_GZ), P())
    out_specs = (P(), P("gx", "gy", GZ), P("gx", "gy", GZ), P())
    return jax.shard_map(
        shards, mesh=split, in_specs=in_specs, out_specs=out_specs, check_vma=False
    )
```

```python
import functools

import jax
import jax.numpy as jnp
from jax import lax
from jax.sharding import Mesh
from jax.sharding import PartitionSpec as P
from jax.experimental import pallas as pl
from jax.experimental.pallas import tpu as pltpu

SNAPS = 16
FIELDS = 4
PATCH = 32
MODES = 32
EDGE = 16
CELLS = 4096
COLS = 64
GZ = ("gz_0", "gz_1")
GX_GY_GZ = ("gx", "gy", "gz_0", "gz_1")


HIGHEST = lax.Precision.HIGHEST


def extended(value, sides, width):
    edges = {}
    for axis, dim in sides:
        devices, length = (lax.axis_size(axis), value.shape[dim])
        up = [(i, (i + 1) % devices) for i in range(devices - 1)]
        last = lax.slice_in_dim(value, length - width, length, axis=dim)
        first = lax.slice_in_dim(value, 0, width, axis=dim)
        edges[dim] = (
            lax.ppermute(last, axis, up),
            lax.ppermute(first, axis, [(b, a) for a, b in up]),
        )
    done = []
    for _, dim in sides:
        low, high = edges[dim]
        around = [(width, width) if d in done else (0, 0) for d in range(value.ndim)]
        value = jnp.concatenate([jnp.pad(low, around), value, jnp.pad(high, around)], axis=dim)
        done.append(dim)
    return value


def extended_2(value, sides, width):
    for axis, dim in sides:
        devices, length = (lax.axis_size(axis), value.shape[dim])
        up = [(i, (i + 1) % devices) for i in range(devices - 1)]
        down = [(j, i) for i, j in up]
        last = lax.slice_in_dim(value, length - width, length, axis=dim)
        first = lax.slice_in_dim(value, 0, width, axis=dim)
        before = lax.ppermute(last, axis, up)
        after = lax.ppermute(first, axis, down)
        value = jnp.concatenate([before, value, after], axis=dim)
    return value


def over_axes(value, axes):
    for axis in axes:
        value = lax.psum(value, axis)
    return value


def pairing_matrix():
    fine = jnp.arange(2 * PATCH * PATCH, dtype=jnp.int32)
    fine_y = fine % (PATCH * PATCH) // PATCH
    fine_z = fine % PATCH
    coarse = jnp.arange(EDGE * EDGE, dtype=jnp.int32)
    hit = ((fine_y // 2 * EDGE + fine_z // 2)[:, None] == coarse[None, :])
    return jnp.where(hit, 0.125, 0.0).astype(jnp.bfloat16)


PAIRS_PER_STEP = 4


def average_kernel(source_ref, fine_ref, pairing_ref, out_ref, means_ref):
    slots = fine_ref.shape[0]
    rows = slots * FIELDS
    span = 2 * PATCH * PATCH
    stacked = jnp.concatenate(
        [fine_ref[:, :, i * span : (i + 1) * span].reshape(rows, span) for i in range(PAIRS_PER_STEP)],
        axis=0,
    )
    means = jnp.dot(stacked, pairing_ref[...], preferred_element_type=jnp.float32)
    width = EDGE * EDGE
    for i in range(PAIRS_PER_STEP):
        means_ref[:, :, i * width : (i + 1) * width] = (
            means[i * rows : (i + 1) * rows].reshape(slots, FIELDS, width).astype(means_ref.dtype)
        )
    for slot in range(slots):
        out_ref[slot] = means_ref[source_ref[slot]]


def average_cells(fine_data, source):
    row_count = fine_data.shape[0]
    span = 2 * PATCH * PATCH * PAIRS_PER_STEP
    width = EDGE * EDGE * PAIRS_PER_STEP
    steps = EDGE // PAIRS_PER_STEP
    grid_spec = pltpu.PrefetchScalarGridSpec(
        num_scalar_prefetch=1,
        grid=(steps,),
        in_specs=[
            pl.BlockSpec((row_count, FIELDS, span), lambda g, order: (0, 0, g)),
            pl.BlockSpec((2 * PATCH * PATCH, EDGE * EDGE), lambda g, order: (0, 0)),
        ],
        out_specs=pl.BlockSpec((row_count, FIELDS, width), lambda g, order: (0, 0, g)),
        scratch_shapes=[pltpu.VMEM((row_count, FIELDS, width), jnp.bfloat16)],
    )
    return pl.pallas_call(
        average_kernel,
        grid_spec=grid_spec,
        out_shape=jax.ShapeDtypeStruct((row_count, FIELDS, CELLS), jnp.bfloat16),
    )(source, fine_data, pairing_matrix())


def modes_kernel(data_ref, image_ref, coeffs_ref, fields_ref, diffused_ref):
    high, low = split(coeffs_ref[...])
    cols, modes = high.shape
    rows = data_ref.shape[0]
    depth = data_ref.shape[1] // cols
    data = jnp.concatenate([data_ref[:, z * cols : (z + 1) * cols] for z in range(depth)], axis=0)
    fields = jnp.dot(data, high, preferred_element_type=jnp.float32)
    fields = fields + jnp.dot(data, low, preferred_element_type=jnp.float32)
    image = jnp.concatenate([image_ref[:, z * cols : (z + 1) * cols] for z in range(depth)], axis=0)
    image_high, image_low = split(image)
    diffused = jnp.dot(image_high, high, preferred_element_type=jnp.float32)
    diffused = diffused + jnp.dot(image_high, low, preferred_element_type=jnp.float32)
    diffused = diffused + jnp.dot(image_low, high, preferred_element_type=jnp.float32)
    for z in range(depth):
        part = slice(z * rows, (z + 1) * rows)
        fields_ref[:, z * modes : (z + 1) * modes] = fields[part].astype(fields_ref.dtype)
        diffused_ref[:, z * modes : (z + 1) * modes] = diffused[part].astype(diffused_ref.dtype)


def project_modes(data, image, coeffs):
    rows, width = data.shape
    out_width = width // coeffs.shape[0] * coeffs.shape[1]
    vmem = pl.BlockSpec(memory_space=pltpu.VMEM)
    shape = jax.ShapeDtypeStruct((rows, out_width), jnp.bfloat16)
    return pl.pallas_call(
        modes_kernel,
        out_shape=(shape, shape),
        in_specs=[vmem, vmem, vmem],
        out_specs=(vmem, vmem),
    )(data, image, coeffs)


def seven_point(center, around_xy, around_z, stride):
    total = around_xy[2:, 1:-1] + around_xy[:-2, 1:-1] + around_xy[1:-1, 2:] + around_xy[1:-1, :-2]
    total = total + around_z[:, :, 2 * stride :] + around_z[:, :, : -2 * stride]
    return total - 6.0 * center


def split(value):
    high = value.astype(jnp.bfloat16)
    return high, (value - high.astype(jnp.float32)).astype(jnp.bfloat16)


def exact_dot(left, right, contract=1):
    numbers = (((contract,), (0,)), ((), ()))
    left_high, left_low = split(left)
    right_high, right_low = split(right)
    total = lax.dot_general(left_high, right_high, numbers, preferred_element_type=jnp.float32)
    total = total + lax.dot_general(left_high, right_low, numbers, preferred_element_type=jnp.float32)
    return total + lax.dot_general(left_low, right_high, numbers, preferred_element_type=jnp.float32)


def factor_kernel(gram_ref, prior_ref, cross_ref, out_ref, reduced_ref):
    size = gram_ref.shape[0]
    rows = lax.broadcasted_iota(jnp.int32, (size, size), 0)
    cols = lax.broadcasted_iota(jnp.int32, (size, size), 1)
    work = gram_ref[...]
    upper = jnp.zeros_like(work)
    for j in range(size):
        pivot = jnp.sqrt(work[j : j + 1, j : j + 1])
        column = jnp.where(rows[:, j : j + 1] >= j, work[:, j : j + 1] / pivot, 0.0)
        row = jnp.where(cols[j : j + 1, :] >= j, work[j : j + 1, :] / pivot, 0.0)
        upper = jnp.where(rows == j, row, upper)
        work = work - column * row
    solved = prior_ref[...]
    result = jnp.zeros_like(solved)
    picks = lax.broadcasted_iota(jnp.int32, solved.shape, 0)
    for i in reversed(range(size)):
        value = solved[i : i + 1, :] / upper[i : i + 1, i : i + 1]
        result = jnp.where(picks == i, value, result)
        solved = solved - upper[:, i : i + 1] * value
    out_ref[...] = result
    inner = exact_dot(cross_ref[...], result)
    reduced_ref[...] = exact_dot(result, inner, contract=0)


def factor_basis(gram_matrix, prior_basis, cross):
    vmem = pl.BlockSpec(memory_space=pltpu.VMEM)
    modes = prior_basis.shape[1]
    return pl.pallas_call(
        factor_kernel,
        out_shape=(
            jax.ShapeDtypeStruct(prior_basis.shape, prior_basis.dtype),
            jax.ShapeDtypeStruct((modes, modes), prior_basis.dtype),
        ),
        in_specs=[vmem, vmem, vmem],
        out_specs=(vmem, vmem),
    )((gram_matrix + gram_matrix.T) * 0.5, prior_basis, cross)


def cross_kernel(data_ref, image_ref, out_ref):
    cols = out_ref.shape[0]
    total = jnp.zeros(out_ref.shape, jnp.float32)
    for z in range(data_ref.shape[1] // cols):
        data = data_ref[:, z * cols : (z + 1) * cols]
        high, low = split(image_ref[:, z * cols : (z + 1) * cols])
        numbers = (((0,), (0,)), ((), ()))
        total = total + lax.dot_general(data, high, numbers, preferred_element_type=jnp.float32)
        total = total + lax.dot_general(data, low, numbers, preferred_element_type=jnp.float32)
    out_ref[...] = total


def cross_products(data, image):
    vmem = pl.BlockSpec(memory_space=pltpu.VMEM)
    return pl.pallas_call(
        cross_kernel,
        out_shape=jax.ShapeDtypeStruct((COLS, COLS), jnp.float32),
        in_specs=[vmem, vmem],
        out_specs=vmem,
    )(data, image)


def tree_sum(values):
    while len(values) > 1:
        values = [values[i] + values[i + 1] for i in range(0, len(values), 2)]
    return values[0]


REDUCE_GROUPS = (("gx", "gz_1"), ("gy",), ("gz_0",))


def allreduce_kernel(groups, part_ref, out_ref, acc, *rest):
    bufs, (send_sems, recv_sems) = rest[: len(groups)], rest[len(groups) :]
    me = {axis: lax.axis_index(axis) for group in groups for axis, _ in group}

    def linear(group):
        index = 0
        for axis, size in group:
            index = index * size + me[axis]
        return index

    def peer(group, step):
        count = 1
        for _, size in group:
            count *= size
        target = lax.rem(linear(group) + step, count)
        device = dict(me)
        for axis, size in reversed(group):
            device[axis] = lax.rem(target, size)
            target = target // size
        return tuple(device[axis] for axis in GX_GY_GZ)

    counts = []
    for group in groups:
        count = 1
        for _, size in group:
            count *= size
        counts.append(count)
    barrier = pltpu.get_barrier_semaphore()
    for group, count in zip(groups, counts):
        for step in range(1, count):
            pl.semaphore_signal(
                barrier, inc=1, device_id=peer(group, step), device_id_type=pl.DeviceIdType.MESH
            )
    pl.semaphore_wait(barrier, sum(counts) - len(counts))
    acc[...] = part_ref[...]
    slot = 0
    for group, count, buf in zip(groups, counts, bufs):
        copies = []
        for step in range(1, count):
            copy = pltpu.make_async_remote_copy(
                src_ref=acc,
                dst_ref=buf.at[step - 1],
                send_sem=send_sems.at[slot],
                recv_sem=recv_sems.at[slot],
                device_id=peer(group, step),
                device_id_type=pl.DeviceIdType.MESH,
            )
            copy.start()
            copies.append(copy)
            slot += 1
        for copy in copies:
            copy.wait()
        own = acc[...]
        mine = linear(group)
        values = []
        for source in range(count):
            held = jnp.maximum(lax.rem(mine - source + count, count) - 1, 0)
            values.append(jnp.where(mine == source, own, buf[held]))
        acc[...] = tree_sum(values)
    out_ref[...] = acc[...]


def allreduce(part):
    groups = tuple(
        tuple((axis, lax.axis_size(axis)) for axis in group) for group in REDUCE_GROUPS
    )
    counts = [functools.reduce(lambda a, b: a * b, [size for _, size in group]) for group in groups]
    copies = sum(count - 1 for count in counts)
    return pl.pallas_call(
        functools.partial(allreduce_kernel, groups),
        out_shape=jax.ShapeDtypeStruct(part.shape, part.dtype),
        in_specs=[pl.BlockSpec(memory_space=pltpu.VMEM)],
        out_specs=pl.BlockSpec(memory_space=pltpu.VMEM),
        scratch_shapes=[pltpu.VMEM(part.shape, part.dtype)]
        + [pltpu.VMEM((max(count - 1, 1),) + part.shape, part.dtype) for count in counts]
        + [pltpu.SemaphoreType.DMA((copies,)), pltpu.SemaphoreType.DMA((copies,))],
        compiler_params=pltpu.CompilerParams(collective_id=0, has_side_effects=True),
    )(part)


def exchange_kernel(plane, size_y, payload_ref, ids_ref, out_ref, out_ids_ref, send_sems, recv_sems, local_sems):
    me = lax.axis_index("gx") * size_y + lax.axis_index("gy")
    rest = tuple(lax.axis_index(axis) for axis in GZ)

    def device(step):
        target = lax.rem(me + step, plane)
        return (target // size_y, lax.rem(target, size_y)) + rest

    barrier = pltpu.get_barrier_semaphore()
    for step in range(1, plane):
        pl.semaphore_signal(barrier, inc=1, device_id=device(step), device_id_type=pl.DeviceIdType.MESH)
    pl.semaphore_wait(barrier, plane - 1)
    pairs = ((payload_ref, out_ref), (ids_ref, out_ids_ref))
    copies = []
    for index, (src, dst) in enumerate(pairs):
        copy = pltpu.make_async_copy(src.at[me], dst.at[me], local_sems.at[index])
        copy.start()
        copies.append(copy)
    for step in range(1, plane):
        target = lax.rem(me + step, plane)
        for index, (src, dst) in enumerate(pairs):
            slot = 2 * (step - 1) + index
            copy = pltpu.make_async_remote_copy(
                src_ref=src.at[target],
                dst_ref=dst.at[me],
                send_sem=send_sems.at[slot],
                recv_sem=recv_sems.at[slot],
                device_id=device(step),
                device_id_type=pl.DeviceIdType.MESH,
            )
            copy.start()
            copies.append(copy)
    for copy in copies:
        copy.wait()


def exchange(payload, ids):
    size_y = lax.axis_size("gy")
    plane = lax.axis_size("gx") * size_y
    vmem = pl.BlockSpec(memory_space=pltpu.VMEM)
    return pl.pallas_call(
        functools.partial(exchange_kernel, plane, size_y),
        out_shape=(
            jax.ShapeDtypeStruct(payload.shape, payload.dtype),
            jax.ShapeDtypeStruct(ids.shape, ids.dtype),
        ),
        in_specs=[vmem, vmem],
        out_specs=(vmem, vmem),
        scratch_shapes=[
            pltpu.SemaphoreType.DMA((2 * (plane - 1),)),
            pltpu.SemaphoreType.DMA((2 * (plane - 1),)),
            pltpu.SemaphoreType.DMA((2,)),
        ],
        compiler_params=pltpu.CompilerParams(collective_id=1, has_side_effects=True),
    )(payload, ids)


def halo_kernel(sizes, faces_ref, out_ref, send_sems, recv_sems):
    me = [lax.axis_index(axis) for axis in GX_GY_GZ]
    size_z1 = sizes[3]
    size_z = sizes[2] * size_z1

    def device(dim, step):
        if dim < 2:
            place = list(me)
            place[dim] = lax.rem(me[dim] + step + sizes[dim], sizes[dim])
            return tuple(place)
        z = lax.rem(me[2] * size_z1 + me[3] + step + size_z, size_z)
        return (me[0], me[1], z // size_z1, lax.rem(z, size_z1))

    targets = [device(dim, step) for dim in range(3) for step in (-1, 1)]
    barrier = pltpu.get_barrier_semaphore()
    for target in targets:
        pl.semaphore_signal(barrier, inc=1, device_id=target, device_id_type=pl.DeviceIdType.MESH)
    pl.semaphore_wait(barrier, len(targets))
    copies = []
    for index, target in enumerate(targets):
        copy = pltpu.make_async_remote_copy(
            src_ref=faces_ref.at[index],
            dst_ref=out_ref.at[index],
            send_sem=send_sems.at[index],
            recv_sem=recv_sems.at[index],
            device_id=target,
            device_id_type=pl.DeviceIdType.MESH,
        )
        copy.start()
        copies.append(copy)
    for copy in copies:
        copy.wait()


def halo(faces):
    sizes = tuple(lax.axis_size(axis) for axis in GX_GY_GZ)
    vmem = pl.BlockSpec(memory_space=pltpu.VMEM)
    return pl.pallas_call(
        functools.partial(halo_kernel, sizes),
        out_shape=jax.ShapeDtypeStruct(faces.shape, faces.dtype),
        in_specs=[vmem],
        out_specs=vmem,
        scratch_shapes=[
            pltpu.SemaphoreType.DMA((faces.shape[0],)),
            pltpu.SemaphoreType.DMA((faces.shape[0],)),
        ],
        compiler_params=pltpu.CompilerParams(collective_id=2, has_side_effects=True),
    )(faces)


def diffusion(data_block):
    edge = data_block.shape[0]
    cells = edge * COLS
    faces = jnp.stack(
        [
            data_block[0],
            data_block[-1],
            data_block[:, 0],
            data_block[:, -1],
            data_block[:, :, :COLS].reshape(edge, cells),
            data_block[:, :, -COLS:].reshape(edge, cells),
        ]
    )
    got = halo(faces).astype(jnp.float32)
    gx, gy, gz = lax.axis_index("gx"), lax.axis_index("gy"), lax.axis_index(GZ)
    last = (lax.axis_size("gx") - 1, lax.axis_size("gy") - 1, lax.axis_size(GZ) - 1)
    above_x = jnp.where(gx < last[0], got[0], 0.0)
    below_x = jnp.where(gx > 0, got[1], 0.0)
    above_y = jnp.where(gy < last[1], got[2], 0.0)
    below_y = jnp.where(gy > 0, got[3], 0.0)
    above_z = jnp.where(gz < last[2], got[4], 0.0).reshape(edge, edge, COLS)
    below_z = jnp.where(gz > 0, got[5], 0.0).reshape(edge, edge, COLS)
    center = data_block.astype(jnp.float32)
    along_x = jnp.concatenate([below_x[None], center, above_x[None]], axis=0)
    along_y = jnp.concatenate([below_y[:, None], center, above_y[:, None]], axis=1)
    along_z = jnp.concatenate([below_z, center, above_z], axis=2)
    total = along_x[2:] + along_x[:-2] + along_y[:, 2:] + along_y[:, :-2]
    total = total + along_z[:, :, 2 * COLS :] + along_z[:, :, : -2 * COLS]
    return total - 6.0 * center


def shards(patch_fields, slot_snapshot, slot_brick, prior_basis):
    size_x = lax.axis_size("gx")
    size_y = lax.axis_size("gy")
    size_z = lax.axis_size(GZ)
    plane_size = size_x * size_y
    slot_count = slot_snapshot.shape[0]
    pair_depth = slot_count // plane_size
    total_cells = CELLS * plane_size * size_z
    is_live = slot_snapshot >= 0
    slot_ids = jnp.arange(slot_count, dtype=jnp.int32)
    target_peer = jnp.where(is_live, slot_brick // size_z, plane_size)
    earlier = (target_peer[:, None] == target_peer[None, :]) & (
        slot_ids[None, :] < slot_ids[:, None]
    )
    pair_rank = jnp.sum(earlier.astype(jnp.int32), axis=1)
    position = jnp.where(is_live, target_peer * pair_depth + pair_rank, slot_count)
    slot_hits = position[:, None] == slot_ids[None, :]
    filled = jnp.any(slot_hits, axis=0)
    source = jnp.sum(jnp.where(slot_hits, slot_ids[:, None], 0), axis=0)
    sent_snapshot = jnp.where(filled, jnp.take(slot_snapshot, source, mode="clip"), -1)
    payload = average_cells(patch_fields, source)
    sent_ids = jnp.broadcast_to(sent_snapshot[:, None, None], (slot_count, 8, 128))
    received, received_ids = exchange(payload, sent_ids)
    received_snapshot = received_ids[:, 0, 0]
    snapshots = jnp.arange(SNAPS, dtype=jnp.int32)
    chosen = jnp.sum(
        jnp.where(received_snapshot[None, :] == snapshots[:, None], slot_ids[None, :], 0), axis=1
    )
    arrived = jnp.take(received, chosen, axis=0, mode="clip")
    columns = arrived.reshape(COLS, CELLS)
    partial_gram = jnp.dot(columns, columns.T, preferred_element_type=jnp.float32)
    data_block = columns.T.reshape(EDGE, EDGE, EDGE * COLS)
    data_block_image = diffusion(data_block)
    plane = data_block.shape[0] * data_block.shape[1]
    partial_cross = cross_products(data_block.reshape(plane, -1), data_block_image.reshape(plane, -1))
    totals = allreduce(jnp.concatenate([partial_gram, partial_cross], axis=1))
    gram_total, cross_total = totals[:, :COLS], totals[:, COLS:]
    gram_matrix = gram_total / total_cells
    coeffs, reduced = factor_basis(gram_matrix, prior_basis, cross_total / total_cells)
    mode_fields, diffused = project_modes(
        data_block.reshape(plane, -1), data_block_image.reshape(plane, -1), coeffs
    )
    mode_fields = mode_fields.reshape(EDGE, EDGE, EDGE * MODES)
    diffused = diffused.reshape(EDGE, EDGE, EDGE * MODES)
    return (gram_matrix, mode_fields, diffused, reduced)


def solution(mesh):
    split = Mesh(
        mesh.devices.reshape(mesh.shape["gx"], mesh.shape["gy"], 4, 2), ("gx", "gy", "gz_0", "gz_1")
    )
    in_specs = (P(GX_GY_GZ, None, None), P(GX_GY_GZ), P(GX_GY_GZ), P())
    out_specs = (P(), P("gx", "gy", GZ), P("gx", "gy", GZ), P())
    return jax.shard_map(
        shards, mesh=split, in_specs=in_specs, out_specs=out_specs, check_vma=False
    )
```
